32 devices in a mesh: wide: 16 (over z, y, x), narrow: 2 (over core).
Axes of the slice: x: 2, y: 2, z: 4, core: 2. Of those that a mesh axis runs over, the one named last changes fastest.
Arguments:
- pd_position: float32 [3, 32768], P(None, ('wide', 'narrow'))
- pd_displace: float32 [3, 32768], P(None, ('wide', 'narrow')), may hold values from -0.1 to 0.1
- pd_velocity: float32 [3, 32768], P(None, ('wide', 'narrow')), may hold values from -0.5 to 0.5
- pair_table: int32 [3, 1600], P(None, ('wide', 'narrow')), may hold values from 0 to 15, as said below
- pair_count: int32 [32], P(('wide', 'narrow')), may hold values from 4 to 18, as said below
- up_list: int32 [64], P(('wide', 'narrow')), may hold values from 0 to 3, as said below
- side_list: int32 [64], P(('wide', 'narrow')), may hold values from 0 to 3, as said below
- hex_displace: float32 [3, 16, 192, 256], P(None, 'wide', None, 'narrow'), may hold values from -0.1 to 0.1
- hex_velocity: float32 [3, 16, 192, 256], P(None, 'wide', None, 'narrow'), may hold values from -0.5 to 0.5
- hex_modulus: float32 [16, 192, 256], P('wide', None, 'narrow'), may hold values from 2 to 16
- blend_pd: int32 [16384], P(('wide', 'narrow')), may hold values from 0 to 1023
- blend_hex: int32 [16384], P(('wide', 'narrow')), may hold values from 0 to 24575
- blend_weight: float32 [16384], P(('wide', 'narrow')), may hold values from 0.25 to 1
Outputs:
- new_pd_displace: float32 [3, 32768], P(None, ('wide', 'narrow'))
- new_pd_velocity: float32 [3, 32768], P(None, ('wide', 'narrow'))
- new_hex_displace: float32 [3, 16, 192, 256], P(None, 'wide', None, 'narrow')
- new_hex_velocity: float32 [3, 16, 192, 256], P(None, 'wide', None, 'narrow')
The draws below stay inside these ranges and needn't reach their ends.
Inputs may be any that keep to these rules, and one draw needn't show every extreme that they name: `pair_table`: column 50 d + e describes device d's e-th pair for e < pair_count[d]: row 0 a block slot of device d (below 4); row 1 the second block: a slot of device d below 4, 4 + q for entry q of the up_list of device d + 2, or 6 + q for entry q of the side_list of the device whose index differs from d in the lowest bit; row 2 a mask of broken quadrants (bit 2 h1 + h2 for the halves h1 of the first and h2 of the second block). Blocks paired with themselves have mask 0. Columns from pair_count[d] on are zero. `pair_count`: device 0 lists 18 pairs. `up_list`: the 2 entries of one device are distinct block slots of that device. `side_list`: the 2 entries of one device are distinct block slots of that device.
All inputs are finite; a program needn't handle non-finite values.
Results may differ from the reference program's by a relative error of at most 0.0003.
Values sent between devices are 32-bit elements; how exact they have to be, the bound alone decides.
No kernel may reach another device: no remote copies, remote signals or barrier semaphores. Data moves between devices by JAX's collectives and lax.ppermute only.
A program may use at most 128 MiB of HBM per device.

```python
import math
import jax
import jax.numpy as jnp
import numpy as np
from jax import lax

BLOCK = 256
BY = 1
NB = 4
HALO = 2
PAIRS = 50
MAXPAIRS = 18
STEPS = 3
EZ = 1
EY = 192
EX = 128
OVL = 512
HZ = 16
HX = 256
PDN = 32768
N_WIDE = 16
N_NARROW = 2
DEVICES = 32


def layout(key):
    keys = jax.random.split(jax.random.fold_in(key, 7001), DEVICES)
    order = jax.vmap(lambda single: jax.random.permutation(single, NB))(keys).astype(jnp.int32)
    inverse = jnp.argsort(order, axis=1).astype(jnp.int32)
    return (order, inverse)


def static_pairs():
    total = 4 * BY
    blocks = np.arange(total)
    place_y = blocks // 2 % BY
    place_z = blocks // (2 * BY)
    local_first, local_second = ([], [])
    for left in range(total):
        for right in range(left, total):
            if abs(place_y[left] - place_y[right]) <= 1 and abs(place_z[left] - place_z[right]) <= 1:
                local_first.append(left)
                local_second.append(right)
    upper_first, upper_second = ([], [])
    for left in range(2 * BY, total):
        for right in range(2 * BY):
            if abs(place_y[left] - right // 2) <= 1:
                upper_first.append(left)
                upper_second.append(right)
    cross_low, cross_high = ([], [])
    for left in range(2 * BY):
        for right in range(2 * BY):
            if abs(left % BY - right % BY) <= 1 and abs(left // BY - right // BY) <= 1:
                cross_low.append(left)
                cross_high.append(right)
    return (np.array(local_first), np.array(local_second), np.array(upper_first), np.array(upper_second), np.array(cross_low), np.array(cross_high))


def pair_lists(key):
    order, inverse = layout(key)
    local_first, local_second, upper_first, upper_second, cross_low, cross_high = static_pairs()
    count_local = local_first.shape[0]
    count_upper = upper_first.shape[0]
    count_cross = cross_low.shape[0]
    device = jnp.arange(DEVICES, dtype=jnp.int32)[:, None]
    narrow_pos = device % 2
    wide_pos = device // 2
    first_local = inverse[:, local_first]
    second_local = inverse[:, local_second]
    first_upper = inverse[:, upper_first]
    second_upper = jnp.broadcast_to(jnp.asarray(NB + upper_second, jnp.int32)[None], (DEVICES, count_upper))
    first_cross = jnp.where(narrow_pos == 0, inverse[:, 1 + 2 * cross_low], inverse[:, 2 * cross_high])
    second_cross = jnp.where(narrow_pos == 0, jnp.asarray(NB + HALO + cross_high, jnp.int32)[None], jnp.asarray(NB + HALO + cross_low, jnp.int32)[None])
    owner = jax.random.randint(jax.random.fold_in(key, 7003), (N_WIDE, count_cross), 0, 2)
    owner = owner.at[0].set(0)
    owner_device = owner[wide_pos[:, 0]]
    enabled = jnp.concatenate([jnp.ones((DEVICES, count_local), bool), jnp.broadcast_to(wide_pos < N_WIDE - 1, (DEVICES, count_upper)), owner_device == narrow_pos], axis=1)
    self_pair = jnp.concatenate([jnp.asarray(local_first == local_second), jnp.zeros((count_upper + count_cross,), bool)])
    self_pair = jnp.broadcast_to(self_pair[None], (DEVICES, MAXPAIRS))
    level = jax.random.randint(jax.random.fold_in(key, 7004), (DEVICES,), 1, 9)
    level = (level * level).at[0].set(64)
    keep = jax.random.randint(jax.random.fold_in(key, 7005), (DEVICES, MAXPAIRS), 0, 64) < level[:, None]
    valid = jnp.logical_and(enabled, jnp.logical_or(keep, self_pair)).astype(jnp.int32)
    broken = (jax.random.randint(jax.random.fold_in(key, 7006), (DEVICES, MAXPAIRS, 4), 0, 4) == 0).astype(jnp.int32)
    tiles = jnp.sum(broken * jnp.array([1, 2, 4, 8], jnp.int32), axis=2) * (1 - self_pair.astype(jnp.int32))
    first = jnp.concatenate([first_local, first_upper, first_cross], axis=1)
    second = jnp.concatenate([second_local, second_upper, second_cross], axis=1)
    rank_keys = jax.random.split(jax.random.fold_in(key, 7007), DEVICES)
    ranks = jax.vmap(lambda single: jax.random.permutation(single, MAXPAIRS))(rank_keys).astype(jnp.int32)
    score = (1 - valid) * MAXPAIRS + ranks
    pick = jnp.argsort(score, axis=1)
    valid_sorted = jnp.take_along_axis(valid, pick, axis=1)
    first_sorted = jnp.take_along_axis(first, pick, axis=1) * valid_sorted
    second_sorted = jnp.take_along_axis(second, pick, axis=1) * valid_sorted
    tiles_sorted = jnp.take_along_axis(tiles, pick, axis=1) * valid_sorted
    padding = jnp.zeros((DEVICES, PAIRS - MAXPAIRS), jnp.int32)
    table = jnp.stack([jnp.concatenate([first_sorted, padding], axis=1), jnp.concatenate([second_sorted, padding], axis=1), jnp.concatenate([tiles_sorted, padding], axis=1)], axis=0)
    return (table.reshape(3, DEVICES * PAIRS).astype(jnp.int32), jnp.sum(valid, axis=1).astype(jnp.int32))


def draw_pair_table(key, part):
    table, count = pair_lists(key)
    return table


def draw_pair_count(key, part):
    table, count = pair_lists(key)
    return count


def draw_up_list(key, part):
    order, inverse = layout(key)
    return inverse[:, :HALO].reshape(DEVICES * HALO).astype(jnp.int32)


def draw_side_list(key, part):
    order, inverse = layout(key)
    device = jnp.arange(DEVICES, dtype=jnp.int32)[:, None]
    places = jnp.arange(HALO, dtype=jnp.int32)[None]
    edge = jnp.where(device % 2 == 0, 1 + 2 * places, 2 * places)
    return jnp.take_along_axis(inverse, edge, axis=1).reshape(DEVICES * HALO).astype(jnp.int32)


def draw_pd_position(key, part):
    order, inverse = layout(key)
    shape = (DEVICES, NB, BLOCK)
    device = jax.lax.broadcasted_iota(jnp.int32, shape, 0)
    node = jax.lax.broadcasted_iota(jnp.int32, shape, 2)
    block = jnp.broadcast_to(order[:, :, None], shape)
    global_x = 2 * (device % 2) + block % 2
    global_y = block // 2 % BY
    global_z = 2 * (device // 2) + block // (2 * BY)
    coord_x = 8 * global_x + node % 8
    coord_y = 8 * global_y + node // 8 % 8
    coord_z = 4 * global_z + node // 64
    lattice = jnp.stack([coord_x, coord_y, coord_z], axis=0).astype(jnp.float32).reshape(3, DEVICES * NB * BLOCK)
    noise_key = jax.random.fold_in(key, 7002)
    jitter = jnp.clip(0.04 * jax.random.normal(noise_key, lattice.shape, jnp.float32), -0.1, 0.1)
    return lattice + jitter


def plant(values, key, least, high):
    index_at = [jax.random.randint(jax.random.fold_in(key, axis), (), 0, length) for axis, length in enumerate(values.shape)]
    longest = values.shape.index(max(values.shape))
    beside = index_at[:longest] + [(index_at[longest] + 1) % values.shape[longest]] + index_at[longest + 1:]
    return values.at[tuple(index_at)].set(least).at[tuple(beside)].set(high)


def shard_levels(own_key, dims, cuts, low, top_value):
    gain = 1.0
    for position, shards_of in cuts:
        draws = jax.random.uniform(jax.random.fold_in(jax.random.fold_in(own_key, 6), position), (shards_of,), jnp.float32, low / len(cuts), top_value / len(cuts))
        gain = gain * jnp.repeat(jnp.exp(draws), dims[position] // shards_of).reshape((-1,) + (1,) * (len(dims) - 1 - position))
    return gain


def scatter_about(own_key, extent, deviation, most, shards=(), kind=jnp.bfloat16):
    entries = deviation * jax.random.normal(own_key, extent, jnp.float32)
    if shards:
        entries = entries * shard_levels(own_key, extent, shards, -0.22, 0.18)
    return jnp.clip(entries, -most, most).astype(kind)


def setup_inputs(seed: int = 0) -> dict:
    splits = jax.random.split(jax.random.key(seed), 14)
    pd_position = draw_pd_position(jax.random.fold_in(splits[13], 71), 0)
    pd_displace = scatter_about(splits[1], (3, PDN), 0.03, 0.1, ((1, 32),), jnp.float32)
    pd_velocity = scatter_about(splits[2], (3, PDN), 0.15, 0.5, ((1, 32),), jnp.float32)
    pair_table = draw_pair_table(jax.random.fold_in(splits[13], 71), 0)
    pair_count = draw_pair_count(jax.random.fold_in(splits[13], 71), 0)
    up_list = draw_up_list(jax.random.fold_in(splits[13], 71), 0)
    side_list = draw_side_list(jax.random.fold_in(splits[13], 71), 0)
    hex_displace = scatter_about(splits[7], (3, HZ, EY, HX), 0.03, 0.1, ((1, 16), (3, 2)), jnp.float32)
    hex_velocity = scatter_about(splits[8], (3, HZ, EY, HX), 0.15, 0.5, ((1, 16), (3, 2)), jnp.float32)
    hex_modulus = jnp.clip(jnp.exp(math.log(16.0) - 2.0794415 * jax.random.uniform(splits[9], (HZ, EY, HX), jnp.float32) ** shard_levels(splits[9], (HZ, EY, HX), ((0, 16), (2, 2)), -0.2, 0.2)), 2.0, 16.0)
    blend_pd = plant(jax.random.randint(splits[10], (DEVICES * OVL,), 0, NB * BLOCK), jax.random.fold_in(splits[10], 1), 0, (NB * BLOCK) - 1).astype(jnp.int32)
    blend_hex = plant(jax.random.randint(splits[11], (DEVICES * OVL,), 0, EZ * EY * EX), jax.random.fold_in(splits[11], 1), 0, (EZ * EY * EX) - 1).astype(jnp.int32)
    blend_weight = jnp.clip(0.25 + 0.75 * jax.random.uniform(splits[12], (DEVICES * OVL,), jnp.float32) ** shard_levels(splits[12], (DEVICES * OVL,), ((0, 32),), -0.2, 0.2), 0.25, 1.0)
    return dict(pd_position=pd_position, pd_displace=pd_displace, pd_velocity=pd_velocity, pair_table=pair_table, pair_count=pair_count, up_list=up_list, side_list=side_list, hex_displace=hex_displace, hex_velocity=hex_velocity, hex_modulus=hex_modulus, blend_pd=blend_pd, blend_hex=blend_hex, blend_weight=blend_weight)


stiffness = 20.0
horizon = 3.0
coupling = 10.0
hourglass = 0.15
poisson = 0.3
time_step = 0.1

def bond_forces(rest_first, motion_first, rest_second, motion_second, tiles, same, live):
    count = rest_first.shape[1]
    size = rest_first.shape[2]
    half = size // 2
    offset = rest_second[:, :, None, :] - rest_first[:, :, :, None]
    current = offset + (motion_second[:, :, None, :] - motion_first[:, :, :, None])
    rest_sq = lax.optimization_barrier(jnp.sum(offset * offset, axis=0))
    now_sq = lax.optimization_barrier(jnp.sum(current * current, axis=0))
    rows = lax.broadcasted_iota(jnp.int32, (size, size), 0)
    cols = lax.broadcasted_iota(jnp.int32, (size, size), 1)
    diagonal = jnp.logical_and(same[:, None, None], (rows == cols)[None])
    rest = jnp.sqrt(jnp.where(diagonal, 1.0, rest_sq))
    length = jnp.sqrt(jnp.where(diagonal, 1.0, now_sq))
    stretch = (length - rest) / rest
    weight = jnp.square(jnp.maximum(1.0 - rest / horizon, 0.0))
    quads = jnp.stack([tiles // 2 ** bit % 2 for bit in range(4)], axis=1).reshape(count, 2, 2)
    intact = (1 - quads).astype(jnp.float32)
    intact = jnp.broadcast_to(intact[:, :, None, :, None], (count, 2, half, 2, half)).reshape(count, size, size)
    factor = jnp.where(same, 0.5, 1.0) * live.astype(jnp.float32)
    scale = stiffness * stretch * weight * intact * jnp.where(diagonal, 0.0, 1.0) * factor[:, None, None] / length
    pulled = scale[None] * current
    return (lax.optimization_barrier(jnp.sum(pulled, axis=3)), -lax.optimization_barrier(jnp.sum(pulled, axis=2)))

def corner_signs():
    return [(2 * (corner % 2) - 1, 2 * (corner // 2 % 2) - 1, 2 * (corner // 4) - 1) for corner in range(8)]

def element_forces(corners, modulus, valid):
    signs = corner_signs()
    gradient = [[sum((corners[corner][outer] * (0.25 * signs[corner][inner]) for corner in range(8))) for inner in range(3)] for outer in range(3)]
    lame = modulus * (poisson / ((1.0 + poisson) * (1.0 - 2.0 * poisson)))
    shear = modulus * (1.0 / (2.0 * (1.0 + poisson)))
    trace = gradient[0][0] + gradient[1][1] + gradient[2][2]
    stress = [[shear * (gradient[outer][inner] + gradient[inner][outer]) + (lame * trace if outer == inner else 0.0) for inner in range(3)] for outer in range(3)]
    modes = [(signs[corner][1] * signs[corner][2], signs[corner][0] * signs[corner][2], signs[corner][0] * signs[corner][1], signs[corner][0] * signs[corner][1] * signs[corner][2]) for corner in range(8)]
    amplitude = [[sum((corners[corner][outer] * modes[corner][mode] for corner in range(8))) for outer in range(3)] for mode in range(4)]
    damping = hourglass * modulus
    result = []
    for corner in range(8):
        parts = []
        for outer in range(3):
            elastic = sum((stress[outer][inner] * (0.25 * signs[corner][inner]) for inner in range(3)))
            resist = sum((amplitude[mode][outer] * modes[corner][mode] for mode in range(4)))
            parts.append(-(elastic + damping * resist) * valid)
        result.append(jnp.stack(parts, axis=0))
    return result

def hex_forces(motion, modulus):
    depth, height, width = (motion.shape[1], motion.shape[2], motion.shape[3])
    padded = jnp.pad(motion, ((0, 0), (0, 1), (0, 1), (0, 1)))
    corners = []
    for corner in range(8):
        step_z, step_y, step_x = (corner // 4, corner // 2 % 2, corner % 2)
        corners.append(padded[:, step_z:step_z + depth, step_y:step_y + height, step_x:step_x + width])
    layer_ids = lax.iota(jnp.int32, depth)
    row_ids = lax.iota(jnp.int32, height)
    column_ids = lax.iota(jnp.int32, width)
    valid = ((layer_ids < depth - 1)[:, None, None] & (row_ids < height - 1)[None, :, None] & (column_ids < width - 1)[None, None, :]).astype(motion.dtype)
    forces = element_forces(corners, modulus, valid)
    total = jnp.zeros_like(motion)
    for corner in range(8):
        step_z, step_y, step_x = (corner // 4, corner // 2 % 2, corner % 2)
        moved = jnp.pad(forces[corner], ((0, 0), (step_z, 0), (step_y, 0), (step_x, 0)))
        total = total + moved[:, :depth, :height, :width]
    return total

def bond_batches(rest_blocks, motion, first, second, tiles, live):

    def one_batch(items):
        first_rows, second_rows, tile_rows, live_rows = items

        def work(unused):
            return bond_forces(rest_blocks[:, first_rows], motion[:, first_rows], rest_blocks[:, second_rows], motion[:, second_rows], tile_rows, first_rows == second_rows, live_rows)

        def skip(unused):
            empty = jnp.zeros((3, first_rows.shape[0], rest_blocks.shape[2]), rest_blocks.dtype)
            return (empty, empty)
        return lax.cond(jnp.any(live_rows > 0), work, skip, 0)
    pull_first, pull_second = lax.map(one_batch, (first, second, tiles, live))
    size = rest_blocks.shape[2]
    pull_first = jnp.moveaxis(pull_first, 0, 1).reshape(3, -1, size)
    pull_second = jnp.moveaxis(pull_second, 0, 1).reshape(3, -1, size)
    total = jnp.zeros_like(motion)
    total = total.at[:, first.reshape(-1)].add(pull_first)
    return total.at[:, second.reshape(-1)].add(pull_second)

def reference(pd_position, pd_displace, pd_velocity, pair_table, pair_count, up_list, side_list, hex_displace, hex_velocity, hex_modulus, blend_pd, blend_hex, blend_weight):
    devices = DEVICES
    batch = 10 * BY
    rest_blocks = pd_position.reshape(3, devices * NB, BLOCK)
    table = pair_table.reshape(3, devices, PAIRS)
    device = lax.broadcasted_iota(jnp.int32, (devices, PAIRS), 0)
    entry = lax.broadcasted_iota(jnp.int32, (devices, PAIRS), 1)
    up_table = up_list.reshape(devices, HALO)
    side_table = side_list.reshape(devices, HALO)
    above = jnp.minimum(device + N_NARROW, devices - 1)
    partner = device + 1 - 2 * (device % 2)
    target = table[1]
    up_slot = up_table[above, jnp.clip(target - NB, 0, HALO - 1)]
    side_slot = side_table[partner, jnp.clip(target - NB - HALO, 0, HALO - 1)]
    second = jnp.where(target < NB, device * NB + target, jnp.where(target < NB + HALO, above * NB + up_slot, partner * NB + side_slot))
    first = device * NB + table[0]
    live = (entry < pair_count[:, None]).astype(jnp.int32)
    order = jnp.argsort((1 - live).reshape(-1), stable=True)
    first_sorted = first.reshape(-1)[order].reshape(-1, batch).astype(jnp.int32)
    second_sorted = second.reshape(-1)[order].reshape(-1, batch).astype(jnp.int32)
    tiles_sorted = table[2].reshape(-1)[order].reshape(-1, batch).astype(jnp.int32)
    live_sorted = live.reshape(-1)[order].reshape(-1, batch)
    row_device = lax.iota(jnp.int32, devices * OVL) // OVL
    pd_index = row_device * (NB * BLOCK) + blend_pd
    layer = blend_hex // (EY * EX)
    row = blend_hex // EX % EY
    column = blend_hex % EX
    wide_pos = row_device // N_NARROW
    narrow_pos = row_device % N_NARROW
    hex_index = ((wide_pos * EZ + layer) * EY + row) * (EX * N_NARROW) + narrow_pos * EX + column
    motion = pd_displace.reshape(3, devices * NB, BLOCK)
    speed = pd_velocity.reshape(3, devices * NB, BLOCK)
    hex_motion = hex_displace
    hex_speed = hex_velocity
    for step in range(STEPS):
        pulls = bond_batches(rest_blocks, motion, first_sorted, second_sorted, tiles_sorted, live_sorted)
        hex_pull = hex_forces(hex_motion, hex_modulus)
        flat_motion = motion.reshape(3, -1)
        flat_hex = hex_motion.reshape(3, -1)
        pull = coupling * blend_weight * (flat_hex[:, hex_index] - flat_motion[:, pd_index])
        pd_total = pulls.reshape(3, -1).at[:, pd_index].add(pull)
        hex_total = hex_pull.reshape(3, -1).at[:, hex_index].add(-pull)
        speed = speed + time_step * pd_total.reshape(speed.shape)
        motion = motion + time_step * speed
        hex_speed = hex_speed + time_step * hex_total.reshape(hex_speed.shape)
        hex_motion = hex_motion + time_step * hex_speed
    return (motion.reshape(3, -1), speed.reshape(3, -1), hex_motion, hex_speed)
```

```python
import functools

import jax
import jax.numpy as jnp
from jax import lax
from jax.experimental import pallas as pl
from jax.experimental.pallas import tpu as pltpu
from jax.sharding import PartitionSpec as P

BLOCK = 256
STEPS = 3
LANES = 128

stiffness = 20.0
horizon = 3.0
coupling = 10.0
hourglass = 0.15
poisson = 0.3
time_step = 0.1
TINY = 1.2e-38
HIGH = lax.Precision.HIGHEST
VM = pl.BlockSpec(memory_space=pltpu.VMEM)
SM = pl.BlockSpec(memory_space=pltpu.SMEM)
ANY = pl.BlockSpec(memory_space=pl.ANY)


class Sizes:
    def __init__(self, nodes, height, pair_slots, halo):
        self.rows = nodes // LANES
        self.height = height
        self.blocks = nodes // BLOCK
        self.pair_slots = pair_slots
        self.halo = halo
        self.pd = height
        self.state = height + self.rows
        self.pos = self.state
        self.meta = self.pos + self.rows
        self.meta_rows = 8
        self.mod = self.meta + self.meta_rows
        self.mod_rows = -(-(height // 3) // 8) * 8
        self.first = self.mod + self.mod_rows


def modulus_parts(sz):
    parts = []
    for part in range(3):
        start = part * sz.mod_rows
        parts.append((part, start, min(sz.mod_rows, sz.height - start)))
    return parts


def pack_kernel(sz, hex_ref, disp_ref, vel_ref, pos_ref, meta_ref, mod_ref, send_ref, own_pos, own_vel):
    for axis in range(3):
        send_ref[axis, 0 : sz.height, :] = hex_ref[axis]
        for row in range(sz.rows):
            span = slice(row * LANES, (row + 1) * LANES)
            send_ref[axis, sz.pd + row : sz.pd + row + 1, :] = disp_ref[axis : axis + 1, span]
            send_ref[axis, sz.pos + row : sz.pos + row + 1, :] = pos_ref[axis : axis + 1, span]
            own_pos[axis, row : row + 1, :] = pos_ref[axis : axis + 1, span]
            own_vel[axis, row : row + 1, :] = vel_ref[axis : axis + 1, span]
        send_ref[axis, sz.meta : sz.mod, :] = meta_ref[...]
    for part, start, count in modulus_parts(sz):
        send_ref[part, sz.mod : sz.mod + count, :] = mod_ref[start : start + count, :]


def run_copies(copies):
    for copy in copies:
        copy.start()
    for copy in copies:
        copy.wait()


def spread_nodes(sz, table, slot, pos, disp):
    rows = sz.rows
    stacked = jnp.concatenate(
        [
            pos.reshape(3 * rows, LANES),
            disp.reshape(3 * rows, LANES),
            jnp.zeros((LANES - 6 * rows, LANES), jnp.float32),
        ],
        axis=0,
    )
    turned = stacked.T
    for row in range(rows):
        table[slot, row] = turned if row == 0 else pltpu.roll(turned, LANES - row, axis=1)


def pair_force(sz, table, pos_ref, disp, acc, target, slot, block, tiles, lane_first, guard):
    halves = BLOCK // LANES
    group = 8
    lane_pos = [
        [jnp.broadcast_to(pos_ref[axis, pl.ds(halves * target + hl, 1), :], (group, LANES)) for axis in range(3)]
        for hl in range(halves)
    ]
    lane_disp = [
        [jnp.broadcast_to(disp[axis, pl.ds(halves * target + hl, 1), :], (group, LANES)) for axis in range(3)]
        for hl in range(halves)
    ]

    def half(h, carry):
        source = table.at[slot, halves * block + h]
        sums = [[jnp.zeros((group, LANES), jnp.float32) for _ in range(3)] for _ in range(halves)]
        for g in range(LANES // group):
            values = source[g * group : (g + 1) * group, :]
            spread = [
                jnp.broadcast_to(values[:, k * sz.rows : k * sz.rows + 1], (group, LANES)) for k in range(6)
            ]
            for hl in range(halves):
                offset = [lane_pos[hl][axis] - spread[axis] for axis in range(3)]
                now = [offset[axis] + (lane_disp[hl][axis] - spread[3 + axis]) for axis in range(3)]
                rest_sq = offset[0] * offset[0] + offset[1] * offset[1] + offset[2] * offset[2]
                now_sq = now[0] * now[0] + now[1] * now[1] + now[2] * now[2]
                if guard:
                    rest_sq = jnp.maximum(rest_sq, TINY)
                    now_sq = jnp.maximum(now_sq, TINY)
                rest_inv = lax.rsqrt(rest_sq)
                now_inv = lax.rsqrt(now_sq)
                weight = jnp.maximum(1.0 - rest_sq * rest_inv * (1.0 / horizon), 0.0)
                scale = (now_inv - rest_inv) * (weight * weight)
                for axis in range(3):
                    sums[hl][axis] = sums[hl][axis] + scale * now[axis]
        for hl in range(halves):
            first, second = (hl, h) if lane_first else (h, hl)
            broken = lax.rem(lax.shift_right_logical(tiles, 2 * first + second), 2)
            keep = (1 - broken).astype(jnp.float32)
            for axis in range(3):
                place = halves * target + hl
                acc[axis, place] = acc[axis, place] + keep * sums[hl][axis]
        return carry

    lax.fori_loop(0, halves, half, 0)


def meta_index(sz, kind, item):
    flat = {"pair": 0, "count": 3 * sz.pair_slots, "up": 3 * sz.pair_slots + 1}
    flat["side"] = flat["up"] + sz.halo
    return flat[kind] + item


def meta_at(sz, ref, kind, item):
    flat = meta_index(sz, kind, item)
    return ref[flat // LANES, lax.rem(jnp.int32(flat), LANES)]


def blend(sz, disp_ref, pd_ref, hex_ref, weight_ref, pd_force, hex_pull):
    rows_h = hex_ref[...] // LANES
    cols_h = lax.rem(hex_ref[...], LANES)
    rows_p = pd_ref[...] // LANES
    cols_p = lax.rem(pd_ref[...], LANES)
    count = rows_h.shape[1]
    at_col = lax.broadcasted_iota(jnp.int32, (LANES, count), 0)
    pick_h = jnp.where(at_col == cols_h, 1.0, 0.0)
    pick_p = jnp.where(at_col == cols_p, 1.0, 0.0)
    in_h = lax.broadcasted_iota(jnp.int32, (sz.height, count), 0) == rows_h
    in_p = lax.broadcasted_iota(jnp.int32, (sz.rows, count), 0) == rows_p
    transposed = (((1,), (1,)), ((), ()))
    for axis in range(3):
        from_h = jnp.dot(disp_ref[axis, 0 : sz.height, :], pick_h, precision=HIGH, preferred_element_type=jnp.float32)
        from_p = jnp.dot(disp_ref[axis, sz.pd : sz.state, :], pick_p, precision=HIGH, preferred_element_type=jnp.float32)
        at_h = jnp.sum(jnp.where(in_h, from_h, 0.0), axis=0, keepdims=True)
        at_p = jnp.sum(jnp.where(in_p, from_p, 0.0), axis=0, keepdims=True)
        pull = coupling * weight_ref[...] * (at_h - at_p)
        hex_pull[axis] = lax.dot_general(
            jnp.where(in_h, pull, 0.0), pick_h, transposed, precision=HIGH, preferred_element_type=jnp.float32
        )
        pd_force[axis] = pd_force[axis] + lax.dot_general(
            jnp.where(in_p, pull, 0.0), pick_p, transposed, precision=HIGH, preferred_element_type=jnp.float32
        )


def near_kernel(
    sz, pairs, count, side_list, side_meta, own, own_pos, side, side_first, blend_pd, blend_hex, blend_weight,
    force, hex_pull, table, acc, side_pos, side_disp, sems,
):
    copies = [
        pltpu.make_async_copy(side_first.at[:, pl.ds(sz.pos, sz.rows), :], side_pos, sems.at[0]),
        pltpu.make_async_copy(side.at[:, pl.ds(sz.pd, sz.rows), :], side_disp, sems.at[1]),
    ]
    for copy in copies:
        copy.start()
    acc[...] = jnp.zeros(acc.shape, jnp.float32)
    disp = own.at[:, pl.ds(sz.pd, sz.rows), :]
    spread_nodes(sz, table, 0, own_pos[...], disp[...])
    for copy in copies:
        copy.wait()
    spread_nodes(sz, table, 1, side_pos[...], side_disp[...])
    go = functools.partial(pair_force, sz, table, own_pos, disp, acc, guard=True)
    edge = sz.blocks + sz.halo

    def listed(e, carry):
        a, c, m = pairs[0, e], pairs[1, e], pairs[2, e]

        @pl.when(c < sz.blocks)
        def _():
            go(a, 0, c, m, lane_first=True)

        @pl.when(jnp.logical_and(c < sz.blocks, c != a))
        def _():
            go(c, 0, a, m, lane_first=False)

        @pl.when(c >= edge)
        def _():
            go(a, 1, meta_at(sz, side_meta, "side", jnp.maximum(c - edge, 0)), m, lane_first=True)

        return carry

    lax.fori_loop(0, count[0], listed, 0)

    def listed_beside(e, carry):
        a = meta_at(sz, side_meta, "pair", e)
        c = meta_at(sz, side_meta, "pair", sz.pair_slots + e)
        m = meta_at(sz, side_meta, "pair", 2 * sz.pair_slots + e)

        @pl.when(c >= edge)
        def _():
            go(side_list[jnp.maximum(c - edge, 0)], 1, a, m, lane_first=False)

        return carry

    lax.fori_loop(0, meta_at(sz, side_meta, "count", 0), listed_beside, 0)
    for axis in range(3):
        force[axis] = stiffness * jnp.sum(acc[axis], axis=1)
    blend(sz, own, blend_pd, blend_hex, blend_weight, force, hex_pull)


def far_kernel(
    sz, pairs, count, up_list, above_meta, below_meta, own, own_pos, one, two, one_first, two_first, near,
    force, table, acc, pos, disp, sems,
):
    even = lax.rem(lax.axis_index("wide"), 2) == 0

    def fetch(above, below, above_first, below_first):
        run_copies(
            [
                pltpu.make_async_copy(above_first.at[:, pl.ds(sz.pos, sz.rows), :], pos.at[0], sems.at[0]),
                pltpu.make_async_copy(below_first.at[:, pl.ds(sz.pos, sz.rows), :], pos.at[1], sems.at[1]),
                pltpu.make_async_copy(above.at[:, pl.ds(sz.pd, sz.rows), :], disp.at[0], sems.at[2]),
                pltpu.make_async_copy(below.at[:, pl.ds(sz.pd, sz.rows), :], disp.at[1], sems.at[3]),
            ]
        )

    @pl.when(even)
    def _():
        fetch(one, two, one_first, two_first)

    @pl.when(jnp.logical_not(even))
    def _():
        fetch(two, one, two_first, one_first)

    acc[...] = jnp.zeros(acc.shape, jnp.float32)
    for slot in range(2):
        spread_nodes(sz, table, slot, pos[slot], disp[slot])
    own_disp = own.at[:, pl.ds(sz.pd, sz.rows), :]
    go = functools.partial(pair_force, sz, table, own_pos, own_disp, acc, guard=False)
    edge = sz.blocks + sz.halo

    def listed(e, carry):
        a, c, m = pairs[0, e], pairs[1, e], pairs[2, e]

        @pl.when(jnp.logical_and(c >= sz.blocks, c < edge))
        def _():
            go(a, 0, meta_at(sz, above_meta, "up", jnp.clip(c - sz.blocks, 0, sz.halo - 1)), m, lane_first=True)

        return carry

    lax.fori_loop(0, count[0], listed, 0)

    def listed_below(e, carry):
        a = meta_at(sz, below_meta, "pair", e)
        c = meta_at(sz, below_meta, "pair", sz.pair_slots + e)
        m = meta_at(sz, below_meta, "pair", 2 * sz.pair_slots + e)

        @pl.when(jnp.logical_and(c >= sz.blocks, c < edge))
        def _():
            go(up_list[jnp.clip(c - sz.blocks, 0, sz.halo - 1)], 1, a, m, lane_first=False)

        return carry

    lax.fori_loop(0, meta_at(sz, below_meta, "count", 0), listed_below, 0)
    for axis in range(3):
        force[axis] = near[axis] + stiffness * jnp.sum(acc[axis], axis=1)


def hex_kernel(sz, first, last, *refs):
    refs = list(refs)
    take = lambda count: [refs.pop(0) for _ in range(count)]
    own, side, one, two, one_side, two_side, force, hex_pull, hex_vel, pd_vel = take(10)
    moduli = take(1)[0]
    outs = take(4) if last else take(3)
    shifted_out = take(1)[0] if first else None
    planes, parts, _, nodes_low, nodes_high, mod_side, sems = take(7)
    height = sz.height
    wide = lax.axis_index("wide")
    narrow = lax.axis_index("narrow")
    even = lax.rem(wide, 2) == 0
    low_half = narrow == 0
    shift = jnp.where(low_half, LANES - 1, 1)
    back = LANES - shift
    edge = jnp.where(low_half, 0, LANES - 1)
    sign = jnp.where(low_half, 1.0, -1.0)
    hexes = pl.ds(0, height)
    near_copies = [pltpu.make_async_copy(side.at[:, hexes, :], planes.at[0], sems.at[0])]
    if first:
        near_copies.append(pltpu.make_async_copy(side.at[:, pl.ds(sz.mod, sz.mod_rows), :], mod_side.at[0], sems.at[5]))

    def fetch(above, above_side, below, below_side):
        copies = list(near_copies)
        for place, ref in enumerate((above, above_side, below, below_side)):
            copies.append(pltpu.make_async_copy(ref.at[:, hexes, :], planes.at[1 + place], sems.at[1 + place]))
        if first:
            for place, ref in enumerate((below, below_side)):
                copies.append(
                    pltpu.make_async_copy(
                        ref.at[:, pl.ds(sz.mod, sz.mod_rows), :], mod_side.at[1 + place], sems.at[6 + place]
                    )
                )
        run_copies(copies)

    @pl.when(even)
    def _():
        fetch(one, one_side, two, two_side)

    @pl.when(jnp.logical_not(even))
    def _():
        fetch(two, two_side, one, one_side)

    if first:
        lanes = lax.broadcasted_iota(jnp.int32, (8, LANES), 1)
        last_lane = lanes == LANES - 1
        has_above = jnp.where(wide < lax.axis_size("wide") - 1, 1.0, 0.0)
        for part, start, count in modulus_parts(sz):
            for row in range(0, count, 8):
                at = start + row
                inside = lax.broadcasted_iota(jnp.int32, (8, LANES), 0) + at < height - 1
                for place, (mine, beside) in enumerate(
                    (
                        (moduli[at : at + 8, :], mod_side[0, part, row : row + 8, :]),
                        (mod_side[1, part, row : row + 8, :], mod_side[2, part, row : row + 8, :]),
                    )
                ):
                    turned = pltpu.roll(jnp.where(last_lane, beside, mine), 1, axis=1)
                    value = jnp.where(inside, jnp.where(low_half, mine, turned), 0.0)
                    if place == 0:
                        value = value * has_above
                    shifted_out[place, at : at + 8, :] = value
        moduli = shifted_out

    tall = 16
    lanes = lax.broadcasted_iota(jnp.int32, (tall, LANES), 1)
    at_edge = lanes == edge

    def along_x(r, carry):
        rows = pl.ds(pl.multiple_of(r * tall, tall), tall)
        for layer in range(3):
            for axis in range(3):
                if layer == 0:
                    mine, beside = own[axis, rows, :], planes[0, axis, rows, :]
                else:
                    mine, beside = planes[2 * layer - 1, axis, rows, :], planes[2 * layer, axis, rows, :]
                if axis == 0:
                    mine, beside = mine * sign, beside * sign
                other = pltpu.roll(jnp.where(at_edge, beside, mine), shift, axis=1)
                parts[layer, axis, 0, rows, :] = mine + other
                parts[layer, axis, 1, rows, :] = other - mine
        return carry

    lax.fori_loop(0, height // tall, along_x, 0)
    for layer in range(3):
        for axis in range(3):
            for px in range(2):
                parts[layer, axis, px, height : height + 8, :] = jnp.zeros((8, LANES), jnp.float32)
    for axis in range(3):
        for px in range(2):
            nodes_high[axis, px, 0:8, :] = jnp.zeros((8, LANES), jnp.float32)

    shear_by = 1.0 / (2.0 * (1.0 + poisson)) / 16.0
    lame_by = poisson / ((1.0 + poisson) * (1.0 - 2.0 * poisson)) / 16.0
    for r in range(0, height, 8):
        grid = [[[None] * 4 for _ in range(3)] for _ in range(3)]
        for layer in range(3):
            for axis in range(3):
                for px in range(2):
                    here = parts[layer, axis, px, r : r + 8, :]
                    after = parts[layer, axis, px, r + 1 : r + 9, :]
                    grid[layer][axis][px] = here + after
                    grid[layer][axis][2 + px] = after - here
        total = [[None] * 4 for _ in range(3)]
        for place, (bottom, top, at_top) in enumerate(((0, 1, False), (2, 0, True))):
            m = [
                [
                    (grid[bottom][axis][k] + grid[top][axis][k], grid[top][axis][k] - grid[bottom][axis][k])
                    for k in range(4)
                ]
                for axis in range(3)
            ]
            modulus = moduli[place, r : r + 8, :]
            shear = modulus * shear_by
            lame = modulus * lame_by
            damp = modulus * hourglass
            slope = [[m[axis][1][0], m[axis][2][0], m[axis][0][1]] for axis in range(3)]
            trace = lame * (slope[0][0] + slope[1][1] + slope[2][2])
            twice = shear + shear
            stress = [[None] * 3 for _ in range(3)]
            for a in range(3):
                stress[a][a] = twice * slope[a][a] + trace
                for b in range(a + 1, 3):
                    stress[a][b] = shear * (slope[a][b] + slope[b][a])
                    stress[b][a] = stress[a][b]
            for axis in range(3):
                plain = [None, stress[axis][0], stress[axis][1], damp * m[axis][3][0]]
                odd = [stress[axis][2], damp * m[axis][1][1], damp * m[axis][2][1], damp * m[axis][3][1]]
                for k in range(4):
                    if k == 0:
                        value = odd[k] if at_top else -odd[k]
                    else:
                        value = plain[k] + odd[k] if at_top else plain[k] - odd[k]
                    total[axis][k] = value if total[axis][k] is None else total[axis][k] + value
        for axis in range(3):
            for px in range(2):
                even_y, odd_y = total[axis][px], total[axis][2 + px]
                nodes_low[axis, px, r : r + 8, :] = even_y - odd_y
                nodes_high[axis, px, r + 8 : r + 16, :] = even_y + odd_y

    lanes = lax.broadcasted_iota(jnp.int32, (8, LANES), 1)
    keep = lanes != edge
    for r in range(0, height, 8):
        for axis in range(3):
            pair = [
                nodes_low[axis, px, r : r + 8, :] + nodes_high[axis, px, r + 7 : r + 15, :] for px in range(2)
            ]
            moved = jnp.where(keep, pltpu.roll(pair[0] + pair[1], back, axis=1), 0.0)
            element = pair[0] - pair[1] + moved
            if axis == 0:
                element = element * sign
            speed = hex_vel[axis, r : r + 8, :] - time_step * (element + hex_pull[axis, r : r + 8, :])
            place = own[axis, r : r + 8, :] + time_step * speed
            outs[0][axis, r : r + 8, :] = place
            outs[1][axis, r : r + 8, :] = speed
    for axis in range(3):
        speed = pd_vel[axis] + time_step * force[axis]
        place = own[axis, sz.pd : sz.state, :] + time_step * speed
        if last:
            for row in range(sz.rows):
                span = slice(row * LANES, (row + 1) * LANES)
                outs[2][axis : axis + 1, span] = place[row : row + 1, :]
                outs[3][axis : axis + 1, span] = speed[row : row + 1, :]
        else:
            outs[0][axis, sz.pd : sz.state, :] = place
            outs[2][axis] = speed


def local(
    pd_position,
    pd_displace,
    pd_velocity,
    pair_table,
    pair_count,
    up_list,
    side_list,
    hex_displace,
    hex_velocity,
    hex_modulus,
    blend_pd,
    blend_hex,
    blend_weight,
):
    f32 = jnp.float32
    nodes = pd_position.shape[1]
    height, width = hex_displace.shape[2], hex_displace.shape[3]
    sz = Sizes(nodes, height, pair_table.shape[1], up_list.shape[0])
    wide = lax.axis_size("wide")
    near_pairs = [(i, i ^ 1) for i in range(wide) if i ^ 1 < wide]
    next_pairs = [(i, i + 1) for i in range(1, wide - 1, 2)] + [(i + 1, i) for i in range(1, wide - 1, 2)]
    swap_near = lambda x: lax.ppermute(x, "wide", near_pairs)
    swap_next = lambda x: lax.ppermute(x, "wide", next_pairs)
    swap_side = lambda x: lax.ppermute(x, "narrow", [(0, 1), (1, 0)])
    shape = lambda *dims: jax.ShapeDtypeStruct(dims, f32)

    lists = jnp.concatenate([pair_table.reshape(-1), pair_count, up_list, side_list]).astype(f32)
    lists = jnp.pad(lists, (0, sz.meta_rows * LANES - lists.shape[0])).reshape(sz.meta_rows, LANES)
    own, own_pos, pd_vel = pl.pallas_call(
        functools.partial(pack_kernel, sz),
        out_shape=(shape(3, sz.first, LANES), shape(3, sz.rows, LANES), shape(3, sz.rows, LANES)),
        in_specs=[VM] * 6,
        out_specs=(VM, VM, VM),
        name="pack",
    )(
        hex_displace.reshape(3, height, width),
        pd_displace,
        pd_velocity,
        pd_position,
        lists,
        hex_modulus.reshape(height, width),
    )
    hex_vel = hex_velocity.reshape(3, height, width)
    moduli = hex_modulus.reshape(height, width)
    rows_pd = blend_pd.reshape(1, -1)
    rows_hex = blend_hex.reshape(1, -1)
    rows_weight = blend_weight.reshape(1, -1)

    state = (own, own_pos, hex_vel, pd_vel, moduli, None)
    fixed = (sz, pair_table, pair_count, up_list, side_list, rows_pd, rows_hex, rows_weight)
    for step in range(STEPS):
        state = advance(step == 0, step == STEPS - 1, fixed, state, swap_side, swap_near, swap_next)
    hex_out, hex_speed, pd_out, pd_speed = state
    return (pd_out, pd_speed, hex_out.reshape(hex_displace.shape), hex_speed.reshape(hex_velocity.shape))


def advance(first, last, fixed, state, swap_side, swap_near, swap_next):
    f32 = jnp.float32
    shape = lambda *dims: jax.ShapeDtypeStruct(dims, f32)
    sz, pair_table, pair_count, up_list, side_list, rows_pd, rows_hex, rows_weight = fixed
    own, own_pos, hex_vel, pd_vel, moduli, kept = state
    height = sz.height
    even = lax.rem(lax.axis_index("wide"), 2) == 0
    side = swap_side(own)
    one = swap_near(own)
    two = swap_next(own)
    lists_of = lambda x: x[0, sz.meta : sz.mod, :].astype(jnp.int32)
    if first:
        side_first, one_first, two_first = side, one, two
        side_meta = lists_of(side)
        one_meta, two_meta = lists_of(one), lists_of(two)
        above_meta = jnp.where(even, one_meta, two_meta)
        below_meta = jnp.where(even, two_meta, one_meta)
        kept = (side_first, one_first, two_first, side_meta, above_meta, below_meta)
    side_first, one_first, two_first, side_meta, above_meta, below_meta = kept
    force, hex_pull = pl.pallas_call(
        functools.partial(near_kernel, sz),
        out_shape=(shape(3, sz.rows, LANES), shape(3, height, LANES)),
        in_specs=[SM] * 4 + [VM, VM, ANY, ANY, VM, VM, VM],
        out_specs=(VM, VM),
        scratch_shapes=[
            pltpu.VMEM((2, sz.rows, LANES, LANES), f32),
            pltpu.VMEM((3, sz.rows, 8, LANES), f32),
            pltpu.VMEM((3, sz.rows, LANES), f32),
            pltpu.VMEM((3, sz.rows, LANES), f32),
            pltpu.SemaphoreType.DMA((2,)),
        ],
        cost_estimate=pl.CostEstimate(flops=60_000_000, transcendentals=2_600_000, bytes_accessed=40_000_000),
        name="near",
    )(pair_table, pair_count, side_list, side_meta, own, own_pos, side, side_first, rows_pd, rows_hex, rows_weight)
    one_side, two_side = swap_side(one), swap_side(two)
    force = pl.pallas_call(
        functools.partial(far_kernel, sz),
        out_shape=shape(3, sz.rows, LANES),
        in_specs=[SM] * 5 + [VM, VM, ANY, ANY, ANY, ANY, VM],
        out_specs=VM,
        scratch_shapes=[
            pltpu.VMEM((2, sz.rows, LANES, LANES), f32),
            pltpu.VMEM((3, sz.rows, 8, LANES), f32),
            pltpu.VMEM((2, 3, sz.rows, LANES), f32),
            pltpu.VMEM((2, 3, sz.rows, LANES), f32),
            pltpu.SemaphoreType.DMA((4,)),
        ],
        name="far",
    )(
        pair_table, pair_count, up_list, above_meta, below_meta, own, own_pos, one, two, one_first, two_first, force
    )
    if last:
        outs = (shape(3, height, LANES), shape(3, height, LANES), shape(3, sz.rows * LANES), shape(3, sz.rows * LANES))
    else:
        outs = (shape(3, sz.state, LANES), shape(3, height, LANES), shape(3, sz.rows, LANES))
    if first:
        outs = outs + (shape(2, height, LANES),)
    results = pl.pallas_call(
        functools.partial(hex_kernel, sz, first, last),
        out_shape=outs,
        in_specs=[VM] + [ANY] * 5 + [VM] * 5,
        out_specs=tuple(VM for _ in outs),
        scratch_shapes=[
            pltpu.VMEM((5, 3, height, LANES), f32),
            pltpu.VMEM((3, 3, 2, height + 8, LANES), f32),
            pltpu.VMEM((8, LANES), f32),
            pltpu.VMEM((3, 2, height, LANES), f32),
            pltpu.VMEM((3, 2, height + 8, LANES), f32),
            pltpu.VMEM((3, 3, sz.mod_rows, LANES), f32),
            pltpu.SemaphoreType.DMA((8,)),
        ],
        name="hexes",
    )(own, side, one, two, one_side, two_side, force, hex_pull, hex_vel, pd_vel, moduli)
    if last:
        return results[:4]
    return results[0], own_pos, results[1], results[2], results[3] if first else moduli, kept


def solution(mesh):
    both = ("wide", "narrow")
    in_specs = (
        P(None, both),
        P(None, both),
        P(None, both),
        P(None, both),
        P(both),
        P(both),
        P(both),
        P(None, "wide", None, "narrow"),
        P(None, "wide", None, "narrow"),
        P("wide", None, "narrow"),
        P(both),
        P(both),
        P(both),
    )
    out_specs = (
        P(None, both),
        P(None, both),
        P(None, "wide", None, "narrow"),
        P(None, "wide", None, "narrow"),
    )
    return jax.shard_map(local, mesh=mesh, in_specs=in_specs, out_specs=out_specs, check_vma=False)
```

```python
import functools

import jax
import jax.numpy as jnp
from jax import lax
from jax.experimental import pallas as pl
from jax.experimental.pallas import tpu as pltpu
from jax.sharding import PartitionSpec as P

BLOCK = 256
STEPS = 3
LANES = 128

stiffness = 20.0
horizon = 3.0
coupling = 10.0
hourglass = 0.15
poisson = 0.3
time_step = 0.1
TINY = 1.2e-38
VM = pl.BlockSpec(memory_space=pltpu.VMEM)
SM = pl.BlockSpec(memory_space=pltpu.SMEM)
LIMIT = pltpu.CompilerParams(vmem_limit_bytes=24 * 1024 * 1024)
kept_near = lambda x: pltpu.with_memory_space_constraint(x, pltpu.VMEM)


class Sizes:
    def __init__(self, nodes, height, pair_slots, halo):
        self.rows = nodes // LANES
        self.height = height
        self.blocks = nodes // BLOCK
        self.pair_slots = pair_slots
        self.halo = halo
        self.pd = height
        self.state = height + self.rows
        self.pos = self.state
        self.meta = self.pos + self.rows
        self.meta_rows = 8
        self.mod = self.meta + self.meta_rows
        self.mod_rows = -(-(height // 3) // 8) * 8
        self.first = self.mod + self.mod_rows


def modulus_parts(sz):
    parts = []
    for part in range(3):
        start = part * sz.mod_rows
        parts.append((part, start, min(sz.mod_rows, sz.height - start)))
    return parts


def pack_kernel(sz, hex_ref, disp_ref, vel_ref, pos_ref, meta_ref, mod_ref, send_ref, own_pos, own_vel):
    for axis in range(3):
        send_ref[axis, 0 : sz.height, :] = hex_ref[axis]
        for row in range(sz.rows):
            span = slice(row * LANES, (row + 1) * LANES)
            send_ref[axis, sz.pd + row : sz.pd + row + 1, :] = disp_ref[axis : axis + 1, span]
            send_ref[axis, sz.pos + row : sz.pos + row + 1, :] = pos_ref[axis : axis + 1, span]
            own_pos[axis, row : row + 1, :] = pos_ref[axis : axis + 1, span]
            own_vel[axis, row : row + 1, :] = vel_ref[axis : axis + 1, span]
        send_ref[axis, sz.meta : sz.mod, :] = meta_ref[...]
    for part, start, count in modulus_parts(sz):
        send_ref[part, sz.mod : sz.mod + count, :] = mod_ref[start : start + count, :]


def spread_nodes(sz, table, slot, pos, disp):
    rows = sz.rows
    stacked = jnp.concatenate(
        [
            pos.reshape(3 * rows, LANES),
            disp.reshape(3 * rows, LANES),
            jnp.zeros((LANES - 6 * rows, LANES), jnp.float32),
        ],
        axis=0,
    )
    turned = stacked.T
    for row in range(rows):
        table[slot, row] = turned if row == 0 else pltpu.roll(turned, LANES - row, axis=1)


def pair_force(sz, table, pos_ref, disp, acc, target, slot, block, tiles, lane_first, guard):
    halves = BLOCK // LANES
    group = 8
    lane_pos = [
        [jnp.broadcast_to(pos_ref[axis, pl.ds(halves * target + hl, 1), :], (group, LANES)) for axis in range(3)]
        for hl in range(halves)
    ]
    lane_disp = [
        [jnp.broadcast_to(disp[axis, pl.ds(halves * target + hl, 1), :], (group, LANES)) for axis in range(3)]
        for hl in range(halves)
    ]

    def half(h, carry):
        source = table.at[slot, halves * block + h]
        sums = [[jnp.zeros((group, LANES), jnp.float32) for _ in range(3)] for _ in range(halves)]
        for g in range(LANES // group):
            values = source[g * group : (g + 1) * group, :]
            spread = [
                jnp.broadcast_to(values[:, k * sz.rows : k * sz.rows + 1], (group, LANES)) for k in range(6)
            ]
            for hl in range(halves):
                offset = [lane_pos[hl][axis] - spread[axis] for axis in range(3)]
                now = [offset[axis] + (lane_disp[hl][axis] - spread[3 + axis]) for axis in range(3)]
                rest_sq = offset[0] * offset[0] + offset[1] * offset[1] + offset[2] * offset[2]
                now_sq = now[0] * now[0] + now[1] * now[1] + now[2] * now[2]
                if guard:
                    rest_sq = jnp.maximum(rest_sq, TINY)
                    now_sq = jnp.maximum(now_sq, TINY)
                rest_inv = lax.rsqrt(rest_sq)
                now_inv = lax.rsqrt(now_sq)
                weight = jnp.maximum(1.0 - rest_sq * rest_inv * (1.0 / horizon), 0.0)
                scale = (now_inv - rest_inv) * (weight * weight)
                for axis in range(3):
                    sums[hl][axis] = sums[hl][axis] + scale * now[axis]
        for hl in range(halves):
            first, second = (hl, h) if lane_first else (h, hl)
            broken = lax.rem(lax.shift_right_logical(tiles, 2 * first + second), 2)
            keep = (1 - broken).astype(jnp.float32)
            for axis in range(3):
                place = halves * target + hl
                acc[axis, place] = acc[axis, place] + keep * sums[hl][axis]
        return carry

    lax.fori_loop(0, halves, half, 0)


def meta_index(sz, kind, item):
    flat = {"pair": 0, "count": 3 * sz.pair_slots, "up": 3 * sz.pair_slots + 1}
    flat["side"] = flat["up"] + sz.halo
    return flat[kind] + item


def meta_at(sz, ref, kind, item):
    flat = meta_index(sz, kind, item)
    return ref[flat // LANES, lax.rem(jnp.int32(flat), LANES)]


def halves_of(x):
    high = x.astype(jnp.bfloat16)
    return high, (x - high.astype(jnp.float32)).astype(jnp.bfloat16)


def blend(sz, disp_ref, pd_ref, hex_ref, weight_ref, pd_force, hex_pull):
    f32, bf16 = jnp.float32, jnp.bfloat16
    rows_h = hex_ref[...] // LANES
    cols_h = lax.rem(hex_ref[...], LANES)
    rows_p = pd_ref[...] // LANES
    cols_p = lax.rem(pd_ref[...], LANES)
    count = rows_h.shape[1]
    tall = -(-sz.rows // 16) * 16
    one_hot = lambda rows, at: (lax.broadcasted_iota(jnp.int32, (rows, count), 0) == at).astype(f32).astype(bf16)
    pick_h, pick_p = one_hot(LANES, cols_h), one_hot(LANES, cols_p)
    row_h, row_p = one_hot(sz.height, rows_h), one_hot(tall, rows_p)
    in_h = lax.broadcasted_iota(jnp.int32, (sz.height, count), 0) == rows_h
    in_p = lax.broadcasted_iota(jnp.int32, (sz.rows, count), 0) == rows_p
    twice = lambda x, axis: jnp.concatenate([x, x], axis=axis)
    gather_h, gather_p = twice(pick_h, 0), twice(pick_p, 0)
    scatter_h, scatter_p = twice(pick_h, 1), twice(pick_p, 1)
    transposed = (((1,), (1,)), ((), ()))
    for axis in range(3):
        hexes = jnp.concatenate(halves_of(disp_ref[axis, 0 : sz.height, :]), axis=1)
        nodes = jnp.concatenate(halves_of(disp_ref[axis, sz.pd : sz.state, :]), axis=1)
        from_h = jnp.dot(hexes, gather_h, preferred_element_type=f32)
        from_p = jnp.dot(nodes, gather_p, preferred_element_type=f32)
        at_h = jnp.sum(jnp.where(in_h, from_h, 0.0), axis=0, keepdims=True)
        at_p = jnp.sum(jnp.where(in_p, from_p, 0.0), axis=0, keepdims=True)
        high, low = halves_of(coupling * weight_ref[...] * (at_h - at_p))
        to_h = jnp.concatenate([row_h * high, row_h * low], axis=1)
        to_p = jnp.concatenate([row_p * high, row_p * low], axis=1)
        hex_pull[axis] = lax.dot_general(to_h, scatter_h, transposed, preferred_element_type=f32)
        pulled = lax.dot_general(to_p, scatter_p, transposed, preferred_element_type=f32)
        pd_force[axis] = pd_force[axis] + pulled[0 : sz.rows, :]


def near_kernel(
    sz, pairs, count, side_list, side_meta, own, own_pos, side, side_first, blend_pd, blend_hex, blend_weight,
    force, hex_pull, table, acc,
):
    acc[...] = jnp.zeros(acc.shape, jnp.float32)
    disp = own.at[:, pl.ds(sz.pd, sz.rows), :]
    spread_nodes(sz, table, 0, own_pos[...], disp[...])
    spread_nodes(sz, table, 1, side_first[:, sz.pos : sz.meta, :], side[:, sz.pd : sz.state, :])
    go = functools.partial(pair_force, sz, table, own_pos, disp, acc, guard=True)
    edge = sz.blocks + sz.halo

    def listed(e, carry):
        a, c, m = pairs[0, e], pairs[1, e], pairs[2, e]

        @pl.when(c < sz.blocks)
        def _():
            go(a, 0, c, m, lane_first=True)

        @pl.when(jnp.logical_and(c < sz.blocks, c != a))
        def _():
            go(c, 0, a, m, lane_first=False)

        @pl.when(c >= edge)
        def _():
            go(a, 1, meta_at(sz, side_meta, "side", jnp.maximum(c - edge, 0)), m, lane_first=True)

        return carry

    lax.fori_loop(0, count[0], listed, 0)

    def listed_beside(e, carry):
        a = meta_at(sz, side_meta, "pair", e)
        c = meta_at(sz, side_meta, "pair", sz.pair_slots + e)
        m = meta_at(sz, side_meta, "pair", 2 * sz.pair_slots + e)

        @pl.when(c >= edge)
        def _():
            go(side_list[jnp.maximum(c - edge, 0)], 1, a, m, lane_first=False)

        return carry

    lax.fori_loop(0, meta_at(sz, side_meta, "count", 0), listed_beside, 0)
    for axis in range(3):
        force[axis] = stiffness * jnp.sum(acc[axis], axis=1)
    blend(sz, own, blend_pd, blend_hex, blend_weight, force, hex_pull)


def far_kernel(
    sz, pairs, count, up_list, above_meta, below_meta, own, own_pos, one, two, one_first, two_first, near,
    force, table, acc,
):
    even = lax.rem(lax.axis_index("wide"), 2) == 0
    acc[...] = jnp.zeros(acc.shape, jnp.float32)
    pos_one, pos_two = one_first[:, sz.pos : sz.meta, :], two_first[:, sz.pos : sz.meta, :]
    disp_one, disp_two = one[:, sz.pd : sz.state, :], two[:, sz.pd : sz.state, :]
    spread_nodes(sz, table, 0, jnp.where(even, pos_one, pos_two), jnp.where(even, disp_one, disp_two))
    spread_nodes(sz, table, 1, jnp.where(even, pos_two, pos_one), jnp.where(even, disp_two, disp_one))
    own_disp = own.at[:, pl.ds(sz.pd, sz.rows), :]
    go = functools.partial(pair_force, sz, table, own_pos, own_disp, acc, guard=False)
    edge = sz.blocks + sz.halo

    def listed(e, carry):
        a, c, m = pairs[0, e], pairs[1, e], pairs[2, e]

        @pl.when(jnp.logical_and(c >= sz.blocks, c < edge))
        def _():
            go(a, 0, meta_at(sz, above_meta, "up", jnp.clip(c - sz.blocks, 0, sz.halo - 1)), m, lane_first=True)

        return carry

    lax.fori_loop(0, count[0], listed, 0)

    def listed_below(e, carry):
        a = meta_at(sz, below_meta, "pair", e)
        c = meta_at(sz, below_meta, "pair", sz.pair_slots + e)
        m = meta_at(sz, below_meta, "pair", 2 * sz.pair_slots + e)

        @pl.when(jnp.logical_and(c >= sz.blocks, c < edge))
        def _():
            go(up_list[jnp.clip(c - sz.blocks, 0, sz.halo - 1)], 1, a, m, lane_first=False)

        return carry

    lax.fori_loop(0, meta_at(sz, below_meta, "count", 0), listed_below, 0)
    for axis in range(3):
        force[axis] = near[axis] + stiffness * jnp.sum(acc[axis], axis=1)


def hex_kernel(sz, first, last, *refs):
    refs = list(refs)
    take = lambda count: [refs.pop(0) for _ in range(count)]
    own, side, one, two, one_side, two_side, force, hex_pull, hex_vel, pd_vel = take(10)
    moduli = take(1)[0]
    outs = take(4) if last else take(3)
    shifted_out = take(1)[0] if first else None
    parts, nodes_low, nodes_high = take(3)
    height = sz.height
    wide = lax.axis_index("wide")
    even = lax.rem(wide, 2) == 0
    low_half = lax.axis_index("narrow") == 0
    shift = jnp.where(low_half, LANES - 1, 1)
    back = LANES - shift
    edge = jnp.where(low_half, 0, LANES - 1)
    signs = (jnp.where(low_half, 1.0, -1.0), None, jnp.where(even, 1.0, -1.0))
    mirrored = lambda axis, x: x if signs[axis] is None else x * signs[axis]

    if first:
        lanes = lax.broadcasted_iota(jnp.int32, (8, LANES), 1)
        last_lane = lanes == LANES - 1
        has_above = jnp.where(wide < lax.axis_size("wide") - 1, 1.0, 0.0)
        for part, start, count in modulus_parts(sz):
            for row in range(0, count, 8):
                at = start + row
                inside = lax.broadcasted_iota(jnp.int32, (8, LANES), 0) + at < height - 1

                def aligned(mine, beside):
                    turned = pltpu.roll(jnp.where(last_lane, beside, mine), 1, axis=1)
                    return jnp.where(inside, jnp.where(low_half, mine, turned), 0.0)

                span = slice(sz.mod + row, sz.mod + row + 8)
                above = aligned(moduli[at : at + 8, :], side[part, span, :]) * has_above
                from_one = aligned(one[part, span, :], one_side[part, span, :])
                from_two = aligned(two[part, span, :], two_side[part, span, :])
                shifted_out[0, at : at + 8, :] = jnp.where(even, above, from_one)
                shifted_out[1, at : at + 8, :] = jnp.where(even, from_two, above)
        moduli = shifted_out

    tall = 16
    lanes = lax.broadcasted_iota(jnp.int32, (tall, LANES), 1)
    at_edge = lanes == edge

    def along_x(r, carry):
        rows = pl.ds(pl.multiple_of(r * tall, tall), tall)
        for layer in range(3):
            for axis in range(3):
                center, flank = ((own, side), (one, one_side), (two, two_side))[layer]
                mine = center[axis, rows, :]
                joined = jnp.where(at_edge, flank[axis, rows, :], mine)
                mine = mirrored(axis, mine)
                other = pltpu.roll(mirrored(axis, joined), shift, axis=1)
                parts[layer, axis, 0, rows, :] = mine + other
                parts[layer, axis, 1, rows, :] = other - mine
        return carry

    lax.fori_loop(0, height // tall, along_x, 0)
    for layer in range(3):
        for axis in range(3):
            for px in range(2):
                parts[layer, axis, px, height : height + 8, :] = jnp.zeros((8, LANES), jnp.float32)
    for axis in range(3):
        for px in range(2):
            nodes_high[axis, px, 0:8, :] = jnp.zeros((8, LANES), jnp.float32)

    shear_by = 1.0 / (2.0 * (1.0 + poisson)) / 16.0
    lame_by = poisson / ((1.0 + poisson) * (1.0 - 2.0 * poisson)) / 16.0
    for r in range(0, height, 8):
        grid = [[[None] * 4 for _ in range(3)] for _ in range(3)]
        for layer in range(3):
            for axis in range(3):
                for px in range(2):
                    here = parts[layer, axis, px, r : r + 8, :]
                    after = parts[layer, axis, px, r + 1 : r + 9, :]
                    grid[layer][axis][px] = here + after
                    grid[layer][axis][2 + px] = after - here
        total = [[None] * 4 for _ in range(3)]
        for place, (bottom, top, at_top) in enumerate(((0, 1, False), (2, 0, True))):
            m = [
                [
                    (grid[bottom][axis][k] + grid[top][axis][k], grid[top][axis][k] - grid[bottom][axis][k])
                    for k in range(4)
                ]
                for axis in range(3)
            ]
            modulus = moduli[place, r : r + 8, :]
            shear = modulus * shear_by
            lame = modulus * lame_by
            damp = modulus * hourglass
            slope = [[m[axis][1][0], m[axis][2][0], m[axis][0][1]] for axis in range(3)]
            trace = lame * (slope[0][0] + slope[1][1] + slope[2][2])
            twice = shear + shear
            stress = [[None] * 3 for _ in range(3)]
            for a in range(3):
                stress[a][a] = twice * slope[a][a] + trace
                for b in range(a + 1, 3):
                    stress[a][b] = shear * (slope[a][b] + slope[b][a])
                    stress[b][a] = stress[a][b]
            for axis in range(3):
                plain = [None, stress[axis][0], stress[axis][1], damp * m[axis][3][0]]
                odd = [stress[axis][2], damp * m[axis][1][1], damp * m[axis][2][1], damp * m[axis][3][1]]
                for k in range(4):
                    if k == 0:
                        value = odd[k] if at_top else -odd[k]
                    else:
                        value = plain[k] + odd[k] if at_top else plain[k] - odd[k]
                    total[axis][k] = value if total[axis][k] is None else total[axis][k] + value
        for axis in range(3):
            for px in range(2):
                even_y, odd_y = total[axis][px], total[axis][2 + px]
                nodes_low[axis, px, r : r + 8, :] = even_y - odd_y
                nodes_high[axis, px, r + 8 : r + 16, :] = even_y + odd_y

    lanes = lax.broadcasted_iota(jnp.int32, (8, LANES), 1)
    keep = lanes != edge
    for r in range(0, height, 8):
        for axis in range(3):
            pair = [
                nodes_low[axis, px, r : r + 8, :] + nodes_high[axis, px, r + 7 : r + 15, :] for px in range(2)
            ]
            moved = jnp.where(keep, pltpu.roll(pair[0] + pair[1], back, axis=1), 0.0)
            element = pair[0] - pair[1] + moved
            element = mirrored(axis, element)
            speed = hex_vel[axis, r : r + 8, :] - time_step * (element + hex_pull[axis, r : r + 8, :])
            place = own[axis, r : r + 8, :] + time_step * speed
            outs[0][axis, r : r + 8, :] = place
            outs[1][axis, r : r + 8, :] = speed
    for axis in range(3):
        speed = pd_vel[axis] + time_step * force[axis]
        place = own[axis, sz.pd : sz.state, :] + time_step * speed
        if last:
            for row in range(sz.rows):
                span = slice(row * LANES, (row + 1) * LANES)
                outs[2][axis : axis + 1, span] = place[row : row + 1, :]
                outs[3][axis : axis + 1, span] = speed[row : row + 1, :]
        else:
            outs[0][axis, sz.pd : sz.state, :] = place
            outs[2][axis] = speed


def local(
    pd_position,
    pd_displace,
    pd_velocity,
    pair_table,
    pair_count,
    up_list,
    side_list,
    hex_displace,
    hex_velocity,
    hex_modulus,
    blend_pd,
    blend_hex,
    blend_weight,
):
    f32 = jnp.float32
    nodes = pd_position.shape[1]
    height, width = hex_displace.shape[2], hex_displace.shape[3]
    sz = Sizes(nodes, height, pair_table.shape[1], up_list.shape[0])
    wide = lax.axis_size("wide")
    near_pairs = [(i, i ^ 1) for i in range(wide) if i ^ 1 < wide]
    next_pairs = [(i, i + 1) for i in range(1, wide - 1, 2)] + [(i + 1, i) for i in range(1, wide - 1, 2)]
    swap_near = lambda x: lax.ppermute(x, "wide", near_pairs)
    swap_next = lambda x: lax.ppermute(x, "wide", next_pairs)
    swap_side = lambda x: lax.ppermute(x, "narrow", [(0, 1), (1, 0)])
    shape = lambda *dims: pltpu.VMEM(dims, f32)

    lists = jnp.concatenate([pair_table.reshape(-1), pair_count, up_list, side_list]).astype(f32)
    lists = jnp.pad(lists, (0, sz.meta_rows * LANES - lists.shape[0])).reshape(sz.meta_rows, LANES)
    own, own_pos, pd_vel = pl.pallas_call(
        functools.partial(pack_kernel, sz),
        out_shape=(shape(3, sz.first, LANES), shape(3, sz.rows, LANES), shape(3, sz.rows, LANES)),
        in_specs=[VM] * 6,
        out_specs=(VM, VM, VM),
        compiler_params=LIMIT,
        name="pack",
    )(
        hex_displace.reshape(3, height, width),
        pd_displace,
        pd_velocity,
        pd_position,
        lists,
        hex_modulus.reshape(height, width),
    )
    hex_vel = hex_velocity.reshape(3, height, width)
    moduli = hex_modulus.reshape(height, width)
    rows_pd = blend_pd.reshape(1, -1)
    rows_hex = blend_hex.reshape(1, -1)
    rows_weight = blend_weight.reshape(1, -1)

    state = (own, own_pos, hex_vel, pd_vel, moduli, None)
    fixed = (sz, pair_table, pair_count, up_list, side_list, rows_pd, rows_hex, rows_weight)
    for step in range(STEPS):
        state = advance(step == 0, step == STEPS - 1, fixed, state, swap_side, swap_near, swap_next)
    hex_out, hex_speed, pd_out, pd_speed = state
    return (pd_out, pd_speed, hex_out.reshape(hex_displace.shape), hex_speed.reshape(hex_velocity.shape))


def advance(first, last, fixed, state, swap_side, swap_near, swap_next):
    f32 = jnp.float32
    shape = lambda *dims: pltpu.VMEM(dims, f32)
    whole = lambda *dims: jax.ShapeDtypeStruct(dims, f32)
    sz, pair_table, pair_count, up_list, side_list, rows_pd, rows_hex, rows_weight = fixed
    own, own_pos, hex_vel, pd_vel, moduli, kept = state
    height = sz.height
    even = lax.rem(lax.axis_index("wide"), 2) == 0
    side = swap_side(own)
    one = swap_near(own)
    two = swap_next(own)
    lists_of = lambda x: x[0, sz.meta : sz.mod, :].astype(jnp.int32)
    if first:
        side_first, one_first, two_first = side, one, two
        side_meta = lists_of(side)
        one_meta, two_meta = lists_of(one), lists_of(two)
        above_meta = jnp.where(even, one_meta, two_meta)
        below_meta = jnp.where(even, two_meta, one_meta)
        kept = (side_first, one_first, two_first, side_meta, above_meta, below_meta)
    side_first, one_first, two_first, side_meta, above_meta, below_meta = kept
    one_side, two_side = map(kept_near, (swap_side(one), swap_side(two)))
    own, own_pos, pd_vel, side, one, two = map(kept_near, (own, own_pos, pd_vel, side, one, two))
    side_first, one_first, two_first = map(kept_near, (side_first, one_first, two_first))
    if not first:
        hex_vel, moduli = map(kept_near, (hex_vel, moduli))
    force, hex_pull = pl.pallas_call(
        functools.partial(near_kernel, sz),
        out_shape=(shape(3, sz.rows, LANES), shape(3, height, LANES)),
        in_specs=[SM] * 4 + [VM] * 7,
        out_specs=(VM, VM),
        scratch_shapes=[
            pltpu.VMEM((2, sz.rows, LANES, LANES), f32),
            pltpu.VMEM((3, sz.rows, 8, LANES), f32),
        ],
        cost_estimate=pl.CostEstimate(flops=60_000_000, transcendentals=2_600_000, bytes_accessed=40_000_000),
        compiler_params=LIMIT,
        name="near",
    )(pair_table, pair_count, side_list, side_meta, own, own_pos, side, side_first, rows_pd, rows_hex, rows_weight)
    force, hex_pull = map(kept_near, (force, hex_pull))
    force = pl.pallas_call(
        functools.partial(far_kernel, sz),
        out_shape=shape(3, sz.rows, LANES),
        in_specs=[SM] * 5 + [VM] * 7,
        out_specs=VM,
        scratch_shapes=[
            pltpu.VMEM((2, sz.rows, LANES, LANES), f32),
            pltpu.VMEM((3, sz.rows, 8, LANES), f32),
        ],
        compiler_params=LIMIT,
        name="far",
    )(
        pair_table, pair_count, up_list, above_meta, below_meta, own, own_pos, one, two, one_first, two_first, force
    )
    force = kept_near(force)
    if last:
        outs = (whole(3, height, LANES), whole(3, height, LANES)) + (whole(3, sz.rows * LANES),) * 2
    else:
        outs = (shape(3, sz.state, LANES), shape(3, height, LANES), shape(3, sz.rows, LANES))
    if first:
        outs = outs + (shape(2, height, LANES),)
    results = pl.pallas_call(
        functools.partial(hex_kernel, sz, first, last),
        out_shape=outs,
        in_specs=[VM] * 11,
        out_specs=tuple(VM for _ in outs),
        scratch_shapes=[
            pltpu.VMEM((3, 3, 2, height + 8, LANES), f32),
            pltpu.VMEM((3, 2, height, LANES), f32),
            pltpu.VMEM((3, 2, height + 8, LANES), f32),
        ],
        compiler_params=LIMIT,
        name="hexes",
    )(own, side, one, two, one_side, two_side, force, hex_pull, hex_vel, pd_vel, moduli)
    if last:
        return results[:4]
    return results[0], own_pos, results[1], results[2], results[3] if first else moduli, kept


def solution(mesh):
    both = ("wide", "narrow")
    in_specs = (
        P(None, both),
        P(None, both),
        P(None, both),
        P(None, both),
        P(both),
        P(both),
        P(both),
        P(None, "wide", None, "narrow"),
        P(None, "wide", None, "narrow"),
        P("wide", None, "narrow"),
        P(both),
        P(both),
        P(both),
    )
    out_specs = (
        P(None, both),
        P(None, both),
        P(None, "wide", None, "narrow"),
        P(None, "wide", None, "narrow"),
    )
    return jax.shard_map(local, mesh=mesh, in_specs=in_specs, out_specs=out_specs, check_vma=False)
```

```python
import functools

import jax
import jax.numpy as jnp
from jax import lax
from jax.experimental import pallas as pl
from jax.experimental.pallas import tpu as pltpu
from jax.sharding import PartitionSpec as P

BLOCK = 256
STEPS = 3
LANES = 128
CHUNK = 64
TOGETHER = 4

stiffness = 20.0
horizon = 3.0
coupling = 10.0
hourglass = 0.15
poisson = 0.3
time_step = 0.1
TINY = 1.2e-38
VM = pl.BlockSpec(memory_space=pltpu.VMEM)
HB = pl.BlockSpec(memory_space=pltpu.HBM)
SM = pl.BlockSpec(memory_space=pltpu.SMEM)
LIMIT = pltpu.CompilerParams(vmem_limit_bytes=24 * 1024 * 1024)
kept_far = lambda x: pltpu.with_memory_space_constraint(x, pltpu.HBM)
kept_near = lambda x: pltpu.with_memory_space_constraint(x, pltpu.VMEM)


class Sizes:
    def __init__(self, nodes, height, pair_slots, halo):
        self.rows = nodes // LANES
        self.height = height
        self.blocks = nodes // BLOCK
        self.pair_slots = pair_slots
        self.halo = halo
        self.pd = height
        self.state = height + self.rows
        self.pos = self.state
        self.meta = self.pos + self.rows
        self.meta_rows = 8
        self.mod = self.meta + self.meta_rows
        self.mod_rows = -(-(height // 3) // 8) * 8
        self.first = self.mod + self.mod_rows


def modulus_parts(sz):
    parts = []
    for part in range(3):
        start = part * sz.mod_rows
        parts.append((part, start, min(sz.mod_rows, sz.height - start)))
    return parts


def pack_kernel(
    sz, counts, ups_in, sides_in, table_in, disp_in, vel_in, pos_in, hex_ref, mod_ref, pd_in, to_in, weight_in,
    send_ref, own_pos, own_vel, lists, moduli, blend_pd, blend_hex, blend_weight,
    ups, sides, table_ref, disp_ref, vel_ref, pos_ref, sems,
):
    moves = (
        (ups_in, ups),
        (sides_in, sides),
        (table_in, table_ref),
        (disp_in, disp_ref),
        (pos_in, pos_ref),
        (vel_in, vel_ref),
        (mod_ref, moduli),
        (hex_ref, send_ref.at[:, pl.ds(0, sz.height), :]),
        (pd_in, blend_pd),
        (to_in, blend_hex),
        (weight_in, blend_weight),
    )
    copies = [pltpu.make_async_copy(source, target, sems.at[k]) for k, (source, target) in enumerate(moves)]
    for copy in copies:
        copy.start()
    for copy in copies[:6]:
        copy.wait()
    lists[...] = jnp.zeros(lists.shape, jnp.int32)
    lists[0:3, 0 : sz.pair_slots] = table_ref[...]
    lane = lax.broadcasted_iota(jnp.int32, (1, LANES), 1)
    for place, ref, size in ((3, counts, 1), (4, ups, sz.halo), (5, sides, sz.halo)):
        row = jnp.zeros((1, LANES), jnp.int32)
        for item in range(size):
            row = jnp.where(lane == item, ref[item], row)
        lists[place : place + 1, :] = row
    for axis in range(3):
        for row in range(sz.rows):
            span = slice(row * LANES, (row + 1) * LANES)
            send_ref[axis, sz.pd + row : sz.pd + row + 1, :] = disp_ref[axis : axis + 1, span]
            own_pos[axis, row : row + 1, :] = pos_ref[axis : axis + 1, span]
            own_vel[axis, row : row + 1, :] = vel_ref[axis : axis + 1, span]
        send_ref[axis, sz.pos : sz.meta, :] = own_pos[axis]
        send_ref[axis, sz.meta : sz.mod, :] = lists[...].astype(jnp.float32)
    for copy in copies[6:]:
        copy.wait()
    for part, start, count in modulus_parts(sz):
        send_ref[part, sz.mod : sz.mod + count, :] = moduli[start : start + count, :]


def selector(sz):
    count = 3 * sz.rows
    part = lax.broadcasted_iota(jnp.int32, (LANES, LANES), 0)
    picks = [
        jnp.where(jnp.logical_and(lax.rem(part, count) == k, part < 3 * count), 1.0, 0.0) for k in range(count)
    ]
    return jnp.concatenate(picks, axis=1).astype(jnp.bfloat16)


def spread_nodes(sz, table, slot, picks, x):
    count = 3 * sz.rows
    flat = x.reshape(count, LANES)
    parts = []
    for _ in range(3):
        rounded = flat.astype(jnp.bfloat16).astype(jnp.float32)
        parts.append(rounded)
        flat = flat - rounded
    stacked = jnp.concatenate(parts + [jnp.zeros((LANES - 3 * count, LANES), jnp.float32)], axis=0)
    turned = stacked.T.astype(jnp.bfloat16)
    width = 8 * LANES
    for start in range(0, count * LANES, width):
        spread = jnp.dot(turned, picks[:, start : start + width], preferred_element_type=jnp.float32)
        for k in range(width // LANES):
            table[slot * count + start // LANES + k] = spread[:, k * LANES : (k + 1) * LANES]


def chunk_forces(sz, pos_table, disp_table, pos_ref, disp, source, target, guard):
    group = 8
    place = jnp.minimum(target, sz.rows - 1)
    lanes = [jnp.broadcast_to(pos_ref[axis, pl.ds(place, 1), :], (group, LANES)) for axis in range(3)]
    moved = [jnp.broadcast_to(disp[axis, pl.ds(place, 1), :], (group, LANES)) for axis in range(3)]
    sums = [jnp.zeros((group, LANES), jnp.float32) for _ in range(3)]
    slot, rest = lax.div(source, sz.rows * LANES), lax.rem(source, sz.rows * LANES)
    entry, start = slot * 3 * sz.rows + lax.div(rest, LANES), lax.rem(rest, LANES)
    for g in range(CHUNK // group):
        span = pl.ds(pl.multiple_of(start + g * group, group), group)
        offset = [lanes[axis] - pos_table[entry + axis * sz.rows, span, :] for axis in range(3)]
        now = [
            offset[axis] + (moved[axis] - disp_table[entry + axis * sz.rows, span, :]) for axis in range(3)
        ]
        rest_sq = offset[0] * offset[0] + offset[1] * offset[1] + offset[2] * offset[2]
        now_sq = now[0] * now[0] + now[1] * now[1] + now[2] * now[2]
        if guard:
            rest_sq = jnp.maximum(rest_sq, TINY)
            now_sq = jnp.maximum(now_sq, TINY)
        rest_inv = lax.rsqrt(rest_sq)
        reach = jnp.maximum(horizon - rest_sq * rest_inv, 0.0)
        scale = (lax.rsqrt(now_sq) - rest_inv) * (reach * reach)
        for axis in range(3):
            sums[axis] = sums[axis] + scale * now[axis]
    return sums


def box_flags(sz, flags, slot, own_pos, pos):
    rows = sz.rows
    lane = lax.broadcasted_iota(jnp.int32, (rows, LANES), 1)
    diagonal = lane == lax.broadcasted_iota(jnp.int32, (rows, LANES), 0)
    along = lambda column: jnp.sum(jnp.where(diagonal, column, 0.0), axis=0, keepdims=True)
    far = 3.0e38
    total = [jnp.zeros((rows, LANES), jnp.float32) for _ in range(LANES // CHUNK)]
    for axis in range(3):
        own = own_pos[axis]
        low = along(jnp.min(own, axis=1, keepdims=True))
        high = along(jnp.max(own, axis=1, keepdims=True))
        for q in range(LANES // CHUNK):
            inside = lane // CHUNK == q
            least = jnp.min(jnp.where(inside, pos[axis], far), axis=1, keepdims=True)
            most = jnp.max(jnp.where(inside, pos[axis], -far), axis=1, keepdims=True)
            gap = jnp.maximum(jnp.maximum(least - high, low - most), 0.0)
            total[q] = total[q] + gap * gap
    for q in range(LANES // CHUNK):
        start = (slot * (LANES // CHUNK) + q) * rows
        flags[start : start + rows, :] = (total[q] < horizon * horizon * 1.001).astype(jnp.int32)


def add_pair(sz, flags, work, target, slot, block, tiles, lane_first):
    halves, quarters = BLOCK // LANES, LANES // CHUNK
    count = work[0]
    for h in range(halves):
        row = halves * block + h
        for hl in range(halves):
            first, second = (hl, h) if lane_first else (h, hl)
            whole = 1 - lax.rem(lax.shift_right_logical(tiles, 2 * first + second), 2)
            place = halves * target + hl
            for q in range(quarters):
                work[1 + 2 * count] = (slot * sz.rows + row) * LANES + q * CHUNK
                work[2 + 2 * count] = place
                count = count + whole * flags[(slot * quarters + q) * sz.rows + row, place]
    work[0] = count


def work_size(sz):
    return 2 * (sz.pair_slots * 24 + 2 * TOGETHER) + 8


def run_work(sz, work, pos_table, disp_table, pos_ref, disp, acc, guard):
    count = work[0]

    def body(i, carry):
        items = []
        for k in range(TOGETHER):
            at = i * TOGETHER + k
            inside = at < count
            source = jnp.where(inside, work[1 + 2 * at], 0)
            target = jnp.where(inside, work[2 + 2 * at], sz.rows)
            items.append((target, chunk_forces(sz, pos_table, disp_table, pos_ref, disp, source, target, guard)))
        for target, sums in items:
            for axis in range(3):
                acc[axis, target] = acc[axis, target] + sums[axis]
        return carry

    lax.fori_loop(0, (count + TOGETHER - 1) // TOGETHER, body, 0)


def total_force(sz, acc, axis):
    return stiffness / (horizon * horizon) * jnp.sum(acc[axis, 0 : sz.rows], axis=1)


def halves_of(x):
    high = x.astype(jnp.bfloat16)
    return high, (x - high.astype(jnp.float32)).astype(jnp.bfloat16)


def blend(sz, disp_ref, pd_ref, hex_ref, weight_ref, pd_force, hex_pull):
    f32, bf16 = jnp.float32, jnp.bfloat16
    rows_h = hex_ref[...] // LANES
    cols_h = lax.rem(hex_ref[...], LANES)
    rows_p = pd_ref[...] // LANES
    cols_p = lax.rem(pd_ref[...], LANES)
    count = rows_h.shape[1]
    tall = -(-sz.rows // 16) * 16
    one_hot = lambda rows, at: (lax.broadcasted_iota(jnp.int32, (rows, count), 0) == at).astype(f32).astype(bf16)
    pick_h, pick_p = one_hot(LANES, cols_h), one_hot(LANES, cols_p)
    row_h, row_p = one_hot(sz.height, rows_h), one_hot(tall, rows_p)
    in_h = lax.broadcasted_iota(jnp.int32, (sz.height, count), 0) == rows_h
    in_p = lax.broadcasted_iota(jnp.int32, (sz.rows, count), 0) == rows_p
    twice = lambda x, axis: jnp.concatenate([x, x], axis=axis)
    gather_h, gather_p = twice(pick_h, 0), twice(pick_p, 0)
    scatter_h, scatter_p = twice(pick_h, 1), twice(pick_p, 1)
    transposed = (((1,), (1,)), ((), ()))
    for axis in range(3):
        hexes = jnp.concatenate(halves_of(disp_ref[axis, 0 : sz.height, :]), axis=1)
        nodes = jnp.concatenate(halves_of(disp_ref[axis, sz.pd : sz.state, :]), axis=1)
        from_h = jnp.dot(hexes, gather_h, preferred_element_type=f32)
        from_p = jnp.dot(nodes, gather_p, preferred_element_type=f32)
        at_h = jnp.sum(jnp.where(in_h, from_h, 0.0), axis=0, keepdims=True)
        at_p = jnp.sum(jnp.where(in_p, from_p, 0.0), axis=0, keepdims=True)
        high, low = halves_of(coupling * weight_ref[...] * (at_h - at_p))
        to_h = jnp.concatenate([row_h * high, row_h * low], axis=1)
        to_p = jnp.concatenate([row_p * high, row_p * low], axis=1)
        hex_pull[axis] = lax.dot_general(to_h, scatter_h, transposed, preferred_element_type=f32)
        pulled = lax.dot_general(to_p, scatter_p, transposed, preferred_element_type=f32)
        pd_force[axis] = pd_force[axis] + pulled[0 : sz.rows, :]


def near_kernel(sz, first, *refs):
    refs = list(refs)
    take = lambda count: [refs.pop(0) for _ in range(count)]
    if first:
        own_lists = take(1)[0]
    else:
        work = take(1)[0]
    own, own_pos, side = take(3)
    if first:
        side_first = side
    else:
        pos_table, picks = take(2)
    blend_pd, blend_hex, blend_weight, force, hex_pull = take(5)
    if first:
        work, pos_table, picks = take(3)
    table, acc = take(2)
    if first:
        side_pos = side_first[:, sz.pos : sz.meta, :]
        flags, flags_scalar, sem = take(3)
        box_flags(sz, flags, 0, own_pos, own_pos)
        box_flags(sz, flags, 1, own_pos, side_pos)
        after = sz.rows * 2 * (LANES // CHUNK)
        flags[after : after + sz.meta_rows, :] = side[0, sz.meta : sz.mod, :].astype(jnp.int32)
        side_lists = flags_scalar.at[pl.ds(after, sz.meta_rows), :]
        copy = pltpu.make_async_copy(flags, flags_scalar, sem)
        copy.start()
        picks[...] = selector(sz)
        spread_nodes(sz, pos_table, 0, picks, own_pos[...])
        spread_nodes(sz, pos_table, 1, picks, side_pos)
    acc[...] = jnp.zeros(acc.shape, jnp.float32)
    disp = own.at[:, pl.ds(sz.pd, sz.rows), :]
    spread_nodes(sz, table, 0, picks, disp[...])
    spread_nodes(sz, table, 1, picks, side[:, sz.pd : sz.state, :])
    if first:
        copy.wait()
        work[0] = 0
        add = functools.partial(add_pair, sz, flags_scalar, work)
        edge = sz.blocks + sz.halo

        def listed(e, carry):
            a, c, m = own_lists[0, e], own_lists[1, e], own_lists[2, e]

            @pl.when(c < sz.blocks)
            def _():
                add(a, 0, c, m, lane_first=True)

            @pl.when(jnp.logical_and(c < sz.blocks, c != a))
            def _():
                add(c, 0, a, m, lane_first=False)

            @pl.when(c >= edge)
            def _():
                add(a, 1, side_lists[5, jnp.maximum(c - edge, 0)], m, lane_first=True)

            return carry

        lax.fori_loop(0, own_lists[3, 0], listed, 0)

        def listed_beside(e, carry):
            a, c, m = side_lists[0, e], side_lists[1, e], side_lists[2, e]

            @pl.when(c >= edge)
            def _():
                add(own_lists[5, jnp.maximum(c - edge, 0)], 1, a, m, lane_first=False)

            return carry

        lax.fori_loop(0, side_lists[3, 0], listed_beside, 0)
    run_work(sz, work, pos_table, table, own_pos, disp, acc, guard=True)
    for axis in range(3):
        force[axis] = total_force(sz, acc, axis)
    blend(sz, own, blend_pd, blend_hex, blend_weight, force, hex_pull)


def far_kernel(sz, first, *refs):
    refs = list(refs)
    take = lambda count: [refs.pop(0) for _ in range(count)]
    if first:
        own_lists = take(1)[0]
    else:
        work = take(1)[0]
    own, own_pos, one, two, picks = take(5)
    if not first:
        pos_table = take(1)[0]
    near, force = take(2)
    if first:
        work, pos_table = take(2)
    table, acc = take(2)
    even = lax.rem(lax.axis_index("wide"), 2) == 0
    disp_one, disp_two = one[:, sz.pd : sz.state, :], two[:, sz.pd : sz.state, :]
    if first:
        pos_one, pos_two = one[:, sz.pos : sz.meta, :], two[:, sz.pos : sz.meta, :]
        pos = (jnp.where(even, pos_one, pos_two), jnp.where(even, pos_two, pos_one))
        flags, flags_scalar, sem = take(3)
        for slot in range(2):
            box_flags(sz, flags, slot, own_pos, pos[slot])
        after = sz.rows * 2 * (LANES // CHUNK)
        below = after + sz.meta_rows
        list_one, list_two = one[0, sz.meta : sz.mod, :], two[0, sz.meta : sz.mod, :]
        flags[after:below, :] = jnp.where(even, list_one, list_two).astype(jnp.int32)
        flags[below : below + sz.meta_rows, :] = jnp.where(even, list_two, list_one).astype(jnp.int32)
        above_lists = flags_scalar.at[pl.ds(after, sz.meta_rows), :]
        below_lists = flags_scalar.at[pl.ds(below, sz.meta_rows), :]
        copy = pltpu.make_async_copy(flags, flags_scalar, sem)
        copy.start()
        for slot in range(2):
            spread_nodes(sz, pos_table, slot, picks, pos[slot])
    acc[...] = jnp.zeros(acc.shape, jnp.float32)
    spread_nodes(sz, table, 0, picks, jnp.where(even, disp_one, disp_two))
    spread_nodes(sz, table, 1, picks, jnp.where(even, disp_two, disp_one))
    if first:
        copy.wait()
        work[0] = 0
        add = functools.partial(add_pair, sz, flags_scalar, work)
        edge = sz.blocks + sz.halo

        def listed(e, carry):
            a, c, m = own_lists[0, e], own_lists[1, e], own_lists[2, e]

            @pl.when(jnp.logical_and(c >= sz.blocks, c < edge))
            def _():
                add(a, 0, above_lists[4, jnp.clip(c - sz.blocks, 0, sz.halo - 1)], m, lane_first=True)

            return carry

        lax.fori_loop(0, own_lists[3, 0], listed, 0)

        def listed_below(e, carry):
            a, c, m = below_lists[0, e], below_lists[1, e], below_lists[2, e]

            @pl.when(jnp.logical_and(c >= sz.blocks, c < edge))
            def _():
                add(own_lists[4, jnp.clip(c - sz.blocks, 0, sz.halo - 1)], 1, a, m, lane_first=False)

            return carry

        lax.fori_loop(0, below_lists[3, 0], listed_below, 0)
    own_disp = own.at[:, pl.ds(sz.pd, sz.rows), :]
    run_work(sz, work, pos_table, table, own_pos, own_disp, acc, guard=False)
    for axis in range(3):
        force[axis] = near[axis] + total_force(sz, acc, axis)


def hex_kernel(sz, first, last, *refs):
    refs = list(refs)
    take = lambda count: [refs.pop(0) for _ in range(count)]
    own, side, one, two, one_side, two_side, force, hex_pull, hex_vel, pd_vel = take(10)
    moduli = take(1)[0]
    outs = take(4) if last else take(3)
    shifted_out = take(1)[0] if first else None
    parts, nodes_low, nodes_high = take(3)
    height = sz.height
    if first:
        speeds, sem = take(2)
        copy = pltpu.make_async_copy(hex_vel, speeds, sem)
        copy.start()
    wide = lax.axis_index("wide")
    even = lax.rem(wide, 2) == 0
    low_half = lax.axis_index("narrow") == 0
    shift = jnp.where(low_half, LANES - 1, 1)
    back = LANES - shift
    edge = jnp.where(low_half, 0, LANES - 1)
    signs = (jnp.where(low_half, 1.0, -1.0), None, jnp.where(even, 1.0, -1.0))
    mirrored = lambda axis, x: x if signs[axis] is None else x * signs[axis]

    if first:
        lanes = lax.broadcasted_iota(jnp.int32, (8, LANES), 1)
        last_lane = lanes == LANES - 1
        has_above = jnp.where(wide < lax.axis_size("wide") - 1, 1.0, 0.0)
        for part, start, count in modulus_parts(sz):
            for row in range(0, count, 8):
                at = start + row
                inside = lax.broadcasted_iota(jnp.int32, (8, LANES), 0) + at < height - 1

                def aligned(mine, beside):
                    turned = pltpu.roll(jnp.where(last_lane, beside, mine), 1, axis=1)
                    return jnp.where(inside, jnp.where(low_half, mine, turned), 0.0)

                span = slice(sz.mod + row, sz.mod + row + 8)
                above = aligned(moduli[at : at + 8, :], side[part, span, :]) * has_above
                from_one = aligned(one[part, span, :], one_side[part, span, :])
                from_two = aligned(two[part, span, :], two_side[part, span, :])
                shifted_out[0, at : at + 8, :] = jnp.where(even, above, from_one)
                shifted_out[1, at : at + 8, :] = jnp.where(even, from_two, above)
        moduli = shifted_out

    tall = 16
    lanes = lax.broadcasted_iota(jnp.int32, (tall, LANES), 1)
    at_edge = lanes == edge

    def along_x(r, carry):
        rows = pl.ds(pl.multiple_of(r * tall, tall), tall)
        for layer in range(3):
            for axis in range(3):
                center, flank = ((own, side), (one, one_side), (two, two_side))[layer]
                mine = center[axis, rows, :]
                joined = jnp.where(at_edge, flank[axis, rows, :], mine)
                mine = mirrored(axis, mine)
                other = pltpu.roll(mirrored(axis, joined), shift, axis=1)
                parts[layer, axis, 0, rows, :] = mine + other
                parts[layer, axis, 1, rows, :] = other - mine
        return carry

    lax.fori_loop(0, height // tall, along_x, 0)
    for layer in range(3):
        for axis in range(3):
            for px in range(2):
                parts[layer, axis, px, height : height + 8, :] = jnp.zeros((8, LANES), jnp.float32)
    for axis in range(3):
        for px in range(2):
            nodes_high[axis, px, 0:8, :] = jnp.zeros((8, LANES), jnp.float32)

    shear_by = 1.0 / (2.0 * (1.0 + poisson)) / 16.0
    lame_by = poisson / ((1.0 + poisson) * (1.0 - 2.0 * poisson)) / 16.0
    for r in range(0, height, 8):
        grid = [[[None] * 4 for _ in range(3)] for _ in range(3)]
        for layer in range(3):
            for axis in range(3):
                for px in range(2):
                    here = parts[layer, axis, px, r : r + 8, :]
                    after = parts[layer, axis, px, r + 1 : r + 9, :]
                    grid[layer][axis][px] = here + after
                    grid[layer][axis][2 + px] = after - here
        total = [[None] * 4 for _ in range(3)]
        for place, (bottom, top, at_top) in enumerate(((0, 1, False), (2, 0, True))):
            m = [
                [
                    (grid[bottom][axis][k] + grid[top][axis][k], grid[top][axis][k] - grid[bottom][axis][k])
                    for k in range(4)
                ]
                for axis in range(3)
            ]
            modulus = moduli[place, r : r + 8, :]
            shear = modulus * shear_by
            lame = modulus * lame_by
            damp = modulus * hourglass
            slope = [[m[axis][1][0], m[axis][2][0], m[axis][0][1]] for axis in range(3)]
            trace = lame * (slope[0][0] + slope[1][1] + slope[2][2])
            twice = shear + shear
            stress = [[None] * 3 for _ in range(3)]
            for a in range(3):
                stress[a][a] = twice * slope[a][a] + trace
                for b in range(a + 1, 3):
                    stress[a][b] = shear * (slope[a][b] + slope[b][a])
                    stress[b][a] = stress[a][b]
            for axis in range(3):
                plain = [None, stress[axis][0], stress[axis][1], damp * m[axis][3][0]]
                odd = [stress[axis][2], damp * m[axis][1][1], damp * m[axis][2][1], damp * m[axis][3][1]]
                for k in range(4):
                    if k == 0:
                        value = odd[k] if at_top else -odd[k]
                    else:
                        value = plain[k] + odd[k] if at_top else plain[k] - odd[k]
                    total[axis][k] = value if total[axis][k] is None else total[axis][k] + value
        for axis in range(3):
            for px in range(2):
                even_y, odd_y = total[axis][px], total[axis][2 + px]
                nodes_low[axis, px, r : r + 8, :] = even_y - odd_y
                nodes_high[axis, px, r + 8 : r + 16, :] = even_y + odd_y

    lanes = lax.broadcasted_iota(jnp.int32, (8, LANES), 1)
    keep = lanes != edge
    if first:
        copy.wait()
        hex_vel = speeds
    for r in range(0, height, 8):
        for axis in range(3):
            pair = [
                nodes_low[axis, px, r : r + 8, :] + nodes_high[axis, px, r + 7 : r + 15, :] for px in range(2)
            ]
            moved = jnp.where(keep, pltpu.roll(pair[0] + pair[1], back, axis=1), 0.0)
            element = pair[0] - pair[1] + moved
            element = mirrored(axis, element)
            speed = hex_vel[axis, r : r + 8, :] - time_step * (element + hex_pull[axis, r : r + 8, :])
            place = own[axis, r : r + 8, :] + time_step * speed
            outs[0][axis, r : r + 8, :] = place
            outs[1][axis, r : r + 8, :] = speed
    for axis in range(3):
        speed = pd_vel[axis] + time_step * force[axis]
        place = own[axis, sz.pd : sz.state, :] + time_step * speed
        if last:
            for row in range(sz.rows):
                span = slice(row * LANES, (row + 1) * LANES)
                outs[2][axis : axis + 1, span] = place[row : row + 1, :]
                outs[3][axis : axis + 1, span] = speed[row : row + 1, :]
        else:
            outs[0][axis, sz.pd : sz.state, :] = place
            outs[2][axis] = speed


def local(
    pd_position,
    pd_displace,
    pd_velocity,
    pair_table,
    pair_count,
    up_list,
    side_list,
    hex_displace,
    hex_velocity,
    hex_modulus,
    blend_pd,
    blend_hex,
    blend_weight,
):
    f32 = jnp.float32
    nodes = pd_position.shape[1]
    height, width = hex_displace.shape[2], hex_displace.shape[3]
    sz = Sizes(nodes, height, pair_table.shape[1], up_list.shape[0])
    wide = lax.axis_size("wide")
    near_pairs = [(i, i ^ 1) for i in range(wide) if i ^ 1 < wide]
    next_pairs = [(i, i + 1) for i in range(1, wide - 1, 2)] + [(i + 1, i) for i in range(1, wide - 1, 2)]
    swap_near = lambda x: lax.ppermute(x, "wide", near_pairs)
    swap_next = lambda x: lax.ppermute(x, "wide", next_pairs)
    swap_side = lambda x: lax.ppermute(x, "narrow", [(0, 1), (1, 0)])
    shape = lambda *dims: pltpu.VMEM(dims, f32)

    rows_of = blend_pd.shape[0]
    own, own_pos, pd_vel, own_lists, moduli, *blends = pl.pallas_call(
        functools.partial(pack_kernel, sz),
        out_shape=(
            shape(3, sz.first, LANES),
            shape(3, sz.rows, LANES),
            shape(3, sz.rows, LANES),
            pltpu.VMEM((sz.meta_rows, LANES), jnp.int32),
            shape(height, LANES),
            pltpu.VMEM((1, rows_of), jnp.int32),
            pltpu.VMEM((1, rows_of), jnp.int32),
            shape(1, rows_of),
        ),
        in_specs=[SM] + [HB] * 11,
        out_specs=(VM,) * 8,
        scratch_shapes=[
            pltpu.SMEM(up_list.shape, jnp.int32),
            pltpu.SMEM(side_list.shape, jnp.int32),
            pltpu.VMEM(pair_table.shape, jnp.int32),
            shape(3, nodes),
            shape(3, nodes),
            shape(3, nodes),
            pltpu.SemaphoreType.DMA((11,)),
        ],
        compiler_params=LIMIT,
        name="pack",
    )(
        pair_count,
        *map(
            kept_far,
            (
                up_list,
                side_list,
                pair_table,
                pd_displace,
                pd_velocity,
                pd_position,
                hex_displace.reshape(3, height, width),
                hex_modulus.reshape(height, width),
                blend_pd.reshape(1, -1),
                blend_hex.reshape(1, -1),
                blend_weight.reshape(1, -1),
            ),
        ),
    )
    hex_vel = hex_velocity.reshape(3, height, width)
    state = (own, own_pos, hex_vel, pd_vel, moduli, None)
    fixed = (sz, own_lists, *blends)
    for step in range(STEPS):
        state = advance(step == 0, step == STEPS - 1, fixed, state, swap_side, swap_near, swap_next)
    hex_out, hex_speed, pd_out, pd_speed = state
    return (pd_out, pd_speed, hex_out.reshape(hex_displace.shape), hex_speed.reshape(hex_velocity.shape))


def advance(first, last, fixed, state, swap_side, swap_near, swap_next):
    f32 = jnp.float32
    shape = lambda *dims: pltpu.VMEM(dims, f32)
    whole = lambda *dims: jax.ShapeDtypeStruct(dims, f32)
    sz, own_lists, *blends = fixed
    blends = list(map(kept_near, blends))
    own, own_pos, hex_vel, pd_vel, moduli, kept = state
    height = sz.height
    side = swap_side(own)
    one = swap_near(own)
    two = swap_next(own)
    listing = jax.ShapeDtypeStruct((work_size(sz),), jnp.int32)
    flag_rows = 2 * sz.rows * (LANES // CHUNK)
    spread = (6 * sz.rows, LANES, LANES)
    scratch = [shape(*spread), shape(3, sz.rows + 1, 8, LANES)]
    if first:
        near_work = far_work = (own_lists,)
        near_table = far_table = ()
        scratch += [
            pltpu.VMEM((flag_rows + 2 * sz.meta_rows, LANES), jnp.int32),
            pltpu.SMEM((flag_rows + 2 * sz.meta_rows, LANES), jnp.int32),
            pltpu.SemaphoreType.DMA,
        ]
    else:
        near_work, far_work, near_table, far_table, picks = kept
        first_ones = tuple(map(kept_near, (near_table, picks)))
        far_table = (kept_near(far_table),)
    one_side, two_side = map(kept_near, (swap_side(one), swap_side(two)))
    own, own_pos, pd_vel, moduli = map(kept_near, (own, own_pos, pd_vel, moduli))
    hex_vel = kept_far(hex_vel) if first else kept_near(hex_vel)
    side, one, two = map(kept_near, (side, one, two))
    if first:
        first_ones = ()
    extra = (listing, shape(*spread), pltpu.VMEM((LANES, 3 * sz.rows * LANES), jnp.bfloat16)) if first else ()
    force, hex_pull, *made = pl.pallas_call(
        functools.partial(near_kernel, sz, first),
        out_shape=(shape(3, sz.rows, LANES), shape(3, height, LANES)) + extra,
        in_specs=[SM] * len(near_work) + [VM] * (6 + len(first_ones)),
        out_specs=(VM, VM) + ((SM, VM, VM) if first else ()),
        scratch_shapes=scratch,
        cost_estimate=pl.CostEstimate(flops=60_000_000, transcendentals=2_600_000, bytes_accessed=40_000_000),
        compiler_params=LIMIT,
        name="near",
    )(*near_work, own, own_pos, side, *first_ones, *blends)
    if first:
        near_work, near_table, picks = (made[0],), made[1], made[2]
    force, hex_pull = map(kept_near, (force, hex_pull))
    results = pl.pallas_call(
        functools.partial(far_kernel, sz, first),
        out_shape=(shape(3, sz.rows, LANES),) + extra[:2],
        in_specs=[SM] * len(far_work) + [VM] * (6 + len(far_table)),
        out_specs=(VM,) + ((SM, VM) if first else ()),
        scratch_shapes=scratch,
        compiler_params=LIMIT,
        name="far",
    )(*far_work, own, own_pos, one, two, kept_near(picks), *far_table, force)
    force = kept_near(results[0])
    if first:
        kept = ((made[0],), (results[1],), near_table, results[2], picks)
    if last:
        outs = (whole(3, height, LANES), whole(3, height, LANES)) + (whole(3, sz.rows * LANES),) * 2
    else:
        outs = (shape(3, sz.state, LANES), shape(3, height, LANES), shape(3, sz.rows, LANES))
    if first:
        outs = outs + (shape(2, height, LANES),)
    results = pl.pallas_call(
        functools.partial(hex_kernel, sz, first, last),
        out_shape=outs,
        in_specs=[VM] * 8 + [HB if first else VM] + [VM] * 2,
        out_specs=tuple(VM for _ in outs),
        scratch_shapes=[
            pltpu.VMEM((3, 3, 2, height + 8, LANES), f32),
            pltpu.VMEM((3, 2, height, LANES), f32),
            pltpu.VMEM((3, 2, height + 8, LANES), f32),
        ]
        + ([shape(3, height, LANES), pltpu.SemaphoreType.DMA] if first else []),
        compiler_params=LIMIT,
        name="hexes",
    )(own, side, one, two, one_side, two_side, force, hex_pull, hex_vel, pd_vel, moduli)
    if last:
        return results[:4]
    return results[0], own_pos, results[1], results[2], results[3] if first else moduli, kept


def solution(mesh):
    both = ("wide", "narrow")
    in_specs = (
        P(None, both),
        P(None, both),
        P(None, both),
        P(None, both),
        P(both),
        P(both),
        P(both),
        P(None, "wide", None, "narrow"),
        P(None, "wide", None, "narrow"),
        P("wide", None, "narrow"),
        P(both),
        P(both),
        P(both),
    )
    out_specs = (
        P(None, both),
        P(None, both),
        P(None, "wide", None, "narrow"),
        P(None, "wide", None, "narrow"),
    )
    return jax.shard_map(local, mesh=mesh, in_specs=in_specs, out_specs=out_specs, check_vma=False)
```

```python
import functools

import jax
import jax.numpy as jnp
from jax import lax
from jax.experimental import pallas as pl
from jax.experimental.pallas import tpu as pltpu
from jax.sharding import PartitionSpec as P

BLOCK = 256
STEPS = 3
LANES = 128
CHUNK = 64
TOGETHER = 4

stiffness = 20.0
horizon = 3.0
coupling = 10.0
hourglass = 0.15
poisson = 0.3
time_step = 0.1
TINY = 1.2e-38
VM = pl.BlockSpec(memory_space=pltpu.VMEM)
HB = pl.BlockSpec(memory_space=pltpu.HBM)
SM = pl.BlockSpec(memory_space=pltpu.SMEM)
LIMIT = pltpu.CompilerParams(vmem_limit_bytes=24 * 1024 * 1024)
kept_far = lambda x: pltpu.with_memory_space_constraint(x, pltpu.HBM)
kept_near = lambda x: pltpu.with_memory_space_constraint(x, pltpu.VMEM)


class Sizes:
    def __init__(self, nodes, height, pair_slots, halo):
        self.rows = nodes // LANES
        self.height = height
        self.blocks = nodes // BLOCK
        self.pair_slots = pair_slots
        self.halo = halo
        self.pd = height
        self.state = height + self.rows
        self.pos = self.state
        self.meta = self.pos + self.rows
        self.meta_rows = 8
        self.first = self.meta + self.meta_rows


def pack_kernel(
    sz, counts, ups_in, sides_in, table_in, disp_in, vel_in, pos_in, hex_ref, mod_ref, pd_in, to_in, weight_in,
    send_ref, own_pos, own_vel, lists, moduli, blend_pd, blend_hex, blend_weight,
    ups, sides, table_ref, disp_ref, vel_ref, pos_ref, sems,
):
    moves = (
        (ups_in, ups),
        (sides_in, sides),
        (table_in, table_ref),
        (disp_in, disp_ref),
        (pos_in, pos_ref),
        (vel_in, vel_ref),
        (mod_ref, moduli),
        (hex_ref, send_ref.at[:, pl.ds(0, sz.height), :]),
        (pd_in, blend_pd),
        (to_in, blend_hex),
        (weight_in, blend_weight),
    )
    copies = [pltpu.make_async_copy(source, target, sems.at[k]) for k, (source, target) in enumerate(moves)]
    for copy in copies:
        copy.start()
    for copy in copies[:6]:
        copy.wait()
    lists[...] = jnp.zeros(lists.shape, jnp.int32)
    lists[0:3, 0 : sz.pair_slots] = table_ref[...]
    lane = lax.broadcasted_iota(jnp.int32, (1, LANES), 1)
    for place, ref, size in ((3, counts, 1), (4, ups, sz.halo), (5, sides, sz.halo)):
        row = jnp.zeros((1, LANES), jnp.int32)
        for item in range(size):
            row = jnp.where(lane == item, ref[item], row)
        lists[place : place + 1, :] = row
    for axis in range(3):
        for row in range(sz.rows):
            span = slice(row * LANES, (row + 1) * LANES)
            send_ref[axis, sz.pd + row : sz.pd + row + 1, :] = disp_ref[axis : axis + 1, span]
            own_pos[axis, row : row + 1, :] = pos_ref[axis : axis + 1, span]
            own_vel[axis, row : row + 1, :] = vel_ref[axis : axis + 1, span]
        send_ref[axis, sz.pos : sz.meta, :] = own_pos[axis]
        send_ref[axis, sz.meta : sz.first, :] = lists[...].astype(jnp.float32)
    for copy in copies[6:]:
        copy.wait()


def selector(sz):
    count = 3 * sz.rows
    part = lax.broadcasted_iota(jnp.int32, (LANES, LANES), 0)
    picks = [
        jnp.where(jnp.logical_and(lax.rem(part, count) == k, part < 3 * count), 1.0, 0.0) for k in range(count)
    ]
    return jnp.concatenate(picks, axis=1).astype(jnp.bfloat16)


def spread_nodes(sz, table, slot, picks, x):
    count = 3 * sz.rows
    flat = x.reshape(count, LANES)
    parts = []
    for _ in range(3):
        rounded = flat.astype(jnp.bfloat16).astype(jnp.float32)
        parts.append(rounded)
        flat = flat - rounded
    stacked = jnp.concatenate(parts + [jnp.zeros((LANES - 3 * count, LANES), jnp.float32)], axis=0)
    turned = stacked.T.astype(jnp.bfloat16)
    width = 8 * LANES
    for start in range(0, count * LANES, width):
        spread = jnp.dot(turned, picks[:, start : start + width], preferred_element_type=jnp.float32)
        for k in range(width // LANES):
            table[slot * count + start // LANES + k] = spread[:, k * LANES : (k + 1) * LANES]


def chunk_forces(sz, pos_table, disp_table, pos_ref, disp, source, target, guard):
    group = 8
    place = jnp.minimum(target, sz.rows - 1)
    lanes = [jnp.broadcast_to(pos_ref[axis, pl.ds(place, 1), :], (group, LANES)) for axis in range(3)]
    moved = [jnp.broadcast_to(disp[axis, pl.ds(place, 1), :], (group, LANES)) for axis in range(3)]
    sums = [jnp.zeros((group, LANES), jnp.float32) for _ in range(3)]
    slot, rest = lax.div(source, sz.rows * LANES), lax.rem(source, sz.rows * LANES)
    entry, start = slot * 3 * sz.rows + lax.div(rest, LANES), lax.rem(rest, LANES)
    for g in range(CHUNK // group):
        span = pl.ds(pl.multiple_of(start + g * group, group), group)
        offset = [lanes[axis] - pos_table[entry + axis * sz.rows, span, :] for axis in range(3)]
        now = [
            offset[axis] + (moved[axis] - disp_table[entry + axis * sz.rows, span, :]) for axis in range(3)
        ]
        rest_sq = offset[0] * offset[0] + offset[1] * offset[1] + offset[2] * offset[2]
        now_sq = now[0] * now[0] + now[1] * now[1] + now[2] * now[2]
        if guard:
            rest_sq = jnp.maximum(rest_sq, TINY)
            now_sq = jnp.maximum(now_sq, TINY)
        rest_inv = lax.rsqrt(rest_sq)
        reach = jnp.maximum(horizon - rest_sq * rest_inv, 0.0)
        scale = (lax.rsqrt(now_sq) - rest_inv) * (reach * reach)
        for axis in range(3):
            sums[axis] = sums[axis] + scale * now[axis]
    return sums


def box_flags(sz, flags, slot, own_pos, pos):
    rows = sz.rows
    lane = lax.broadcasted_iota(jnp.int32, (rows, LANES), 1)
    diagonal = lane == lax.broadcasted_iota(jnp.int32, (rows, LANES), 0)
    along = lambda column: jnp.sum(jnp.where(diagonal, column, 0.0), axis=0, keepdims=True)
    far = 3.0e38
    total = [jnp.zeros((rows, LANES), jnp.float32) for _ in range(LANES // CHUNK)]
    for axis in range(3):
        own = own_pos[axis]
        low = along(jnp.min(own, axis=1, keepdims=True))
        high = along(jnp.max(own, axis=1, keepdims=True))
        for q in range(LANES // CHUNK):
            inside = lane // CHUNK == q
            least = jnp.min(jnp.where(inside, pos[axis], far), axis=1, keepdims=True)
            most = jnp.max(jnp.where(inside, pos[axis], -far), axis=1, keepdims=True)
            gap = jnp.maximum(jnp.maximum(least - high, low - most), 0.0)
            total[q] = total[q] + gap * gap
    for q in range(LANES // CHUNK):
        start = (slot * (LANES // CHUNK) + q) * rows
        flags[start : start + rows, :] = (total[q] < horizon * horizon * 1.001).astype(jnp.int32)


def add_pair(sz, flags, work, target, slot, block, tiles, lane_first):
    halves, quarters = BLOCK // LANES, LANES // CHUNK
    count = work[0]
    for h in range(halves):
        row = halves * block + h
        for hl in range(halves):
            first, second = (hl, h) if lane_first else (h, hl)
            whole = 1 - lax.rem(lax.shift_right_logical(tiles, 2 * first + second), 2)
            place = halves * target + hl
            for q in range(quarters):
                work[1 + 2 * count] = (slot * sz.rows + row) * LANES + q * CHUNK
                work[2 + 2 * count] = place
                count = count + whole * flags[(slot * quarters + q) * sz.rows + row, place]
    work[0] = count


def work_size(sz):
    return 2 * (sz.pair_slots * 24 + 2 * TOGETHER) + 8


def run_work(sz, work, pos_table, disp_table, pos_ref, disp, acc, guard):
    count = work[0]

    def body(i, carry):
        items = []
        for k in range(TOGETHER):
            at = i * TOGETHER + k
            inside = at < count
            source = jnp.where(inside, work[1 + 2 * at], 0)
            target = jnp.where(inside, work[2 + 2 * at], sz.rows)
            items.append((target, chunk_forces(sz, pos_table, disp_table, pos_ref, disp, source, target, guard)))
        for target, sums in items:
            for axis in range(3):
                acc[axis, target] = acc[axis, target] + sums[axis]
        return carry

    lax.fori_loop(0, (count + TOGETHER - 1) // TOGETHER, body, 0)


def total_force(sz, acc, axis):
    return stiffness / (horizon * horizon) * jnp.sum(acc[axis, 0 : sz.rows], axis=1)


def halves_of(x):
    high = x.astype(jnp.bfloat16)
    return high, (x - high.astype(jnp.float32)).astype(jnp.bfloat16)


def blend(sz, disp_ref, pd_ref, hex_ref, weight_ref, pd_force, hex_pull):
    f32, bf16 = jnp.float32, jnp.bfloat16
    rows_h = hex_ref[...] // LANES
    cols_h = lax.rem(hex_ref[...], LANES)
    rows_p = pd_ref[...] // LANES
    cols_p = lax.rem(pd_ref[...], LANES)
    count = rows_h.shape[1]
    tall = -(-sz.rows // 16) * 16
    one_hot = lambda rows, at: (lax.broadcasted_iota(jnp.int32, (rows, count), 0) == at).astype(f32).astype(bf16)
    pick_h, pick_p = one_hot(LANES, cols_h), one_hot(LANES, cols_p)
    row_h, row_p = one_hot(sz.height, rows_h), one_hot(tall, rows_p)
    in_h = lax.broadcasted_iota(jnp.int32, (sz.height, count), 0) == rows_h
    in_p = lax.broadcasted_iota(jnp.int32, (sz.rows, count), 0) == rows_p
    twice = lambda x, axis: jnp.concatenate([x, x], axis=axis)
    gather_h, gather_p = twice(pick_h, 0), twice(pick_p, 0)
    scatter_h, scatter_p = twice(pick_h, 1), twice(pick_p, 1)
    transposed = (((1,), (1,)), ((), ()))
    for axis in range(3):
        hexes = jnp.concatenate(halves_of(disp_ref[axis, 0 : sz.height, :]), axis=1)
        nodes = jnp.concatenate(halves_of(disp_ref[axis, sz.pd : sz.state, :]), axis=1)
        from_h = jnp.dot(hexes, gather_h, preferred_element_type=f32)
        from_p = jnp.dot(nodes, gather_p, preferred_element_type=f32)
        at_h = jnp.sum(jnp.where(in_h, from_h, 0.0), axis=0, keepdims=True)
        at_p = jnp.sum(jnp.where(in_p, from_p, 0.0), axis=0, keepdims=True)
        high, low = halves_of(coupling * weight_ref[...] * (at_h - at_p))
        to_h = jnp.concatenate([row_h * high, row_h * low], axis=1)
        to_p = jnp.concatenate([row_p * high, row_p * low], axis=1)
        hex_pull[axis] = lax.dot_general(to_h, scatter_h, transposed, preferred_element_type=f32)
        pulled = lax.dot_general(to_p, scatter_p, transposed, preferred_element_type=f32)
        pd_force[axis] = pd_force[axis] + pulled[0 : sz.rows, :]


def near_kernel(sz, first, *refs):
    refs = list(refs)
    take = lambda count: [refs.pop(0) for _ in range(count)]
    if first:
        own_lists = take(1)[0]
    else:
        work = take(1)[0]
    own, own_pos, side = take(3)
    if first:
        side_first = side
    else:
        pos_table, picks = take(2)
    blend_pd, blend_hex, blend_weight, force, hex_pull = take(5)
    if first:
        work, pos_table, picks = take(3)
    table, acc = take(2)
    if first:
        side_pos = side_first[:, sz.pos : sz.meta, :]
        flags, flags_scalar, sem = take(3)
        box_flags(sz, flags, 0, own_pos, own_pos)
        box_flags(sz, flags, 1, own_pos, side_pos)
        after = sz.rows * 2 * (LANES // CHUNK)
        flags[after : after + sz.meta_rows, :] = side[0, sz.meta : sz.first, :].astype(jnp.int32)
        side_lists = flags_scalar.at[pl.ds(after, sz.meta_rows), :]
        copy = pltpu.make_async_copy(flags, flags_scalar, sem)
        copy.start()
        picks[...] = selector(sz)
        spread_nodes(sz, pos_table, 0, picks, own_pos[...])
        spread_nodes(sz, pos_table, 1, picks, side_pos)
    acc[...] = jnp.zeros(acc.shape, jnp.float32)
    disp = own.at[:, pl.ds(sz.pd, sz.rows), :]
    spread_nodes(sz, table, 0, picks, disp[...])
    spread_nodes(sz, table, 1, picks, side[:, sz.pd : sz.state, :])
    if first:
        copy.wait()
        work[0] = 0
        add = functools.partial(add_pair, sz, flags_scalar, work)
        edge = sz.blocks + sz.halo

        def listed(e, carry):
            a, c, m = own_lists[0, e], own_lists[1, e], own_lists[2, e]

            @pl.when(c < sz.blocks)
            def _():
                add(a, 0, c, m, lane_first=True)

            @pl.when(jnp.logical_and(c < sz.blocks, c != a))
            def _():
                add(c, 0, a, m, lane_first=False)

            @pl.when(c >= edge)
            def _():
                add(a, 1, side_lists[5, jnp.maximum(c - edge, 0)], m, lane_first=True)

            return carry

        lax.fori_loop(0, own_lists[3, 0], listed, 0)

        def listed_beside(e, carry):
            a, c, m = side_lists[0, e], side_lists[1, e], side_lists[2, e]

            @pl.when(c >= edge)
            def _():
                add(own_lists[5, jnp.maximum(c - edge, 0)], 1, a, m, lane_first=False)

            return carry

        lax.fori_loop(0, side_lists[3, 0], listed_beside, 0)
    run_work(sz, work, pos_table, table, own_pos, disp, acc, guard=True)
    for axis in range(3):
        force[axis] = total_force(sz, acc, axis)
    blend(sz, own, blend_pd, blend_hex, blend_weight, force, hex_pull)


def far_kernel(sz, first, *refs):
    refs = list(refs)
    take = lambda count: [refs.pop(0) for _ in range(count)]
    if first:
        own_lists = take(1)[0]
    else:
        work = take(1)[0]
    own, own_pos, one, two, picks = take(5)
    if not first:
        pos_table = take(1)[0]
    near, force = take(2)
    if first:
        work, pos_table = take(2)
    table, acc = take(2)
    even = lax.rem(lax.axis_index("wide"), 2) == 0
    disp_one, disp_two = one[:, sz.pd : sz.state, :], two[:, sz.pd : sz.state, :]
    if first:
        pos_one, pos_two = one[:, sz.pos : sz.meta, :], two[:, sz.pos : sz.meta, :]
        pos = (jnp.where(even, pos_one, pos_two), jnp.where(even, pos_two, pos_one))
        flags, flags_scalar, sem = take(3)
        for slot in range(2):
            box_flags(sz, flags, slot, own_pos, pos[slot])
        after = sz.rows * 2 * (LANES // CHUNK)
        below = after + sz.meta_rows
        list_one, list_two = one[0, sz.meta : sz.first, :], two[0, sz.meta : sz.first, :]
        flags[after:below, :] = jnp.where(even, list_one, list_two).astype(jnp.int32)
        flags[below : below + sz.meta_rows, :] = jnp.where(even, list_two, list_one).astype(jnp.int32)
        above_lists = flags_scalar.at[pl.ds(after, sz.meta_rows), :]
        below_lists = flags_scalar.at[pl.ds(below, sz.meta_rows), :]
        copy = pltpu.make_async_copy(flags, flags_scalar, sem)
        copy.start()
        for slot in range(2):
            spread_nodes(sz, pos_table, slot, picks, pos[slot])
    acc[...] = jnp.zeros(acc.shape, jnp.float32)
    spread_nodes(sz, table, 0, picks, jnp.where(even, disp_one, disp_two))
    spread_nodes(sz, table, 1, picks, jnp.where(even, disp_two, disp_one))
    if first:
        copy.wait()
        work[0] = 0
        add = functools.partial(add_pair, sz, flags_scalar, work)
        edge = sz.blocks + sz.halo

        def listed(e, carry):
            a, c, m = own_lists[0, e], own_lists[1, e], own_lists[2, e]

            @pl.when(jnp.logical_and(c >= sz.blocks, c < edge))
            def _():
                add(a, 0, above_lists[4, jnp.clip(c - sz.blocks, 0, sz.halo - 1)], m, lane_first=True)

            return carry

        lax.fori_loop(0, own_lists[3, 0], listed, 0)

        def listed_below(e, carry):
            a, c, m = below_lists[0, e], below_lists[1, e], below_lists[2, e]

            @pl.when(jnp.logical_and(c >= sz.blocks, c < edge))
            def _():
                add(own_lists[4, jnp.clip(c - sz.blocks, 0, sz.halo - 1)], 1, a, m, lane_first=False)

            return carry

        lax.fori_loop(0, below_lists[3, 0], listed_below, 0)
    own_disp = own.at[:, pl.ds(sz.pd, sz.rows), :]
    run_work(sz, work, pos_table, table, own_pos, own_disp, acc, guard=False)
    for axis in range(3):
        force[axis] = near[axis] + total_force(sz, acc, axis)


def hex_kernel(sz, first, last, *refs):
    refs = list(refs)
    take = lambda count: [refs.pop(0) for _ in range(count)]
    own, side, one, two, one_side, two_side, force, hex_pull, hex_vel, pd_vel = take(10)
    moduli = take(1)[0]
    if first:
        moduli_side, moduli_below, moduli_below_side = take(3)
    outs = take(4) if last else take(3)
    shifted_out = take(1)[0] if first else None
    parts, nodes_low, nodes_high = take(3)
    height = sz.height
    if first:
        speeds, sem = take(2)
        copy = pltpu.make_async_copy(hex_vel, speeds, sem)
        copy.start()
    wide = lax.axis_index("wide")
    even = lax.rem(wide, 2) == 0
    low_half = lax.axis_index("narrow") == 0
    shift = jnp.where(low_half, LANES - 1, 1)
    back = LANES - shift
    edge = jnp.where(low_half, 0, LANES - 1)
    signs = (jnp.where(low_half, 1.0, -1.0), None, jnp.where(even, 1.0, -1.0))
    mirrored = lambda axis, x: x if signs[axis] is None else x * signs[axis]

    if first:
        lanes = lax.broadcasted_iota(jnp.int32, (8, LANES), 1)
        last_lane = lanes == LANES - 1
        has_above = jnp.where(wide < lax.axis_size("wide") - 1, 1.0, 0.0)
        for row in range(0, height, 8):
            span = slice(row, row + 8)
            inside = lax.broadcasted_iota(jnp.int32, (8, LANES), 0) + row < height - 1

            def aligned(mine, beside):
                turned = pltpu.roll(jnp.where(last_lane, beside, mine), 1, axis=1)
                return jnp.where(inside, jnp.where(low_half, mine, turned), 0.0)

            above = aligned(moduli[span, :], moduli_side[span, :]) * has_above
            below = aligned(moduli_below[span, :], moduli_below_side[span, :])
            shifted_out[0, span, :] = jnp.where(even, above, below)
            shifted_out[1, span, :] = jnp.where(even, below, above)
        moduli = shifted_out

    tall = 16
    lanes = lax.broadcasted_iota(jnp.int32, (tall, LANES), 1)
    at_edge = lanes == edge

    def along_x(r, carry):
        rows = pl.ds(pl.multiple_of(r * tall, tall), tall)
        for layer in range(3):
            for axis in range(3):
                center, flank = ((own, side), (one, one_side), (two, two_side))[layer]
                mine = center[axis, rows, :]
                joined = jnp.where(at_edge, flank[axis, rows, :], mine)
                mine = mirrored(axis, mine)
                other = pltpu.roll(mirrored(axis, joined), shift, axis=1)
                parts[layer, axis, 0, rows, :] = mine + other
                parts[layer, axis, 1, rows, :] = other - mine
        return carry

    lax.fori_loop(0, height // tall, along_x, 0)
    for layer in range(3):
        for axis in range(3):
            for px in range(2):
                parts[layer, axis, px, height : height + 8, :] = jnp.zeros((8, LANES), jnp.float32)
    for axis in range(3):
        for px in range(2):
            nodes_high[axis, px, 0:8, :] = jnp.zeros((8, LANES), jnp.float32)

    shear_by = 1.0 / (2.0 * (1.0 + poisson)) / 16.0
    lame_by = poisson / ((1.0 + poisson) * (1.0 - 2.0 * poisson)) / 16.0
    for r in range(0, height, 8):
        grid = [[[None] * 4 for _ in range(3)] for _ in range(3)]
        for layer in range(3):
            for axis in range(3):
                for px in range(2):
                    here = parts[layer, axis, px, r : r + 8, :]
                    after = parts[layer, axis, px, r + 1 : r + 9, :]
                    grid[layer][axis][px] = here + after
                    grid[layer][axis][2 + px] = after - here
        total = [[None] * 4 for _ in range(3)]
        for place, (bottom, top, at_top) in enumerate(((0, 1, False), (2, 0, True))):
            m = [
                [
                    (grid[bottom][axis][k] + grid[top][axis][k], grid[top][axis][k] - grid[bottom][axis][k])
                    for k in range(4)
                ]
                for axis in range(3)
            ]
            modulus = moduli[place, r : r + 8, :]
            shear = modulus * shear_by
            lame = modulus * lame_by
            damp = modulus * hourglass
            slope = [[m[axis][1][0], m[axis][2][0], m[axis][0][1]] for axis in range(3)]
            trace = lame * (slope[0][0] + slope[1][1] + slope[2][2])
            twice = shear + shear
            stress = [[None] * 3 for _ in range(3)]
            for a in range(3):
                stress[a][a] = twice * slope[a][a] + trace
                for b in range(a + 1, 3):
                    stress[a][b] = shear * (slope[a][b] + slope[b][a])
                    stress[b][a] = stress[a][b]
            for axis in range(3):
                plain = [None, stress[axis][0], stress[axis][1], damp * m[axis][3][0]]
                odd = [stress[axis][2], damp * m[axis][1][1], damp * m[axis][2][1], damp * m[axis][3][1]]
                for k in range(4):
                    if k == 0:
                        value = odd[k] if at_top else -odd[k]
                    else:
                        value = plain[k] + odd[k] if at_top else plain[k] - odd[k]
                    total[axis][k] = value if total[axis][k] is None else total[axis][k] + value
        for axis in range(3):
            for px in range(2):
                even_y, odd_y = total[axis][px], total[axis][2 + px]
                nodes_low[axis, px, r : r + 8, :] = even_y - odd_y
                nodes_high[axis, px, r + 8 : r + 16, :] = even_y + odd_y

    lanes = lax.broadcasted_iota(jnp.int32, (8, LANES), 1)
    keep = lanes != edge
    if first:
        copy.wait()
        hex_vel = speeds
    for r in range(0, height, 8):
        for axis in range(3):
            pair = [
                nodes_low[axis, px, r : r + 8, :] + nodes_high[axis, px, r + 7 : r + 15, :] for px in range(2)
            ]
            moved = jnp.where(keep, pltpu.roll(pair[0] + pair[1], back, axis=1), 0.0)
            element = pair[0] - pair[1] + moved
            element = mirrored(axis, element)
            speed = hex_vel[axis, r : r + 8, :] - time_step * (element + hex_pull[axis, r : r + 8, :])
            place = own[axis, r : r + 8, :] + time_step * speed
            outs[0][axis, r : r + 8, :] = place
            outs[1][axis, r : r + 8, :] = speed
    for axis in range(3):
        speed = pd_vel[axis] + time_step * force[axis]
        place = own[axis, sz.pd : sz.state, :] + time_step * speed
        if last:
            for row in range(sz.rows):
                span = slice(row * LANES, (row + 1) * LANES)
                outs[2][axis : axis + 1, span] = place[row : row + 1, :]
                outs[3][axis : axis + 1, span] = speed[row : row + 1, :]
        else:
            outs[0][axis, sz.pd : sz.state, :] = place
            outs[2][axis] = speed


def local(
    pd_position,
    pd_displace,
    pd_velocity,
    pair_table,
    pair_count,
    up_list,
    side_list,
    hex_displace,
    hex_velocity,
    hex_modulus,
    blend_pd,
    blend_hex,
    blend_weight,
):
    f32 = jnp.float32
    nodes = pd_position.shape[1]
    height, width = hex_displace.shape[2], hex_displace.shape[3]
    sz = Sizes(nodes, height, pair_table.shape[1], up_list.shape[0])
    wide = lax.axis_size("wide")
    near_pairs = [(i, i ^ 1) for i in range(wide) if i ^ 1 < wide]
    next_pairs = [(i, i + 1) for i in range(1, wide - 1, 2)] + [(i + 1, i) for i in range(1, wide - 1, 2)]
    swap_near = lambda x: lax.ppermute(x, "wide", near_pairs)
    swap_next = lambda x: lax.ppermute(x, "wide", next_pairs)
    shift_up = lambda x: lax.ppermute(x, "wide", [(i, i + 1) for i in range(wide - 1)])
    swap_side = lambda x: lax.ppermute(x, "narrow", [(0, 1), (1, 0)])
    shape = lambda *dims: pltpu.VMEM(dims, f32)

    rows_of = blend_pd.shape[0]
    own, own_pos, pd_vel, own_lists, moduli, *blends = pl.pallas_call(
        functools.partial(pack_kernel, sz),
        out_shape=(
            shape(3, sz.first, LANES),
            shape(3, sz.rows, LANES),
            shape(3, sz.rows, LANES),
            pltpu.VMEM((sz.meta_rows, LANES), jnp.int32),
            shape(height, LANES),
            pltpu.VMEM((1, rows_of), jnp.int32),
            pltpu.VMEM((1, rows_of), jnp.int32),
            shape(1, rows_of),
        ),
        in_specs=[SM] + [HB] * 11,
        out_specs=(VM,) * 8,
        scratch_shapes=[
            pltpu.SMEM(up_list.shape, jnp.int32),
            pltpu.SMEM(side_list.shape, jnp.int32),
            pltpu.VMEM(pair_table.shape, jnp.int32),
            shape(3, nodes),
            shape(3, nodes),
            shape(3, nodes),
            pltpu.SemaphoreType.DMA((11,)),
        ],
        compiler_params=LIMIT,
        name="pack",
    )(
        pair_count,
        *map(
            kept_far,
            (
                up_list,
                side_list,
                pair_table,
                pd_displace,
                pd_velocity,
                pd_position,
                hex_displace.reshape(3, height, width),
                hex_modulus.reshape(height, width),
                blend_pd.reshape(1, -1),
                blend_hex.reshape(1, -1),
                blend_weight.reshape(1, -1),
            ),
        ),
    )
    hex_vel = hex_velocity.reshape(3, height, width)
    state = (own, own_pos, hex_vel, pd_vel, moduli, None)
    fixed = (sz, own_lists, *blends)
    for step in range(STEPS):
        state = advance(step == 0, step == STEPS - 1, fixed, state, swap_side, swap_near, swap_next, shift_up)
    hex_out, hex_speed, pd_out, pd_speed = state
    return (pd_out, pd_speed, hex_out.reshape(hex_displace.shape), hex_speed.reshape(hex_velocity.shape))


def advance(first, last, fixed, state, swap_side, swap_near, swap_next, shift_up):
    f32 = jnp.float32
    shape = lambda *dims: pltpu.VMEM(dims, f32)
    whole = lambda *dims: jax.ShapeDtypeStruct(dims, f32)
    sz, own_lists, *blends = fixed
    blends = list(map(kept_near, blends))
    own, own_pos, hex_vel, pd_vel, moduli, kept = state
    height = sz.height
    side = swap_side(own)
    one = swap_near(own)
    two = swap_next(own)
    more = ()
    if first:
        below = shift_up(moduli)
        below_side = swap_side(below)
        more = tuple(map(kept_near, (swap_side(moduli), below, below_side)))
    listing = jax.ShapeDtypeStruct((work_size(sz),), jnp.int32)
    flag_rows = 2 * sz.rows * (LANES // CHUNK)
    spread = (6 * sz.rows, LANES, LANES)
    scratch = [shape(*spread), shape(3, sz.rows + 1, 8, LANES)]
    if first:
        near_work = far_work = (own_lists,)
        near_table = far_table = ()
        scratch += [
            pltpu.VMEM((flag_rows + 2 * sz.meta_rows, LANES), jnp.int32),
            pltpu.SMEM((flag_rows + 2 * sz.meta_rows, LANES), jnp.int32),
            pltpu.SemaphoreType.DMA,
        ]
    else:
        near_work, far_work, near_table, far_table, picks = kept
        first_ones = tuple(map(kept_near, (near_table, picks)))
        far_table = (kept_near(far_table),)
    one_side, two_side = map(kept_near, (swap_side(one), swap_side(two)))
    own, own_pos, pd_vel, moduli = map(kept_near, (own, own_pos, pd_vel, moduli))
    hex_vel = kept_far(hex_vel) if first else kept_near(hex_vel)
    side, one, two = map(kept_near, (side, one, two))
    if first:
        first_ones = ()
    extra = (listing, shape(*spread), pltpu.VMEM((LANES, 3 * sz.rows * LANES), jnp.bfloat16)) if first else ()
    force, hex_pull, *made = pl.pallas_call(
        functools.partial(near_kernel, sz, first),
        out_shape=(shape(3, sz.rows, LANES), shape(3, height, LANES)) + extra,
        in_specs=[SM] * len(near_work) + [VM] * (6 + len(first_ones)),
        out_specs=(VM, VM) + ((SM, VM, VM) if first else ()),
        scratch_shapes=scratch,
        cost_estimate=pl.CostEstimate(flops=60_000_000, transcendentals=2_600_000, bytes_accessed=40_000_000),
        compiler_params=LIMIT,
        name="near",
    )(*near_work, own, own_pos, side, *first_ones, *blends)
    if first:
        near_work, near_table, picks = (made[0],), made[1], made[2]
    force, hex_pull = map(kept_near, (force, hex_pull))
    results = pl.pallas_call(
        functools.partial(far_kernel, sz, first),
        out_shape=(shape(3, sz.rows, LANES),) + extra[:2],
        in_specs=[SM] * len(far_work) + [VM] * (6 + len(far_table)),
        out_specs=(VM,) + ((SM, VM) if first else ()),
        scratch_shapes=scratch,
        compiler_params=LIMIT,
        name="far",
    )(*far_work, own, own_pos, one, two, kept_near(picks), *far_table, force)
    force = kept_near(results[0])
    if first:
        kept = ((made[0],), (results[1],), near_table, results[2], picks)
    if last:
        outs = (whole(3, height, LANES), whole(3, height, LANES)) + (whole(3, sz.rows * LANES),) * 2
    else:
        outs = (shape(3, sz.state, LANES), shape(3, height, LANES), shape(3, sz.rows, LANES))
    if first:
        outs = outs + (shape(2, height, LANES),)
    results = pl.pallas_call(
        functools.partial(hex_kernel, sz, first, last),
        out_shape=outs,
        in_specs=[VM] * 8 + [HB if first else VM] + [VM] * (2 + len(more)),
        out_specs=tuple(VM for _ in outs),
        scratch_shapes=[
            pltpu.VMEM((3, 3, 2, height + 8, LANES), f32),
            pltpu.VMEM((3, 2, height, LANES), f32),
            pltpu.VMEM((3, 2, height + 8, LANES), f32),
        ]
        + ([shape(3, height, LANES), pltpu.SemaphoreType.DMA] if first else []),
        compiler_params=LIMIT,
        name="hexes",
    )(own, side, one, two, one_side, two_side, force, hex_pull, hex_vel, pd_vel, moduli, *more)
    if last:
        return results[:4]
    return results[0], own_pos, results[1], results[2], results[3] if first else moduli, kept


def solution(mesh):
    both = ("wide", "narrow")
    in_specs = (
        P(None, both),
        P(None, both),
        P(None, both),
        P(None, both),
        P(both),
        P(both),
        P(both),
        P(None, "wide", None, "narrow"),
        P(None, "wide", None, "narrow"),
        P("wide", None, "narrow"),
        P(both),
        P(both),
        P(both),
    )
    out_specs = (
        P(None, both),
        P(None, both),
        P(None, "wide", None, "narrow"),
        P(None, "wide", None, "narrow"),
    )
    return jax.shard_map(local, mesh=mesh, in_specs=in_specs, out_specs=out_specs, check_vma=False)
```

```python
import functools

import jax
import jax.numpy as jnp
from jax import lax
from jax.experimental import pallas as pl
from jax.experimental.pallas import tpu as pltpu
from jax.sharding import PartitionSpec as P

BLOCK = 256
STEPS = 3
LANES = 128
CHUNK = 64
TOGETHER = 4
WORK_ROWS = 2
TARGETS = 64

stiffness = 20.0
horizon = 3.0
coupling = 10.0
hourglass = 0.15
poisson = 0.3
time_step = 0.1
TINY = 1.2e-38
VM = pl.BlockSpec(memory_space=pltpu.VMEM)
HB = pl.BlockSpec(memory_space=pltpu.HBM)
SM = pl.BlockSpec(memory_space=pltpu.SMEM)
LIMIT = pltpu.CompilerParams(vmem_limit_bytes=24 * 1024 * 1024)
kept_far = lambda x: pltpu.with_memory_space_constraint(x, pltpu.HBM)
kept_near = lambda x: pltpu.with_memory_space_constraint(x, pltpu.VMEM)


class Sizes:
    def __init__(self, nodes, height, pair_slots, halo):
        self.rows = nodes // LANES
        self.height = height
        self.blocks = nodes // BLOCK
        self.pair_slots = pair_slots
        self.halo = halo
        self.pd = height
        self.state = height + self.rows
        self.pos = self.state
        self.meta = self.pos + self.rows
        self.meta_rows = 8
        self.first = self.meta + self.meta_rows


def pack_kernel(
    sz, counts, ups_in, sides_in, table_in, disp_in, vel_in, pos_in, hex_ref, mod_ref, pd_in, to_in, weight_in,
    send_ref, own_pos, own_vel, lists, moduli, blend_pd, blend_hex, blend_weight,
    ups, sides, table_ref, disp_ref, vel_ref, pos_ref, sems,
):
    moves = (
        (ups_in, ups),
        (sides_in, sides),
        (table_in, table_ref),
        (disp_in, disp_ref),
        (pos_in, pos_ref),
        (vel_in, vel_ref),
        (mod_ref, moduli),
        (hex_ref, send_ref.at[:, pl.ds(0, sz.height), :]),
        (pd_in, blend_pd),
        (to_in, blend_hex),
        (weight_in, blend_weight),
    )
    copies = [pltpu.make_async_copy(source, target, sems.at[k]) for k, (source, target) in enumerate(moves)]
    for copy in copies:
        copy.start()
    for copy in copies[:6]:
        copy.wait()
    lists[...] = jnp.zeros(lists.shape, jnp.int32)
    lists[0:3, 0 : sz.pair_slots] = table_ref[...]
    lane = lax.broadcasted_iota(jnp.int32, (1, LANES), 1)
    for place, ref, size in ((3, counts, 1), (4, ups, sz.halo), (5, sides, sz.halo)):
        row = jnp.zeros((1, LANES), jnp.int32)
        for item in range(size):
            row = jnp.where(lane == item, ref[item], row)
        lists[place : place + 1, :] = row
    for axis in range(3):
        for row in range(sz.rows):
            span = slice(row * LANES, (row + 1) * LANES)
            send_ref[axis, sz.pd + row : sz.pd + row + 1, :] = disp_ref[axis : axis + 1, span]
            own_pos[axis, row : row + 1, :] = pos_ref[axis : axis + 1, span]
            own_vel[axis, row : row + 1, :] = vel_ref[axis : axis + 1, span]
        send_ref[axis, sz.pos : sz.meta, :] = own_pos[axis]
        send_ref[axis, sz.meta : sz.first, :] = lists[...].astype(jnp.float32)
    for copy in copies[6:]:
        copy.wait()


def selector(sz):
    count = 3 * sz.rows
    part = lax.broadcasted_iota(jnp.int32, (LANES, LANES), 0)
    picks = [
        jnp.where(jnp.logical_and(lax.rem(part, count) == k, part < 3 * count), 1.0, 0.0) for k in range(count)
    ]
    return jnp.concatenate(picks, axis=1).astype(jnp.bfloat16)


def spread_nodes(sz, table, slot, picks, x):
    count = 3 * sz.rows
    flat = x.reshape(count, LANES)
    parts = []
    for _ in range(3):
        rounded = flat.astype(jnp.bfloat16).astype(jnp.float32)
        parts.append(rounded)
        flat = flat - rounded
    stacked = jnp.concatenate(parts + [jnp.zeros((LANES - 3 * count, LANES), jnp.float32)], axis=0)
    turned = stacked.T.astype(jnp.bfloat16)
    width = 8 * LANES
    for start in range(0, count * LANES, width):
        spread = jnp.dot(turned, picks[:, start : start + width], preferred_element_type=jnp.float32)
        for k in range(width // LANES):
            table[slot * count + start // LANES + k] = spread[:, k * LANES : (k + 1) * LANES]


def chunk_forces(sz, pos_table, disp_table, pos_ref, disp, source, target, guard):
    group = 8
    place = jnp.minimum(target, sz.rows - 1)
    lanes = [jnp.broadcast_to(pos_ref[axis, pl.ds(place, 1), :], (group, LANES)) for axis in range(3)]
    moved = [jnp.broadcast_to(disp[axis, pl.ds(place, 1), :], (group, LANES)) for axis in range(3)]
    sums = [jnp.zeros((group, LANES), jnp.float32) for _ in range(3)]
    slot, rest = lax.div(source, sz.rows * LANES), lax.rem(source, sz.rows * LANES)
    entry, start = slot * 3 * sz.rows + lax.div(rest, LANES), lax.rem(rest, LANES)
    for g in range(CHUNK // group):
        span = pl.ds(pl.multiple_of(start + g * group, group), group)
        offset = [lanes[axis] - pos_table[entry + axis * sz.rows, span, :] for axis in range(3)]
        now = [
            offset[axis] + (moved[axis] - disp_table[entry + axis * sz.rows, span, :]) for axis in range(3)
        ]
        rest_sq = offset[0] * offset[0] + offset[1] * offset[1] + offset[2] * offset[2]
        now_sq = now[0] * now[0] + now[1] * now[1] + now[2] * now[2]
        if guard:
            rest_sq = jnp.maximum(rest_sq, TINY)
            now_sq = jnp.maximum(now_sq, TINY)
        rest_inv = lax.rsqrt(rest_sq)
        reach = jnp.maximum(horizon - rest_sq * rest_inv, 0.0)
        scale = (lax.rsqrt(now_sq) - rest_inv) * (reach * reach)
        for axis in range(3):
            sums[axis] = sums[axis] + scale * now[axis]
    return sums


def box_flags(sz, flags, slot, own_pos, pos):
    rows = sz.rows
    lane = lax.broadcasted_iota(jnp.int32, (rows, LANES), 1)
    diagonal = lane == lax.broadcasted_iota(jnp.int32, (rows, LANES), 0)
    along = lambda column: jnp.sum(jnp.where(diagonal, column, 0.0), axis=0, keepdims=True)
    far = 3.0e38
    total = [jnp.zeros((rows, LANES), jnp.float32) for _ in range(LANES // CHUNK)]
    for axis in range(3):
        own = own_pos[axis]
        low = along(jnp.min(own, axis=1, keepdims=True))
        high = along(jnp.max(own, axis=1, keepdims=True))
        for q in range(LANES // CHUNK):
            inside = lane // CHUNK == q
            least = jnp.min(jnp.where(inside, pos[axis], far), axis=1, keepdims=True)
            most = jnp.max(jnp.where(inside, pos[axis], -far), axis=1, keepdims=True)
            gap = jnp.maximum(jnp.maximum(least - high, low - most), 0.0)
            total[q] = total[q] + gap * gap
    for q in range(LANES // CHUNK):
        start = (slot * (LANES // CHUNK) + q) * rows
        flags[start : start + rows, :] = (total[q] < horizon * horizon * 1.001).astype(jnp.int32)


def add_pair(sz, flags, work, target, slot, block, tiles, lane_first):
    halves, quarters = BLOCK // LANES, LANES // CHUNK
    count = work[0, 0]
    for h in range(halves):
        row = halves * block + h
        for hl in range(halves):
            first, second = (hl, h) if lane_first else (h, hl)
            whole = 1 - lax.rem(lax.shift_right_logical(tiles, 2 * first + second), 2)
            place = halves * target + hl
            for q in range(quarters):
                source = (slot * sz.rows + row) * LANES + q * CHUNK
                at = count + 1
                work[lax.shift_right_logical(at, 7), lax.bitwise_and(at, LANES - 1)] = source * TARGETS + place
                count = count + whole * flags[(slot * quarters + q) * sz.rows + row, place]
    work[0, 0] = count


def work_shape(sz):
    entries = sz.pair_slots * 24 + 2 * TOGETHER + 1
    return (-(-entries // (8 * LANES)) * 8, LANES)


def move_work(source, target, sem, part):
    if part == 0:
        return pltpu.make_async_copy(source.at[pl.ds(0, WORK_ROWS), :], target.at[pl.ds(0, WORK_ROWS), :], sem)
    return pltpu.make_async_copy(source, target, sem)


def move_rest(source, target, sem, count):
    @pl.when(count >= WORK_ROWS * LANES)
    def _():
        copy = move_work(source, target, sem, 1)
        copy.start()
        copy.wait()


def run_work(sz, work, pos_table, disp_table, pos_ref, disp, acc, guard):
    count = work[0, 0]

    def body(i, carry):
        items = []
        for k in range(TOGETHER):
            at = i * TOGETHER + k
            inside = at < count
            entry = jnp.where(inside, work[lax.shift_right_logical(at + 1, 7), lax.bitwise_and(at + 1, LANES - 1)], 0)
            source = lax.shift_right_logical(entry, 6)
            target = jnp.where(inside, lax.bitwise_and(entry, TARGETS - 1), sz.rows)
            items.append((target, chunk_forces(sz, pos_table, disp_table, pos_ref, disp, source, target, guard)))
        for target, sums in items:
            for axis in range(3):
                acc[axis, target] = acc[axis, target] + sums[axis]
        return carry

    lax.fori_loop(0, (count + TOGETHER - 1) // TOGETHER, body, 0)


def total_force(sz, acc, axis):
    return stiffness / (horizon * horizon) * jnp.sum(acc[axis, 0 : sz.rows], axis=1)


def halves_of(x):
    high = x.astype(jnp.bfloat16)
    return high, (x - high.astype(jnp.float32)).astype(jnp.bfloat16)


def blend(sz, disp_ref, pd_ref, hex_ref, weight_ref, pd_force, hex_pull):
    f32, bf16 = jnp.float32, jnp.bfloat16
    rows_h = hex_ref[...] // LANES
    cols_h = lax.rem(hex_ref[...], LANES)
    rows_p = pd_ref[...] // LANES
    cols_p = lax.rem(pd_ref[...], LANES)
    count = rows_h.shape[1]
    tall = -(-sz.rows // 16) * 16
    one_hot = lambda rows, at: (lax.broadcasted_iota(jnp.int32, (rows, count), 0) == at).astype(f32).astype(bf16)
    pick_h, pick_p = one_hot(LANES, cols_h), one_hot(LANES, cols_p)
    row_h, row_p = one_hot(sz.height, rows_h), one_hot(tall, rows_p)
    in_h = lax.broadcasted_iota(jnp.int32, (sz.height, count), 0) == rows_h
    in_p = lax.broadcasted_iota(jnp.int32, (sz.rows, count), 0) == rows_p
    twice = lambda x, axis: jnp.concatenate([x, x], axis=axis)
    gather_h, gather_p = twice(pick_h, 0), twice(pick_p, 0)
    scatter_h, scatter_p = twice(pick_h, 1), twice(pick_p, 1)
    transposed = (((1,), (1,)), ((), ()))
    for axis in range(3):
        hexes = jnp.concatenate(halves_of(disp_ref[axis, 0 : sz.height, :]), axis=1)
        nodes = jnp.concatenate(halves_of(disp_ref[axis, sz.pd : sz.state, :]), axis=1)
        from_h = jnp.dot(hexes, gather_h, preferred_element_type=f32)
        from_p = jnp.dot(nodes, gather_p, preferred_element_type=f32)
        at_h = jnp.sum(jnp.where(in_h, from_h, 0.0), axis=0, keepdims=True)
        at_p = jnp.sum(jnp.where(in_p, from_p, 0.0), axis=0, keepdims=True)
        high, low = halves_of(coupling * weight_ref[...] * (at_h - at_p))
        to_h = jnp.concatenate([row_h * high, row_h * low], axis=1)
        to_p = jnp.concatenate([row_p * high, row_p * low], axis=1)
        hex_pull[axis] = lax.dot_general(to_h, scatter_h, transposed, preferred_element_type=f32)
        pulled = lax.dot_general(to_p, scatter_p, transposed, preferred_element_type=f32)
        pd_force[axis] = pd_force[axis] + pulled[0 : sz.rows, :]


def near_kernel(sz, first, *refs):
    refs = list(refs)
    take = lambda count: [refs.pop(0) for _ in range(count)]
    if first:
        own_lists = take(1)[0]
    else:
        listed_work = take(1)[0]
    own, own_pos, side = take(3)
    if first:
        side_first = side
    else:
        pos_table, picks = take(2)
    blend_pd, blend_hex, blend_weight, force, hex_pull = take(5)
    if first:
        listed_work, pos_table, picks = take(3)
    table, acc, work, work_sem = take(4)
    fetch = move_work(listed_work, work, work_sem, 0)
    if not first:
        fetch.start()
    if first:
        side_pos = side_first[:, sz.pos : sz.meta, :]
        flags, flags_scalar, sem = take(3)
        box_flags(sz, flags, 0, own_pos, own_pos)
        box_flags(sz, flags, 1, own_pos, side_pos)
        after = sz.rows * 2 * (LANES // CHUNK)
        flags[after : after + sz.meta_rows, :] = side[0, sz.meta : sz.first, :].astype(jnp.int32)
        side_lists = flags_scalar.at[pl.ds(after, sz.meta_rows), :]
        copy = pltpu.make_async_copy(flags, flags_scalar, sem)
        copy.start()
        picks[...] = selector(sz)
        spread_nodes(sz, pos_table, 0, picks, own_pos[...])
        spread_nodes(sz, pos_table, 1, picks, side_pos)
    acc[...] = jnp.zeros(acc.shape, jnp.float32)
    disp = own.at[:, pl.ds(sz.pd, sz.rows), :]
    spread_nodes(sz, table, 0, picks, disp[...])
    spread_nodes(sz, table, 1, picks, side[:, sz.pd : sz.state, :])
    if first:
        copy.wait()
        work[0, 0] = 0
        add = functools.partial(add_pair, sz, flags_scalar, work)
        edge = sz.blocks + sz.halo

        def listed(e, carry):
            a, c, m = own_lists[0, e], own_lists[1, e], own_lists[2, e]

            @pl.when(c < sz.blocks)
            def _():
                add(a, 0, c, m, lane_first=True)

            @pl.when(jnp.logical_and(c < sz.blocks, c != a))
            def _():
                add(c, 0, a, m, lane_first=False)

            @pl.when(c >= edge)
            def _():
                add(a, 1, side_lists[5, jnp.maximum(c - edge, 0)], m, lane_first=True)

            return carry

        lax.fori_loop(0, own_lists[3, 0], listed, 0)

        def listed_beside(e, carry):
            a, c, m = side_lists[0, e], side_lists[1, e], side_lists[2, e]

            @pl.when(c >= edge)
            def _():
                add(own_lists[5, jnp.maximum(c - edge, 0)], 1, a, m, lane_first=False)

            return carry

        lax.fori_loop(0, side_lists[3, 0], listed_beside, 0)
        keep = move_work(work, listed_work, work_sem, 0)
        keep.start()
    else:
        fetch.wait()
        move_rest(listed_work, work, work_sem, work[0, 0])
    run_work(sz, work, pos_table, table, own_pos, disp, acc, guard=True)
    for axis in range(3):
        force[axis] = total_force(sz, acc, axis)
    blend(sz, own, blend_pd, blend_hex, blend_weight, force, hex_pull)
    if first:
        keep.wait()
        move_rest(work, listed_work, work_sem, work[0, 0])


def far_kernel(sz, first, *refs):
    refs = list(refs)
    take = lambda count: [refs.pop(0) for _ in range(count)]
    if first:
        own_lists = take(1)[0]
    else:
        listed_work = take(1)[0]
    own, own_pos, one, two, picks = take(5)
    if not first:
        pos_table = take(1)[0]
    near, force = take(2)
    if first:
        listed_work, pos_table = take(2)
    table, acc, work, work_sem = take(4)
    fetch = move_work(listed_work, work, work_sem, 0)
    if not first:
        fetch.start()
    even = lax.rem(lax.axis_index("wide"), 2) == 0
    disp_one, disp_two = one[:, sz.pd : sz.state, :], two[:, sz.pd : sz.state, :]
    if first:
        pos_one, pos_two = one[:, sz.pos : sz.meta, :], two[:, sz.pos : sz.meta, :]
        pos = (jnp.where(even, pos_one, pos_two), jnp.where(even, pos_two, pos_one))
        flags, flags_scalar, sem = take(3)
        for slot in range(2):
            box_flags(sz, flags, slot, own_pos, pos[slot])
        after = sz.rows * 2 * (LANES // CHUNK)
        below = after + sz.meta_rows
        list_one, list_two = one[0, sz.meta : sz.first, :], two[0, sz.meta : sz.first, :]
        flags[after:below, :] = jnp.where(even, list_one, list_two).astype(jnp.int32)
        flags[below : below + sz.meta_rows, :] = jnp.where(even, list_two, list_one).astype(jnp.int32)
        above_lists = flags_scalar.at[pl.ds(after, sz.meta_rows), :]
        below_lists = flags_scalar.at[pl.ds(below, sz.meta_rows), :]
        copy = pltpu.make_async_copy(flags, flags_scalar, sem)
        copy.start()
        for slot in range(2):
            spread_nodes(sz, pos_table, slot, picks, pos[slot])
    acc[...] = jnp.zeros(acc.shape, jnp.float32)
    spread_nodes(sz, table, 0, picks, jnp.where(even, disp_one, disp_two))
    spread_nodes(sz, table, 1, picks, jnp.where(even, disp_two, disp_one))
    if first:
        copy.wait()
        work[0, 0] = 0
        add = functools.partial(add_pair, sz, flags_scalar, work)
        edge = sz.blocks + sz.halo

        def listed(e, carry):
            a, c, m = own_lists[0, e], own_lists[1, e], own_lists[2, e]

            @pl.when(jnp.logical_and(c >= sz.blocks, c < edge))
            def _():
                add(a, 0, above_lists[4, jnp.clip(c - sz.blocks, 0, sz.halo - 1)], m, lane_first=True)

            return carry

        lax.fori_loop(0, own_lists[3, 0], listed, 0)

        def listed_below(e, carry):
            a, c, m = below_lists[0, e], below_lists[1, e], below_lists[2, e]

            @pl.when(jnp.logical_and(c >= sz.blocks, c < edge))
            def _():
                add(own_lists[4, jnp.clip(c - sz.blocks, 0, sz.halo - 1)], 1, a, m, lane_first=False)

            return carry

        lax.fori_loop(0, below_lists[3, 0], listed_below, 0)
        keep = move_work(work, listed_work, work_sem, 0)
        keep.start()
    else:
        fetch.wait()
        move_rest(listed_work, work, work_sem, work[0, 0])
    own_disp = own.at[:, pl.ds(sz.pd, sz.rows), :]
    run_work(sz, work, pos_table, table, own_pos, own_disp, acc, guard=False)
    for axis in range(3):
        force[axis] = near[axis] + total_force(sz, acc, axis)
    if first:
        keep.wait()
        move_rest(work, listed_work, work_sem, work[0, 0])


def hex_kernel(sz, first, last, *refs):
    refs = list(refs)
    take = lambda count: [refs.pop(0) for _ in range(count)]
    own, side, one, two, one_side, two_side, force, hex_pull, hex_vel, pd_vel = take(10)
    moduli = take(1)[0]
    if first:
        moduli_side, moduli_below, moduli_below_side = take(3)
    outs = take(4) if last else take(3)
    shifted_out = take(1)[0] if first else None
    parts, nodes_low, nodes_high = take(3)
    height = sz.height
    if last:
        results, outs = outs, take(4)
        out_sems = take(1)[0]
        half = height // 16 * 8

        def leave(k, rows):
            place = outs[k].at[:, rows, :], results[k].at[:, rows, :]
            return pltpu.make_async_copy(*place, out_sems.at[2 * k + (0 if rows.start == 0 else 1)])

        leaving = [leave(k, rows) for rows in (pl.ds(0, half), pl.ds(half, height - half)) for k in range(2)]
        leaving += [pltpu.make_async_copy(outs[k], results[k], out_sems.at[k + 2]) for k in (2, 3)]
    if first:
        speeds, sem = take(2)
        copy = pltpu.make_async_copy(hex_vel, speeds, sem)
        copy.start()
    wide = lax.axis_index("wide")
    even = lax.rem(wide, 2) == 0
    low_half = lax.axis_index("narrow") == 0
    shift = jnp.where(low_half, LANES - 1, 1)
    back = LANES - shift
    edge = jnp.where(low_half, 0, LANES - 1)
    signs = (jnp.where(low_half, 1.0, -1.0), None, jnp.where(even, 1.0, -1.0))
    mirrored = lambda axis, x: x if signs[axis] is None else x * signs[axis]

    if first:
        lanes = lax.broadcasted_iota(jnp.int32, (8, LANES), 1)
        last_lane = lanes == LANES - 1
        has_above = jnp.where(wide < lax.axis_size("wide") - 1, 1.0, 0.0)
        for row in range(0, height, 8):
            span = slice(row, row + 8)
            inside = lax.broadcasted_iota(jnp.int32, (8, LANES), 0) + row < height - 1

            def aligned(mine, beside):
                turned = pltpu.roll(jnp.where(last_lane, beside, mine), 1, axis=1)
                return jnp.where(inside, jnp.where(low_half, mine, turned), 0.0)

            above = aligned(moduli[span, :], moduli_side[span, :]) * has_above
            below = aligned(moduli_below[span, :], moduli_below_side[span, :])
            shifted_out[0, span, :] = jnp.where(even, above, below)
            shifted_out[1, span, :] = jnp.where(even, below, above)
        moduli = shifted_out

    for axis in range(3):
        speed = pd_vel[axis] + time_step * force[axis]
        place = own[axis, sz.pd : sz.state, :] + time_step * speed
        if last:
            for row in range(sz.rows):
                span = slice(row * LANES, (row + 1) * LANES)
                outs[2][axis : axis + 1, span] = place[row : row + 1, :]
                outs[3][axis : axis + 1, span] = speed[row : row + 1, :]
        else:
            outs[0][axis, sz.pd : sz.state, :] = place
            outs[2][axis] = speed
    if last:
        for copy in leaving[4:]:
            copy.start()

    tall = 16
    lanes = lax.broadcasted_iota(jnp.int32, (tall, LANES), 1)
    at_edge = lanes == edge

    def along_x(r, carry):
        rows = pl.ds(pl.multiple_of(r * tall, tall), tall)
        for layer in range(3):
            for axis in range(3):
                center, flank = ((own, side), (one, one_side), (two, two_side))[layer]
                mine = center[axis, rows, :]
                joined = jnp.where(at_edge, flank[axis, rows, :], mine)
                mine = mirrored(axis, mine)
                other = pltpu.roll(mirrored(axis, joined), shift, axis=1)
                parts[layer, axis, 0, rows, :] = mine + other
                parts[layer, axis, 1, rows, :] = other - mine
        return carry

    lax.fori_loop(0, height // tall, along_x, 0)
    for layer in range(3):
        for axis in range(3):
            for px in range(2):
                parts[layer, axis, px, height : height + 8, :] = jnp.zeros((8, LANES), jnp.float32)
    for axis in range(3):
        for px in range(2):
            nodes_high[axis, px, 0:8, :] = jnp.zeros((8, LANES), jnp.float32)

    shear_by = 1.0 / (2.0 * (1.0 + poisson)) / 16.0
    lame_by = poisson / ((1.0 + poisson) * (1.0 - 2.0 * poisson)) / 16.0
    for r in range(0, height, 8):
        grid = [[[None] * 4 for _ in range(3)] for _ in range(3)]
        for layer in range(3):
            for axis in range(3):
                for px in range(2):
                    here = parts[layer, axis, px, r : r + 8, :]
                    after = parts[layer, axis, px, r + 1 : r + 9, :]
                    grid[layer][axis][px] = here + after
                    grid[layer][axis][2 + px] = after - here
        total = [[None] * 4 for _ in range(3)]
        for place, (bottom, top, at_top) in enumerate(((0, 1, False), (2, 0, True))):
            m = [
                [
                    (grid[bottom][axis][k] + grid[top][axis][k], grid[top][axis][k] - grid[bottom][axis][k])
                    for k in range(4)
                ]
                for axis in range(3)
            ]
            modulus = moduli[place, r : r + 8, :]
            shear = modulus * shear_by
            lame = modulus * lame_by
            damp = modulus * hourglass
            slope = [[m[axis][1][0], m[axis][2][0], m[axis][0][1]] for axis in range(3)]
            trace = lame * (slope[0][0] + slope[1][1] + slope[2][2])
            twice = shear + shear
            stress = [[None] * 3 for _ in range(3)]
            for a in range(3):
                stress[a][a] = twice * slope[a][a] + trace
                for b in range(a + 1, 3):
                    stress[a][b] = shear * (slope[a][b] + slope[b][a])
                    stress[b][a] = stress[a][b]
            for axis in range(3):
                plain = [None, stress[axis][0], stress[axis][1], damp * m[axis][3][0]]
                odd = [stress[axis][2], damp * m[axis][1][1], damp * m[axis][2][1], damp * m[axis][3][1]]
                for k in range(4):
                    if k == 0:
                        value = odd[k] if at_top else -odd[k]
                    else:
                        value = plain[k] + odd[k] if at_top else plain[k] - odd[k]
                    total[axis][k] = value if total[axis][k] is None else total[axis][k] + value
        for axis in range(3):
            for px in range(2):
                even_y, odd_y = total[axis][px], total[axis][2 + px]
                nodes_low[axis, px, r : r + 8, :] = even_y - odd_y
                nodes_high[axis, px, r + 8 : r + 16, :] = even_y + odd_y

    lanes = lax.broadcasted_iota(jnp.int32, (8, LANES), 1)
    keep = lanes != edge
    if first:
        copy.wait()
        hex_vel = speeds
    for r in range(0, height, 8):
        for axis in range(3):
            pair = [
                nodes_low[axis, px, r : r + 8, :] + nodes_high[axis, px, r + 7 : r + 15, :] for px in range(2)
            ]
            moved = jnp.where(keep, pltpu.roll(pair[0] + pair[1], back, axis=1), 0.0)
            element = pair[0] - pair[1] + moved
            element = mirrored(axis, element)
            speed = hex_vel[axis, r : r + 8, :] - time_step * (element + hex_pull[axis, r : r + 8, :])
            place = own[axis, r : r + 8, :] + time_step * speed
            outs[0][axis, r : r + 8, :] = place
            outs[1][axis, r : r + 8, :] = speed
        if last and r + 8 == half:
            for copy in leaving[:2]:
                copy.start()
    if last:
        for copy in leaving[2:4]:
            copy.start()
        for copy in leaving:
            copy.wait()


def local(
    pd_position,
    pd_displace,
    pd_velocity,
    pair_table,
    pair_count,
    up_list,
    side_list,
    hex_displace,
    hex_velocity,
    hex_modulus,
    blend_pd,
    blend_hex,
    blend_weight,
):
    f32 = jnp.float32
    nodes = pd_position.shape[1]
    height, width = hex_displace.shape[2], hex_displace.shape[3]
    sz = Sizes(nodes, height, pair_table.shape[1], up_list.shape[0])
    wide = lax.axis_size("wide")
    near_pairs = [(i, i ^ 1) for i in range(wide) if i ^ 1 < wide]
    next_pairs = [(i, i + 1) for i in range(1, wide - 1, 2)] + [(i + 1, i) for i in range(1, wide - 1, 2)]
    swap_near = lambda x: lax.ppermute(x, "wide", near_pairs)
    swap_next = lambda x: lax.ppermute(x, "wide", next_pairs)
    shift_up = lambda x: lax.ppermute(x, "wide", [(i, i + 1) for i in range(wide - 1)])
    swap_side = lambda x: lax.ppermute(x, "narrow", [(0, 1), (1, 0)])
    shape = lambda *dims: pltpu.VMEM(dims, f32)

    rows_of = blend_pd.shape[0]
    own, own_pos, pd_vel, own_lists, moduli, *blends = pl.pallas_call(
        functools.partial(pack_kernel, sz),
        out_shape=(
            shape(3, sz.first, LANES),
            shape(3, sz.rows, LANES),
            shape(3, sz.rows, LANES),
            pltpu.VMEM((sz.meta_rows, LANES), jnp.int32),
            shape(height, LANES),
            pltpu.VMEM((1, rows_of), jnp.int32),
            pltpu.VMEM((1, rows_of), jnp.int32),
            shape(1, rows_of),
        ),
        in_specs=[SM] + [HB] * 11,
        out_specs=(VM,) * 8,
        scratch_shapes=[
            pltpu.SMEM(up_list.shape, jnp.int32),
            pltpu.SMEM(side_list.shape, jnp.int32),
            pltpu.VMEM(pair_table.shape, jnp.int32),
            shape(3, nodes),
            shape(3, nodes),
            shape(3, nodes),
            pltpu.SemaphoreType.DMA((11,)),
        ],
        compiler_params=LIMIT,
        name="pack",
    )(
        pair_count,
        *map(
            kept_far,
            (
                up_list,
                side_list,
                pair_table,
                pd_displace,
                pd_velocity,
                pd_position,
                hex_displace.reshape(3, height, width),
                hex_modulus.reshape(height, width),
                blend_pd.reshape(1, -1),
                blend_hex.reshape(1, -1),
                blend_weight.reshape(1, -1),
            ),
        ),
    )
    hex_vel = hex_velocity.reshape(3, height, width)
    state = (own, own_pos, hex_vel, pd_vel, moduli, None)
    fixed = (sz, own_lists, *blends)
    for step in range(STEPS):
        state = advance(step == 0, step == STEPS - 1, fixed, state, swap_side, swap_near, swap_next, shift_up)
    hex_out, hex_speed, pd_out, pd_speed = state
    return (pd_out, pd_speed, hex_out.reshape(hex_displace.shape), hex_speed.reshape(hex_velocity.shape))


def advance(first, last, fixed, state, swap_side, swap_near, swap_next, shift_up):
    f32 = jnp.float32
    shape = lambda *dims: pltpu.VMEM(dims, f32)
    whole = lambda *dims: jax.ShapeDtypeStruct(dims, f32)
    sz, own_lists, *blends = fixed
    blends = list(map(kept_near, blends))
    own, own_pos, hex_vel, pd_vel, moduli, kept = state
    height = sz.height
    side = swap_side(own)
    one = swap_near(own)
    two = swap_next(own)
    more = ()
    if first:
        below = shift_up(moduli)
        below_side = swap_side(below)
        more = tuple(map(kept_near, (swap_side(moduli), below, below_side)))
    listing = pltpu.VMEM(work_shape(sz), jnp.int32)
    flag_rows = 2 * sz.rows * (LANES // CHUNK)
    spread = (6 * sz.rows, LANES, LANES)
    scratch = [
        shape(*spread),
        shape(3, sz.rows + 1, 8, LANES),
        pltpu.SMEM(work_shape(sz), jnp.int32),
        pltpu.SemaphoreType.DMA,
    ]
    if first:
        near_work = far_work = (own_lists,)
        near_table = far_table = ()
        scratch += [
            pltpu.VMEM((flag_rows + 2 * sz.meta_rows, LANES), jnp.int32),
            pltpu.SMEM((flag_rows + 2 * sz.meta_rows, LANES), jnp.int32),
            pltpu.SemaphoreType.DMA,
        ]
    else:
        near_work, far_work, near_table, far_table, picks = kept
        near_work, far_work = (kept_near(near_work[0]),), (kept_near(far_work[0]),)
        first_ones = tuple(map(kept_near, (near_table, picks)))
        far_table = (kept_near(far_table),)
    one_side, two_side = map(kept_near, (swap_side(one), swap_side(two)))
    own, own_pos, pd_vel, moduli = map(kept_near, (own, own_pos, pd_vel, moduli))
    hex_vel = kept_far(hex_vel) if first else kept_near(hex_vel)
    side, one, two = map(kept_near, (side, one, two))
    if first:
        first_ones = ()
    extra = (listing, shape(*spread), pltpu.VMEM((LANES, 3 * sz.rows * LANES), jnp.bfloat16)) if first else ()
    force, hex_pull, *made = pl.pallas_call(
        functools.partial(near_kernel, sz, first),
        out_shape=(shape(3, sz.rows, LANES), shape(3, height, LANES)) + extra,
        in_specs=[SM if first else VM] + [VM] * (6 + len(first_ones)),
        out_specs=(VM, VM) + ((VM,) * 3 if first else ()),
        scratch_shapes=scratch,
        cost_estimate=pl.CostEstimate(flops=60_000_000, transcendentals=2_600_000, bytes_accessed=40_000_000),
        compiler_params=LIMIT,
        name="near",
    )(*near_work, own, own_pos, side, *first_ones, *blends)
    if first:
        near_work, near_table, picks = (made[0],), made[1], made[2]
    force, hex_pull = map(kept_near, (force, hex_pull))
    results = pl.pallas_call(
        functools.partial(far_kernel, sz, first),
        out_shape=(shape(3, sz.rows, LANES),) + extra[:2],
        in_specs=[SM if first else VM] + [VM] * (6 + len(far_table)),
        out_specs=(VM,) + ((VM,) * 2 if first else ()),
        scratch_shapes=scratch,
        compiler_params=LIMIT,
        name="far",
    )(*far_work, own, own_pos, one, two, kept_near(picks), *far_table, force)
    force = kept_near(results[0])
    if first:
        kept = ((made[0],), (results[1],), near_table, results[2], picks)
    if last:
        outs = (whole(3, height, LANES), whole(3, height, LANES)) + (whole(3, sz.rows * LANES),) * 2
    else:
        outs = (shape(3, sz.state, LANES), shape(3, height, LANES), shape(3, sz.rows, LANES))
    if first:
        outs = outs + (shape(2, height, LANES),)
    results = pl.pallas_call(
        functools.partial(hex_kernel, sz, first, last),
        out_shape=outs,
        in_specs=[VM] * 8 + [HB if first else VM] + [VM] * (2 + len(more)),
        out_specs=tuple(HB if last else VM for _ in outs),
        scratch_shapes=[
            pltpu.VMEM((3, 3, 2, height + 8, LANES), f32),
            pltpu.VMEM((3, 2, height, LANES), f32),
            pltpu.VMEM((3, 2, height + 8, LANES), f32),
        ]
        + ([shape(3, height, LANES), pltpu.SemaphoreType.DMA] if first else [])
        + ([shape(*out.shape) for out in outs] + [pltpu.SemaphoreType.DMA((6,))] if last else []),
        compiler_params=LIMIT,
        name="hexes",
    )(own, side, one, two, one_side, two_side, force, hex_pull, hex_vel, pd_vel, moduli, *more)
    if last:
        return results[:4]
    return results[0], own_pos, results[1], results[2], results[3] if first else moduli, kept


def solution(mesh):
    both = ("wide", "narrow")
    in_specs = (
        P(None, both),
        P(None, both),
        P(None, both),
        P(None, both),
        P(both),
        P(both),
        P(both),
        P(None, "wide", None, "narrow"),
        P(None, "wide", None, "narrow"),
        P("wide", None, "narrow"),
        P(both),
        P(both),
        P(both),
    )
    out_specs = (
        P(None, both),
        P(None, both),
        P(None, "wide", None, "narrow"),
        P(None, "wide", None, "narrow"),
    )
    return jax.shard_map(local, mesh=mesh, in_specs=in_specs, out_specs=out_specs, check_vma=False)
```

```python
import functools

import jax
import jax.numpy as jnp
from jax import lax
from jax.experimental import pallas as pl
from jax.experimental.pallas import tpu as pltpu
from jax.sharding import PartitionSpec as P

BLOCK = 256
STEPS = 3
LANES = 128
CHUNK = 64
TOGETHER = 6
WORK_ROWS = 2
TARGETS = 64

stiffness = 20.0
horizon = 3.0
coupling = 10.0
hourglass = 0.15
poisson = 0.3
time_step = 0.1
TINY = 1.2e-38
VM = pl.BlockSpec(memory_space=pltpu.VMEM)
HB = pl.BlockSpec(memory_space=pltpu.HBM)
SM = pl.BlockSpec(memory_space=pltpu.SMEM)
LIMIT = pltpu.CompilerParams(vmem_limit_bytes=24 * 1024 * 1024)
kept_far = lambda x: pltpu.with_memory_space_constraint(x, pltpu.HBM)
kept_near = lambda x: pltpu.with_memory_space_constraint(x, pltpu.VMEM)


class Sizes:
    def __init__(self, nodes, height, pair_slots, halo):
        self.rows = nodes // LANES
        self.height = height
        self.blocks = nodes // BLOCK
        self.pair_slots = pair_slots
        self.halo = halo
        self.pd = height
        self.state = height + self.rows
        self.pos = self.state
        self.meta = self.pos + self.rows
        self.meta_rows = 8
        self.first = self.meta + self.meta_rows


def pack_kernel(
    sz, counts, ups_in, sides_in, table_in, disp_in, vel_in, pos_in, hex_ref, mod_ref, pd_in, to_in, weight_in,
    send_ref, own_pos, own_vel, lists, moduli, blend_pd, blend_hex, blend_weight,
    ups, sides, table_ref, disp_ref, vel_ref, pos_ref, sems,
):
    moves = (
        (ups_in, ups),
        (sides_in, sides),
        (table_in, table_ref),
        (disp_in, disp_ref),
        (pos_in, pos_ref),
        (vel_in, vel_ref),
        (mod_ref, moduli),
        (hex_ref, send_ref.at[:, pl.ds(0, sz.height), :]),
        (pd_in, blend_pd),
        (to_in, blend_hex),
        (weight_in, blend_weight),
    )
    copies = [pltpu.make_async_copy(source, target, sems.at[k]) for k, (source, target) in enumerate(moves)]
    for copy in copies:
        copy.start()
    for copy in copies[:6]:
        copy.wait()
    lists[...] = jnp.zeros(lists.shape, jnp.int32)
    lists[0:3, 0 : sz.pair_slots] = table_ref[...]
    lane = lax.broadcasted_iota(jnp.int32, (1, LANES), 1)
    for place, ref, size in ((3, counts, 1), (4, ups, sz.halo), (5, sides, sz.halo)):
        row = jnp.zeros((1, LANES), jnp.int32)
        for item in range(size):
            row = jnp.where(lane == item, ref[item], row)
        lists[place : place + 1, :] = row
    for axis in range(3):
        for row in range(sz.rows):
            span = slice(row * LANES, (row + 1) * LANES)
            send_ref[axis, sz.pd + row : sz.pd + row + 1, :] = disp_ref[axis : axis + 1, span]
            own_pos[axis, row : row + 1, :] = pos_ref[axis : axis + 1, span]
            own_vel[axis, row : row + 1, :] = vel_ref[axis : axis + 1, span]
        send_ref[axis, sz.pos : sz.meta, :] = own_pos[axis]
        send_ref[axis, sz.meta : sz.first, :] = lists[...].astype(jnp.float32)
    for copy in copies[6:]:
        copy.wait()


def selector(sz):
    count = 3 * sz.rows
    part = lax.broadcasted_iota(jnp.int32, (LANES, LANES), 0)
    picks = [
        jnp.where(jnp.logical_and(lax.rem(part, count) == k, part < 3 * count), 1.0, 0.0) for k in range(count)
    ]
    return jnp.concatenate(picks, axis=1).astype(jnp.bfloat16)


def spread_nodes(sz, table, slot, picks, x):
    count = 3 * sz.rows
    flat = x.reshape(count, LANES)
    parts = []
    for _ in range(3):
        rounded = flat.astype(jnp.bfloat16).astype(jnp.float32)
        parts.append(rounded)
        flat = flat - rounded
    stacked = jnp.concatenate(parts + [jnp.zeros((LANES - 3 * count, LANES), jnp.float32)], axis=0)
    turned = stacked.T.astype(jnp.bfloat16)
    width = 8 * LANES
    for start in range(0, count * LANES, width):
        spread = jnp.dot(turned, picks[:, start : start + width], preferred_element_type=jnp.float32)
        for k in range(width // LANES):
            table[slot * count + start // LANES + k] = spread[:, k * LANES : (k + 1) * LANES]


def chunk_forces(sz, pos_table, disp_table, pos_ref, disp, source, target, guard):
    group = 8
    place = jnp.minimum(target, sz.rows - 1)
    lanes = [jnp.broadcast_to(pos_ref[axis, pl.ds(place, 1), :], (group, LANES)) for axis in range(3)]
    moved = [jnp.broadcast_to(disp[axis, pl.ds(place, 1), :], (group, LANES)) for axis in range(3)]
    sums = [jnp.zeros((group, LANES), jnp.float32) for _ in range(3)]
    slot, rest = lax.div(source, sz.rows * LANES), lax.rem(source, sz.rows * LANES)
    entry, start = slot * 3 * sz.rows + lax.div(rest, LANES), lax.rem(rest, LANES)
    for g in range(CHUNK // group):
        span = pl.ds(pl.multiple_of(start + g * group, group), group)
        offset = [lanes[axis] - pos_table[entry + axis * sz.rows, span, :] for axis in range(3)]
        now = [
            offset[axis] + (moved[axis] - disp_table[entry + axis * sz.rows, span, :]) for axis in range(3)
        ]
        rest_sq = offset[0] * offset[0] + offset[1] * offset[1] + offset[2] * offset[2]
        now_sq = now[0] * now[0] + now[1] * now[1] + now[2] * now[2]
        if guard:
            rest_sq = jnp.maximum(rest_sq, TINY)
            now_sq = jnp.maximum(now_sq, TINY)
        rest_inv = lax.rsqrt(rest_sq)
        reach = jnp.maximum(horizon - rest_sq * rest_inv, 0.0)
        scale = (lax.rsqrt(now_sq) - rest_inv) * (reach * reach)
        for axis in range(3):
            sums[axis] = sums[axis] + scale * now[axis]
    return sums


def box_flags(sz, flags, slot, own_pos, pos):
    rows = sz.rows
    lane = lax.broadcasted_iota(jnp.int32, (rows, LANES), 1)
    diagonal = lane == lax.broadcasted_iota(jnp.int32, (rows, LANES), 0)
    along = lambda column: jnp.sum(jnp.where(diagonal, column, 0.0), axis=0, keepdims=True)
    far = 3.0e38
    total = [jnp.zeros((rows, LANES), jnp.float32) for _ in range(LANES // CHUNK)]
    for axis in range(3):
        own = own_pos[axis]
        low = along(jnp.min(own, axis=1, keepdims=True))
        high = along(jnp.max(own, axis=1, keepdims=True))
        for q in range(LANES // CHUNK):
            inside = lane // CHUNK == q
            least = jnp.min(jnp.where(inside, pos[axis], far), axis=1, keepdims=True)
            most = jnp.max(jnp.where(inside, pos[axis], -far), axis=1, keepdims=True)
            gap = jnp.maximum(jnp.maximum(least - high, low - most), 0.0)
            total[q] = total[q] + gap * gap
    for q in range(LANES // CHUNK):
        start = (slot * (LANES // CHUNK) + q) * rows
        flags[start : start + rows, :] = (total[q] < horizon * horizon * 1.001).astype(jnp.int32)


def add_pair(sz, flags, work, target, slot, block, tiles, lane_first):
    halves, quarters = BLOCK // LANES, LANES // CHUNK
    count = work[0, 0]
    for h in range(halves):
        row = halves * block + h
        for hl in range(halves):
            first, second = (hl, h) if lane_first else (h, hl)
            whole = 1 - lax.rem(lax.shift_right_logical(tiles, 2 * first + second), 2)
            place = halves * target + hl
            for q in range(quarters):
                source = (slot * sz.rows + row) * LANES + q * CHUNK
                at = count + 1
                work[lax.shift_right_logical(at, 7), lax.bitwise_and(at, LANES - 1)] = source * TARGETS + place
                count = count + whole * flags[(slot * quarters + q) * sz.rows + row, place]
    work[0, 0] = count


def work_shape(sz):
    entries = sz.pair_slots * 24 + 2 * TOGETHER + 1
    return (-(-entries // (8 * LANES)) * 8, LANES)


def move_work(source, target, sem, part):
    if part == 0:
        return pltpu.make_async_copy(source.at[pl.ds(0, WORK_ROWS), :], target.at[pl.ds(0, WORK_ROWS), :], sem)
    return pltpu.make_async_copy(source, target, sem)


def move_rest(source, target, sem, count):
    @pl.when(count >= WORK_ROWS * LANES)
    def _():
        copy = move_work(source, target, sem, 1)
        copy.start()
        copy.wait()


def run_work(sz, work, pos_table, disp_table, pos_ref, disp, acc, guard, together):
    count = work[0, 0]

    def body(i, carry):
        items = []
        for k in range(together):
            at = i * together + k
            inside = at < count
            entry = jnp.where(inside, work[lax.shift_right_logical(at + 1, 7), lax.bitwise_and(at + 1, LANES - 1)], 0)
            source = lax.shift_right_logical(entry, 6)
            target = jnp.where(inside, lax.bitwise_and(entry, TARGETS - 1), sz.rows)
            items.append((target, chunk_forces(sz, pos_table, disp_table, pos_ref, disp, source, target, guard)))
        for target, sums in items:
            for axis in range(3):
                acc[axis, target] = acc[axis, target] + sums[axis]
        return carry

    lax.fori_loop(0, (count + together - 1) // together, body, 0)


def total_force(sz, acc, axis):
    return stiffness / (horizon * horizon) * jnp.sum(acc[axis, 0 : sz.rows], axis=1)


def halves_of(x):
    high = x.astype(jnp.bfloat16)
    return high, (x - high.astype(jnp.float32)).astype(jnp.bfloat16)


def blend(sz, disp_ref, pd_ref, hex_ref, weight_ref, pd_force, hex_pull):
    f32, bf16 = jnp.float32, jnp.bfloat16
    rows_h = hex_ref[...] // LANES
    cols_h = lax.rem(hex_ref[...], LANES)
    rows_p = pd_ref[...] // LANES
    cols_p = lax.rem(pd_ref[...], LANES)
    count = rows_h.shape[1]
    tall = -(-sz.rows // 16) * 16
    one_hot = lambda rows, at: (lax.broadcasted_iota(jnp.int32, (rows, count), 0) == at).astype(f32).astype(bf16)
    pick_h, pick_p = one_hot(LANES, cols_h), one_hot(LANES, cols_p)
    row_h, row_p = one_hot(sz.height, rows_h), one_hot(tall, rows_p)
    in_h = lax.broadcasted_iota(jnp.int32, (sz.height, count), 0) == rows_h
    in_p = lax.broadcasted_iota(jnp.int32, (sz.rows, count), 0) == rows_p
    twice = lambda x, axis: jnp.concatenate([x, x], axis=axis)
    gather_h, gather_p = twice(pick_h, 0), twice(pick_p, 0)
    scatter_h, scatter_p = twice(pick_h, 1), twice(pick_p, 1)
    transposed = (((1,), (1,)), ((), ()))
    for axis in range(3):
        hexes = jnp.concatenate(halves_of(disp_ref[axis, 0 : sz.height, :]), axis=1)
        nodes = jnp.concatenate(halves_of(disp_ref[axis, sz.pd : sz.state, :]), axis=1)
        from_h = jnp.dot(hexes, gather_h, preferred_element_type=f32)
        from_p = jnp.dot(nodes, gather_p, preferred_element_type=f32)
        at_h = jnp.sum(jnp.where(in_h, from_h, 0.0), axis=0, keepdims=True)
        at_p = jnp.sum(jnp.where(in_p, from_p, 0.0), axis=0, keepdims=True)
        high, low = halves_of(coupling * weight_ref[...] * (at_h - at_p))
        to_h = jnp.concatenate([row_h * high, row_h * low], axis=1)
        to_p = jnp.concatenate([row_p * high, row_p * low], axis=1)
        hex_pull[axis] = lax.dot_general(to_h, scatter_h, transposed, preferred_element_type=f32)
        pulled = lax.dot_general(to_p, scatter_p, transposed, preferred_element_type=f32)
        pd_force[axis] = pd_force[axis] + pulled[0 : sz.rows, :]


def near_kernel(sz, first, *refs):
    refs = list(refs)
    take = lambda count: [refs.pop(0) for _ in range(count)]
    if first:
        own_lists = take(1)[0]
    else:
        listed_work = take(1)[0]
    own, own_pos, side = take(3)
    if first:
        side_first = side
    else:
        pos_table, picks = take(2)
    blend_pd, blend_hex, blend_weight, force, hex_pull = take(5)
    if first:
        listed_work, pos_table, picks = take(3)
    table, acc, work, work_sem = take(4)
    fetch = move_work(listed_work, work, work_sem, 0)
    if not first:
        fetch.start()
    if first:
        side_pos = side_first[:, sz.pos : sz.meta, :]
        flags, flags_scalar, sem = take(3)
        box_flags(sz, flags, 0, own_pos, own_pos)
        box_flags(sz, flags, 1, own_pos, side_pos)
        after = sz.rows * 2 * (LANES // CHUNK)
        flags[after : after + sz.meta_rows, :] = side[0, sz.meta : sz.first, :].astype(jnp.int32)
        side_lists = flags_scalar.at[pl.ds(after, sz.meta_rows), :]
        copy = pltpu.make_async_copy(flags, flags_scalar, sem)
        copy.start()
        picks[...] = selector(sz)
        spread_nodes(sz, pos_table, 0, picks, own_pos[...])
        spread_nodes(sz, pos_table, 1, picks, side_pos)
    acc[...] = jnp.zeros(acc.shape, jnp.float32)
    disp = own.at[:, pl.ds(sz.pd, sz.rows), :]
    spread_nodes(sz, table, 0, picks, disp[...])
    spread_nodes(sz, table, 1, picks, side[:, sz.pd : sz.state, :])
    if first:
        copy.wait()
        work[0, 0] = 0
        add = functools.partial(add_pair, sz, flags_scalar, work)
        edge = sz.blocks + sz.halo

        def listed(e, carry):
            a, c, m = own_lists[0, e], own_lists[1, e], own_lists[2, e]

            @pl.when(c < sz.blocks)
            def _():
                add(a, 0, c, m, lane_first=True)

            @pl.when(jnp.logical_and(c < sz.blocks, c != a))
            def _():
                add(c, 0, a, m, lane_first=False)

            @pl.when(c >= edge)
            def _():
                add(a, 1, side_lists[5, jnp.maximum(c - edge, 0)], m, lane_first=True)

            return carry

        lax.fori_loop(0, own_lists[3, 0], listed, 0)

        def listed_beside(e, carry):
            a, c, m = side_lists[0, e], side_lists[1, e], side_lists[2, e]

            @pl.when(c >= edge)
            def _():
                add(own_lists[5, jnp.maximum(c - edge, 0)], 1, a, m, lane_first=False)

            return carry

        lax.fori_loop(0, side_lists[3, 0], listed_beside, 0)
        keep = move_work(work, listed_work, work_sem, 0)
        keep.start()
    else:
        fetch.wait()
        move_rest(listed_work, work, work_sem, work[0, 0])
    run_work(sz, work, pos_table, table, own_pos, disp, acc, guard=True, together=6)
    for axis in range(3):
        force[axis] = total_force(sz, acc, axis)
    blend(sz, own, blend_pd, blend_hex, blend_weight, force, hex_pull)
    if first:
        keep.wait()
        move_rest(work, listed_work, work_sem, work[0, 0])


def far_kernel(sz, first, *refs):
    refs = list(refs)
    take = lambda count: [refs.pop(0) for _ in range(count)]
    if first:
        own_lists = take(1)[0]
    else:
        listed_work = take(1)[0]
    own, own_pos, one, two, picks = take(5)
    if not first:
        pos_table = take(1)[0]
    near, force = take(2)
    if first:
        listed_work, pos_table = take(2)
    table, acc, work, work_sem = take(4)
    fetch = move_work(listed_work, work, work_sem, 0)
    if not first:
        fetch.start()
    even = lax.rem(lax.axis_index("wide"), 2) == 0
    disp_one, disp_two = one[:, sz.pd : sz.state, :], two[:, sz.pd : sz.state, :]
    if first:
        pos_one, pos_two = one[:, sz.pos : sz.meta, :], two[:, sz.pos : sz.meta, :]
        pos = (jnp.where(even, pos_one, pos_two), jnp.where(even, pos_two, pos_one))
        flags, flags_scalar, sem = take(3)
        for slot in range(2):
            box_flags(sz, flags, slot, own_pos, pos[slot])
        after = sz.rows * 2 * (LANES // CHUNK)
        below = after + sz.meta_rows
        list_one, list_two = one[0, sz.meta : sz.first, :], two[0, sz.meta : sz.first, :]
        flags[after:below, :] = jnp.where(even, list_one, list_two).astype(jnp.int32)
        flags[below : below + sz.meta_rows, :] = jnp.where(even, list_two, list_one).astype(jnp.int32)
        above_lists = flags_scalar.at[pl.ds(after, sz.meta_rows), :]
        below_lists = flags_scalar.at[pl.ds(below, sz.meta_rows), :]
        copy = pltpu.make_async_copy(flags, flags_scalar, sem)
        copy.start()
        for slot in range(2):
            spread_nodes(sz, pos_table, slot, picks, pos[slot])
    acc[...] = jnp.zeros(acc.shape, jnp.float32)
    spread_nodes(sz, table, 0, picks, jnp.where(even, disp_one, disp_two))
    spread_nodes(sz, table, 1, picks, jnp.where(even, disp_two, disp_one))
    if first:
        copy.wait()
        work[0, 0] = 0
        add = functools.partial(add_pair, sz, flags_scalar, work)
        edge = sz.blocks + sz.halo

        def listed(e, carry):
            a, c, m = own_lists[0, e], own_lists[1, e], own_lists[2, e]

            @pl.when(jnp.logical_and(c >= sz.blocks, c < edge))
            def _():
                add(a, 0, above_lists[4, jnp.clip(c - sz.blocks, 0, sz.halo - 1)], m, lane_first=True)

            return carry

        lax.fori_loop(0, own_lists[3, 0], listed, 0)

        def listed_below(e, carry):
            a, c, m = below_lists[0, e], below_lists[1, e], below_lists[2, e]

            @pl.when(jnp.logical_and(c >= sz.blocks, c < edge))
            def _():
                add(own_lists[4, jnp.clip(c - sz.blocks, 0, sz.halo - 1)], 1, a, m, lane_first=False)

            return carry

        lax.fori_loop(0, below_lists[3, 0], listed_below, 0)
        keep = move_work(work, listed_work, work_sem, 0)
        keep.start()
    else:
        fetch.wait()
        move_rest(listed_work, work, work_sem, work[0, 0])
    own_disp = own.at[:, pl.ds(sz.pd, sz.rows), :]
    run_work(sz, work, pos_table, table, own_pos, own_disp, acc, guard=False, together=4)
    for axis in range(3):
        force[axis] = near[axis] + total_force(sz, acc, axis)
    if first:
        keep.wait()
        move_rest(work, listed_work, work_sem, work[0, 0])


def hex_kernel(sz, first, last, *refs):
    refs = list(refs)
    take = lambda count: [refs.pop(0) for _ in range(count)]
    own, side, one, two, one_side, two_side, force, hex_pull, hex_vel, pd_vel = take(10)
    moduli = take(1)[0]
    if first:
        moduli_side, moduli_below, moduli_below_side = take(3)
    outs = take(4) if last else take(3)
    shifted_out = take(1)[0] if first else None
    parts, nodes_low, nodes_high = take(3)
    height = sz.height
    if last:
        results, outs = outs, take(4)
        out_sems = take(1)[0]
        half = height // 16 * 8

        def leave(k, rows):
            place = outs[k].at[:, rows, :], results[k].at[:, rows, :]
            return pltpu.make_async_copy(*place, out_sems.at[2 * k + (0 if rows.start == 0 else 1)])

        leaving = [leave(k, rows) for rows in (pl.ds(0, half), pl.ds(half, height - half)) for k in range(2)]
        leaving += [pltpu.make_async_copy(outs[k], results[k], out_sems.at[k + 2]) for k in (2, 3)]
    if first:
        speeds, sem = take(2)
        copy = pltpu.make_async_copy(hex_vel, speeds, sem)
        copy.start()
    wide = lax.axis_index("wide")
    even = lax.rem(wide, 2) == 0
    low_half = lax.axis_index("narrow") == 0
    shift = jnp.where(low_half, LANES - 1, 1)
    back = LANES - shift
    edge = jnp.where(low_half, 0, LANES - 1)
    signs = (jnp.where(low_half, 1.0, -1.0), None, jnp.where(even, 1.0, -1.0))
    mirrored = lambda axis, x: x if signs[axis] is None else x * signs[axis]

    if first:
        lanes = lax.broadcasted_iota(jnp.int32, (8, LANES), 1)
        last_lane = lanes == LANES - 1
        has_above = jnp.where(wide < lax.axis_size("wide") - 1, 1.0, 0.0)
        for row in range(0, height, 8):
            span = slice(row, row + 8)
            inside = lax.broadcasted_iota(jnp.int32, (8, LANES), 0) + row < height - 1

            def aligned(mine, beside):
                turned = pltpu.roll(jnp.where(last_lane, beside, mine), 1, axis=1)
                return jnp.where(inside, jnp.where(low_half, mine, turned), 0.0)

            above = aligned(moduli[span, :], moduli_side[span, :]) * has_above
            below = aligned(moduli_below[span, :], moduli_below_side[span, :])
            shifted_out[0, span, :] = jnp.where(even, above, below)
            shifted_out[1, span, :] = jnp.where(even, below, above)
        moduli = shifted_out

    for axis in range(3):
        speed = pd_vel[axis] + time_step * force[axis]
        place = own[axis, sz.pd : sz.state, :] + time_step * speed
        if last:
            for row in range(sz.rows):
                span = slice(row * LANES, (row + 1) * LANES)
                outs[2][axis : axis + 1, span] = place[row : row + 1, :]
                outs[3][axis : axis + 1, span] = speed[row : row + 1, :]
        else:
            outs[0][axis, sz.pd : sz.state, :] = place
            outs[2][axis] = speed
    if last:
        for copy in leaving[4:]:
            copy.start()

    tall = 16
    lanes = lax.broadcasted_iota(jnp.int32, (tall, LANES), 1)
    at_edge = lanes == edge

    def along_x(r, carry):
        rows = pl.ds(pl.multiple_of(r * tall, tall), tall)
        for layer in range(3):
            for axis in range(3):
                center, flank = ((own, side), (one, one_side), (two, two_side))[layer]
                mine = center[axis, rows, :]
                joined = jnp.where(at_edge, flank[axis, rows, :], mine)
                mine = mirrored(axis, mine)
                other = pltpu.roll(mirrored(axis, joined), shift, axis=1)
                parts[layer, axis, 0, rows, :] = mine + other
                parts[layer, axis, 1, rows, :] = other - mine
        return carry

    lax.fori_loop(0, height // tall, along_x, 0)
    for layer in range(3):
        for axis in range(3):
            for px in range(2):
                parts[layer, axis, px, height : height + 8, :] = jnp.zeros((8, LANES), jnp.float32)
    for axis in range(3):
        for px in range(2):
            nodes_high[axis, px, 0:8, :] = jnp.zeros((8, LANES), jnp.float32)

    shear_by = 1.0 / (2.0 * (1.0 + poisson)) / 16.0
    lame_by = poisson / ((1.0 + poisson) * (1.0 - 2.0 * poisson)) / 16.0
    for r in range(0, height, 8):
        grid = [[[None] * 4 for _ in range(3)] for _ in range(3)]
        for layer in range(3):
            for axis in range(3):
                for px in range(2):
                    here = parts[layer, axis, px, r : r + 8, :]
                    after = parts[layer, axis, px, r + 1 : r + 9, :]
                    grid[layer][axis][px] = here + after
                    grid[layer][axis][2 + px] = after - here
        total = [[None] * 4 for _ in range(3)]
        for place, (bottom, top, at_top) in enumerate(((0, 1, False), (2, 0, True))):
            m = [
                [
                    (grid[bottom][axis][k] + grid[top][axis][k], grid[top][axis][k] - grid[bottom][axis][k])
                    for k in range(4)
                ]
                for axis in range(3)
            ]
            modulus = moduli[place, r : r + 8, :]
            shear = modulus * shear_by
            lame = modulus * lame_by
            damp = modulus * hourglass
            slope = [[m[axis][1][0], m[axis][2][0], m[axis][0][1]] for axis in range(3)]
            trace = lame * (slope[0][0] + slope[1][1] + slope[2][2])
            twice = shear + shear
            stress = [[None] * 3 for _ in range(3)]
            for a in range(3):
                stress[a][a] = twice * slope[a][a] + trace
                for b in range(a + 1, 3):
                    stress[a][b] = shear * (slope[a][b] + slope[b][a])
                    stress[b][a] = stress[a][b]
            for axis in range(3):
                plain = [None, stress[axis][0], stress[axis][1], damp * m[axis][3][0]]
                odd = [stress[axis][2], damp * m[axis][1][1], damp * m[axis][2][1], damp * m[axis][3][1]]
                for k in range(4):
                    if k == 0:
                        value = odd[k] if at_top else -odd[k]
                    else:
                        value = plain[k] + odd[k] if at_top else plain[k] - odd[k]
                    total[axis][k] = value if total[axis][k] is None else total[axis][k] + value
        for axis in range(3):
            for px in range(2):
                even_y, odd_y = total[axis][px], total[axis][2 + px]
                nodes_low[axis, px, r : r + 8, :] = even_y - odd_y
                nodes_high[axis, px, r + 8 : r + 16, :] = even_y + odd_y

    lanes = lax.broadcasted_iota(jnp.int32, (8, LANES), 1)
    keep = lanes != edge
    if first:
        copy.wait()
        hex_vel = speeds
    for r in range(0, height, 8):
        for axis in range(3):
            pair = [
                nodes_low[axis, px, r : r + 8, :] + nodes_high[axis, px, r + 7 : r + 15, :] for px in range(2)
            ]
            moved = jnp.where(keep, pltpu.roll(pair[0] + pair[1], back, axis=1), 0.0)
            element = pair[0] - pair[1] + moved
            element = mirrored(axis, element)
            speed = hex_vel[axis, r : r + 8, :] - time_step * (element + hex_pull[axis, r : r + 8, :])
            place = own[axis, r : r + 8, :] + time_step * speed
            outs[0][axis, r : r + 8, :] = place
            outs[1][axis, r : r + 8, :] = speed
        if last and r + 8 == half:
            for copy in leaving[:2]:
                copy.start()
    if last:
        for copy in leaving[2:4]:
            copy.start()
        for copy in leaving:
            copy.wait()


def local(
    pd_position,
    pd_displace,
    pd_velocity,
    pair_table,
    pair_count,
    up_list,
    side_list,
    hex_displace,
    hex_velocity,
    hex_modulus,
    blend_pd,
    blend_hex,
    blend_weight,
):
    f32 = jnp.float32
    nodes = pd_position.shape[1]
    height, width = hex_displace.shape[2], hex_displace.shape[3]
    sz = Sizes(nodes, height, pair_table.shape[1], up_list.shape[0])
    wide = lax.axis_size("wide")
    near_pairs = [(i, i ^ 1) for i in range(wide) if i ^ 1 < wide]
    next_pairs = [(i, i + 1) for i in range(1, wide - 1, 2)] + [(i + 1, i) for i in range(1, wide - 1, 2)]
    swap_near = lambda x: lax.ppermute(x, "wide", near_pairs)
    swap_next = lambda x: lax.ppermute(x, "wide", next_pairs)
    shift_up = lambda x: lax.ppermute(x, "wide", [(i, i + 1) for i in range(wide - 1)])
    swap_side = lambda x: lax.ppermute(x, "narrow", [(0, 1), (1, 0)])
    shape = lambda *dims: pltpu.VMEM(dims, f32)

    rows_of = blend_pd.shape[0]
    own, own_pos, pd_vel, own_lists, moduli, *blends = pl.pallas_call(
        functools.partial(pack_kernel, sz),
        out_shape=(
            shape(3, sz.first, LANES),
            shape(3, sz.rows, LANES),
            shape(3, sz.rows, LANES),
            pltpu.VMEM((sz.meta_rows, LANES), jnp.int32),
            shape(height, LANES),
            pltpu.VMEM((1, rows_of), jnp.int32),
            pltpu.VMEM((1, rows_of), jnp.int32),
            shape(1, rows_of),
        ),
        in_specs=[SM] + [HB] * 11,
        out_specs=(VM,) * 8,
        scratch_shapes=[
            pltpu.SMEM(up_list.shape, jnp.int32),
            pltpu.SMEM(side_list.shape, jnp.int32),
            pltpu.VMEM(pair_table.shape, jnp.int32),
            shape(3, nodes),
            shape(3, nodes),
            shape(3, nodes),
            pltpu.SemaphoreType.DMA((11,)),
        ],
        compiler_params=LIMIT,
        name="pack",
    )(
        pair_count,
        *map(
            kept_far,
            (
                up_list,
                side_list,
                pair_table,
                pd_displace,
                pd_velocity,
                pd_position,
                hex_displace.reshape(3, height, width),
                hex_modulus.reshape(height, width),
                blend_pd.reshape(1, -1),
                blend_hex.reshape(1, -1),
                blend_weight.reshape(1, -1),
            ),
        ),
    )
    hex_vel = hex_velocity.reshape(3, height, width)
    state = (own, own_pos, hex_vel, pd_vel, moduli, None)
    fixed = (sz, own_lists, *blends)
    for step in range(STEPS):
        state = advance(step == 0, step == STEPS - 1, fixed, state, swap_side, swap_near, swap_next, shift_up)
    hex_out, hex_speed, pd_out, pd_speed = state
    return (pd_out, pd_speed, hex_out.reshape(hex_displace.shape), hex_speed.reshape(hex_velocity.shape))


def advance(first, last, fixed, state, swap_side, swap_near, swap_next, shift_up):
    f32 = jnp.float32
    shape = lambda *dims: pltpu.VMEM(dims, f32)
    whole = lambda *dims: jax.ShapeDtypeStruct(dims, f32)
    sz, own_lists, *blends = fixed
    blends = list(map(kept_near, blends))
    own, own_pos, hex_vel, pd_vel, moduli, kept = state
    height = sz.height
    side = swap_side(own)
    one = swap_near(own)
    two = swap_next(own)
    more = ()
    if first:
        below = shift_up(moduli)
        below_side = swap_side(below)
        more = tuple(map(kept_near, (swap_side(moduli), below, below_side)))
    listing = pltpu.VMEM(work_shape(sz), jnp.int32)
    flag_rows = 2 * sz.rows * (LANES // CHUNK)
    spread = (6 * sz.rows, LANES, LANES)
    scratch = [
        shape(*spread),
        shape(3, sz.rows + 1, 8, LANES),
        pltpu.SMEM(work_shape(sz), jnp.int32),
        pltpu.SemaphoreType.DMA,
    ]
    if first:
        near_work = far_work = (own_lists,)
        near_table = far_table = ()
        scratch += [
            pltpu.VMEM((flag_rows + 2 * sz.meta_rows, LANES), jnp.int32),
            pltpu.SMEM((flag_rows + 2 * sz.meta_rows, LANES), jnp.int32),
            pltpu.SemaphoreType.DMA,
        ]
    else:
        near_work, far_work, near_table, far_table, picks = kept
        near_work, far_work = (kept_near(near_work[0]),), (kept_near(far_work[0]),)
        first_ones = tuple(map(kept_near, (near_table, picks)))
        far_table = (kept_near(far_table),)
    one_side, two_side = map(kept_near, (swap_side(one), swap_side(two)))
    own, own_pos, pd_vel, moduli = map(kept_near, (own, own_pos, pd_vel, moduli))
    hex_vel = kept_far(hex_vel) if first else kept_near(hex_vel)
    side, one, two = map(kept_near, (side, one, two))
    if first:
        first_ones = ()
    extra = (listing, shape(*spread), pltpu.VMEM((LANES, 3 * sz.rows * LANES), jnp.bfloat16)) if first else ()
    force, hex_pull, *made = pl.pallas_call(
        functools.partial(near_kernel, sz, first),
        out_shape=(shape(3, sz.rows, LANES), shape(3, height, LANES)) + extra,
        in_specs=[SM if first else VM] + [VM] * (6 + len(first_ones)),
        out_specs=(VM, VM) + ((VM,) * 3 if first else ()),
        scratch_shapes=scratch,
        cost_estimate=pl.CostEstimate(flops=60_000_000, transcendentals=2_600_000, bytes_accessed=40_000_000),
        compiler_params=LIMIT,
        name="near",
    )(*near_work, own, own_pos, side, *first_ones, *blends)
    if first:
        near_work, near_table, picks = (made[0],), made[1], made[2]
    force, hex_pull = map(kept_near, (force, hex_pull))
    results = pl.pallas_call(
        functools.partial(far_kernel, sz, first),
        out_shape=(shape(3, sz.rows, LANES),) + extra[:2],
        in_specs=[SM if first else VM] + [VM] * (6 + len(far_table)),
        out_specs=(VM,) + ((VM,) * 2 if first else ()),
        scratch_shapes=scratch,
        compiler_params=LIMIT,
        name="far",
    )(*far_work, own, own_pos, one, two, kept_near(picks), *far_table, force)
    force = kept_near(results[0])
    if first:
        kept = ((made[0],), (results[1],), near_table, results[2], picks)
    if last:
        outs = (whole(3, height, LANES), whole(3, height, LANES)) + (whole(3, sz.rows * LANES),) * 2
    else:
        outs = (shape(3, sz.state, LANES), shape(3, height, LANES), shape(3, sz.rows, LANES))
    if first:
        outs = outs + (shape(2, height, LANES),)
    results = pl.pallas_call(
        functools.partial(hex_kernel, sz, first, last),
        out_shape=outs,
        in_specs=[VM] * 8 + [HB if first else VM] + [VM] * (2 + len(more)),
        out_specs=tuple(HB if last else VM for _ in outs),
        scratch_shapes=[
            pltpu.VMEM((3, 3, 2, height + 8, LANES), f32),
            pltpu.VMEM((3, 2, height, LANES), f32),
            pltpu.VMEM((3, 2, height + 8, LANES), f32),
        ]
        + ([shape(3, height, LANES), pltpu.SemaphoreType.DMA] if first else [])
        + ([shape(*out.shape) for out in outs] + [pltpu.SemaphoreType.DMA((6,))] if last else []),
        compiler_params=LIMIT,
        name="hexes",
    )(own, side, one, two, one_side, two_side, force, hex_pull, hex_vel, pd_vel, moduli, *more)
    if last:
        return results[:4]
    return results[0], own_pos, results[1], results[2], results[3] if first else moduli, kept


def solution(mesh):
    both = ("wide", "narrow")
    in_specs = (
        P(None, both),
        P(None, both),
        P(None, both),
        P(None, both),
        P(both),
        P(both),
        P(both),
        P(None, "wide", None, "narrow"),
        P(None, "wide", None, "narrow"),
        P("wide", None, "narrow"),
        P(both),
        P(both),
        P(both),
    )
    out_specs = (
        P(None, both),
        P(None, both),
        P(None, "wide", None, "narrow"),
        P(None, "wide", None, "narrow"),
    )
    return jax.shard_map(local, mesh=mesh, in_specs=in_specs, out_specs=out_specs, check_vma=False)
```
